32 devices in a mesh: ctx: 4 (over y, x), fsdp: 8 (over z, core).
Axes of the slice: x: 2, y: 2, z: 4, core: 2. Of those that a mesh axis runs over, the one named last changes fastest.
Arguments:
- tokens: bfloat16 [8, 1536, 768], P('fsdp', 'ctx'), may hold values from -15 to 15
- cotangent: bfloat16 [8, 1536, 768], P('fsdp', 'ctx'), may hold values from -6 to 6
- block_order: int32 [8, 8], P('fsdp'), may hold values from 0 to 7, as said below
- segment_ids: int32 [8, 1536], P('fsdp'), may hold values from 0 to 4, as said below
- valid_mask: int32 [8, 1536], P('fsdp'), may hold values from 0 to 1
- routes: int32 [8, 1536, 2], P('fsdp', 'ctx'), may hold values from 0 to 7, all different within a row; in each aligned block of 384 rows (0 to 383, 384 to 767, ..., all dimensions but the last counted through in order) at most 192 rows name the same one
- attention_gain: bfloat16 [768], P(('ctx', 'fsdp')), may hold values from 0.5 to 1.5
- query_weight: bfloat16 [768, 768], P(('ctx', 'fsdp')), may hold values from -0.21875 to 0.21875
- key_weight: bfloat16 [768, 768], P(('ctx', 'fsdp')), may hold values from -0.21875 to 0.21875
- value_weight: bfloat16 [768, 768], P(('ctx', 'fsdp')), may hold values from -0.21875 to 0.21875
- out_weight: bfloat16 [768, 768], P(('ctx', 'fsdp')), may hold values from -3 to 3
- feedforward_gain: bfloat16 [768], P(('ctx', 'fsdp')), may hold values from 0.5 to 1.5
- router: bfloat16 [768, 8], P(('ctx', 'fsdp')), may hold values from -0.15625 to 0.15625
- shared_gate: bfloat16 [768, 2048], P(('ctx', 'fsdp')), may hold values from -0.21875 to 0.21875
- shared_up: bfloat16 [768, 2048], P(('ctx', 'fsdp')), may hold values from -0.21875 to 0.21875
- shared_down: bfloat16 [2048, 768], P(('ctx', 'fsdp')), may hold values from -0.125 to 0.125
- expert_gate: bfloat16 [8, 768, 2048], P('fsdp', None, 'ctx'), may hold values from -0.21875 to 0.21875
- expert_up: bfloat16 [8, 768, 2048], P('fsdp', None, 'ctx'), may hold values from -0.21875 to 0.21875
- expert_down: bfloat16 [8, 2048, 768], P('fsdp', 'ctx'), may hold values from -0.25 to 0.25
Outputs:
- output: bfloat16 [8, 1536, 768], P('fsdp', 'ctx')
- input_grad: float32 [8, 1536, 768], P('fsdp', 'ctx')
- grad_attention_gain: float32 [768], P(('ctx', 'fsdp'))
- grad_query_weight: float32 [768, 768], P(('ctx', 'fsdp'))
- grad_key_weight: float32 [768, 768], P(('ctx', 'fsdp'))
- grad_value_weight: float32 [768, 768], P(('ctx', 'fsdp'))
- grad_out_weight: float32 [768, 768], P(('ctx', 'fsdp'))
- grad_feedforward_gain: float32 [768], P(('ctx', 'fsdp'))
- grad_router: float32 [768, 8], P(('ctx', 'fsdp'))
- grad_shared_gate: float32 [768, 2048], P(('ctx', 'fsdp'))
- grad_shared_up: float32 [768, 2048], P(('ctx', 'fsdp'))
- grad_shared_down: float32 [2048, 768], P(('ctx', 'fsdp'))
- grad_expert_gate: float32 [8, 768, 2048], P('fsdp', None, 'ctx')
- grad_expert_up: float32 [8, 768, 2048], P('fsdp', None, 'ctx')
- grad_expert_down: float32 [8, 2048, 768], P('fsdp', 'ctx')
- stats: float32 [8, 4], P('fsdp')
The draws below stay inside these ranges and needn't reach their ends.
Inputs may be any that keep to these rules, and one draw needn't show every extreme that they name: `block_order`: in each group's row, entries 2c and 2c + 1 are some i and 7 - i, each block once. `segment_ids`: positions 0 to 767 are segment 0; segments 1 to 4 follow in order, each 96 to 288 positions long, one of them exactly the longest. `routes`: the two entries of a row differ; among the rows of one device no expert is named more than 192 times, and in some device one expert exactly 192 times.
All inputs are finite; a program needn't handle non-finite values.
Results may differ from the reference program's by a relative error of at most 0.025.
Values may be sent and summed in bfloat16 or wider, within the bound.
No kernel may reach another device: no remote copies, remote signals or barrier semaphores. Data moves between devices by JAX's collectives and lax.ppermute only.
A program may use at most 256 MiB of HBM per device.

```python
import math
import jax
import jax.numpy as jnp
import numpy as np
from jax import lax

D = 768
HEADS = 12
HD = 64
FF = 2048
TOPK = 2
TOK_DEV = 384
NCONT = 4
EXPERTS = 8
GROUPS = 8
GROUP_TOK = 1536
PROMPT = 768
CONT = 192
NBLK = 8
CAP = 192
N_CTX = 4


def draw_tokens(key, part):
    keys = jax.random.split(key, 1)
    ramp = jnp.exp(jnp.log(3.0) * jnp.arange(GROUP_TOK, dtype=jnp.float32) / GROUP_TOK)
    base = jnp.clip(jax.random.normal(keys[0], (GROUPS, GROUP_TOK, D), jnp.float32), -5.0, 5.0)
    return jnp.clip(base * ramp[None, :, None], -15.0, 15.0).astype(jnp.bfloat16)


def draw_block_order(key, part):

    def one_group(group_key):
        perm_key, flip_key = jax.random.split(group_key)
        pair_ids = jax.random.permutation(perm_key, NBLK // 2).astype(jnp.int32)
        flips = jax.random.randint(flip_key, (NBLK // 2,), 0, 2)
        high_ids = NBLK - 1 - pair_ids
        leading = jnp.where(flips > 0, high_ids, pair_ids)
        trailing = jnp.where(flips > 0, pair_ids, high_ids)
        return jnp.stack([leading, trailing], axis=1).reshape(NBLK).astype(jnp.int32)
    return jax.vmap(one_group)(jax.random.split(key, GROUPS))


def draw_segment_ids(key, part):

    def one_group(group_key):
        shift_key, order_key = jax.random.split(group_key)
        half_len = CONT // 2
        shifts = jax.random.randint(shift_key, (NCONT // 2,), 0, half_len + 1)
        shifts = shifts.at[0].set(half_len)
        lengths = jnp.concatenate([CONT + shifts, CONT - shifts])
        lengths = jnp.take(lengths, jax.random.permutation(order_key, NCONT))
        ends = PROMPT + jnp.cumsum(lengths)
        position = jnp.arange(GROUP_TOK, dtype=jnp.int32)
        later = jnp.sum((position[:, None] >= ends[None, :]).astype(jnp.int32), axis=1)
        return jnp.where(position < PROMPT, 0, 1 + later).astype(jnp.int32)
    return jax.vmap(one_group)(jax.random.split(key, GROUPS))


def draw_valid_mask(key, part):
    draws = jax.random.randint(key, (GROUPS, GROUP_TOK), 0, 8)
    validity = (draws < 7).astype(jnp.int32)
    return validity.at[:, 0].set(1)


def levels(stream_key, shape, cuts, smallest, top_value):
    level = 1.0
    for axis_at, shards_of in cuts:
        heights = jax.random.uniform(jax.random.fold_in(jax.random.fold_in(stream_key, 6), axis_at), (shards_of,), jnp.float32, smallest / len(cuts), top_value / len(cuts))
        level = level * jnp.repeat(jnp.exp(heights), shape[axis_at] // shards_of).reshape((-1,) + (1,) * (len(shape) - 1 - axis_at))
    return level


def deal_out(key, own, number, rows, count, top, reach, skew):
    sequence = jax.random.permutation(key, count)
    crowded, usual = shares(count, rows * top, reach, skew, True), shares(count, rows * top, reach, skew, False)
    places = jnp.arange(count)

    def named(sizes, turn):
        used = int((sizes > 0).sum())
        fixed = max(1, used // 4)
        passed = fixed + (places - fixed + turn * (used - fixed)) % max(1, count - fixed)
        return jnp.zeros((count,), jnp.int32).at[sequence[jnp.where(places < fixed, places, passed)]].set(jnp.asarray(sizes, jnp.int32))

    sizes = jnp.where(number % 4 == 0, named(crowded, number // 4), named(usual, number - number // 4 - 1))
    mixed = jax.random.permutation(jax.random.fold_in(own, 3), count)
    source_of, receiver = mixed[0:count // 2 * 2:2], mixed[1:count // 2 * 2:2]
    margin = jnp.minimum(sizes[source_of] - 1, reach - sizes[receiver]) // 2
    margin = jnp.where((source_of == sequence[0]) | (receiver == sequence[0]) | (sizes[receiver] == 0), 0, jnp.maximum(margin, 0))
    passed = jax.random.randint(jax.random.fold_in(own, 4), (count // 2,), 0, 1 << 20) % (margin + 1)
    sizes = sizes.at[source_of].add(-passed).at[receiver].add(passed)
    labels = jnp.searchsorted(jnp.cumsum(sizes), jnp.arange(rows * top), side="right").astype(jnp.int32)
    grid = labels.reshape(top, rows).T
    grid = grid[jax.random.permutation(jax.random.fold_in(own, 1), rows)]
    turn = jax.random.randint(jax.random.fold_in(own, 2), (rows, 1), 0, top)
    return jnp.take_along_axis(grid, (jnp.arange(top)[None, :] + turn) % top, axis=1)


def shares(count, total, limit, lean, full):
    weights = [(1 << 20) // math.isqrt(rank ** lean) + 1 for rank in range(1, count + 1)]
    largest = limit if full else min(limit, max(-(-total // count), total * weights[0] // sum(weights)))
    least = 1 if total - largest >= count - 1 else 0
    holding, spare = [largest] + [least] * (count - 1), total - largest - least * (count - 1)
    while spare > 0:
        free = [i for i in range(1, count) if holding[i] < largest] or [i for i in range(1, count) if holding[i] < limit]
        mass, remaining = sum([weights[i] for i in free]), spare
        for i in free:
            extra = min(limit - holding[i], max(1, remaining * weights[i] // mass), spare)
            holding[i] = holding[i] + extra
            spare = spare - extra
    return np.array(holding)


def noise(own_key, dims, spread, most, cuts=(), kind=jnp.bfloat16):
    array = spread * jax.random.normal(own_key, dims, jnp.float32)
    if cuts:
        array = array * levels(own_key, dims, cuts, -0.22, 0.18)
    return jnp.clip(array, -most, most).astype(kind)


def setup_inputs(seed: int = 0) -> dict:
    key_list = jax.random.split(jax.random.key(seed), 20)
    tokens = draw_tokens(jax.random.fold_in(key_list[19], 71), 0)
    cotangent = noise(key_list[1], (GROUPS, GROUP_TOK, D), 1.0, 6.0, ((0, 8), (1, 4)))
    block_order = draw_block_order(jax.random.fold_in(key_list[19], 71), 0)
    segment_ids = draw_segment_ids(jax.random.fold_in(key_list[19], 71), 0)
    valid_mask = draw_valid_mask(jax.random.fold_in(key_list[19], 71), 0)
    routes_keys = jax.random.split(jax.random.fold_in(key_list[5], 1), GROUPS * GROUP_TOK // TOK_DEV)
    routes_turns = jax.random.permutation(jax.random.fold_in(key_list[5], 3), GROUPS * GROUP_TOK // TOK_DEV)
    routes = jax.vmap(lambda own, number: deal_out(jax.random.fold_in(key_list[5], 2), own, number, TOK_DEV, EXPERTS, TOPK, CAP, 2))(routes_keys, routes_turns).reshape((GROUPS, GROUP_TOK, TOPK))
    attention_gain = jnp.clip(1.0 + 0.1 * jax.random.normal(key_list[6], (D,), jnp.float32), 0.5, 1.5).astype(jnp.bfloat16)
    query_weight = noise(key_list[7], (D, D), D ** -0.5, 0.21875, ((0, 32),))
    key_weight = noise(key_list[8], (D, D), D ** -0.5, 0.21875, ((0, 32),))
    value_weight = noise(key_list[9], (D, D), D ** -0.5, 0.21875, ((0, 32),))
    out_weight = noise(key_list[10], (D, D), (max(1, D * 8 // GROUP_TOK)) ** -0.5, 3.0, ((0, 32),))
    feedforward_gain = jnp.clip(1.0 + 0.1 * jax.random.normal(key_list[11], (D,), jnp.float32), 0.5, 1.5).astype(jnp.bfloat16)
    router = noise(key_list[12], (D, EXPERTS), (2 * D) ** -0.5, 0.15625, ((0, 32),))
    shared_gate = noise(key_list[13], (D, FF), D ** -0.5, 0.21875, ((0, 32),))
    shared_up = noise(key_list[14], (D, FF), D ** -0.5, 0.21875, ((0, 32),))
    shared_down = noise(key_list[15], (FF, D), FF ** -0.5, 0.125, ((0, 32),))
    expert_gate = noise(key_list[16], (EXPERTS, D, FF), D ** -0.5, 0.21875, ((0, 8), (2, 4)))
    expert_up = noise(key_list[17], (EXPERTS, D, FF), D ** -0.5, 0.21875, ((0, 8), (2, 4)))
    expert_down = noise(key_list[18], (EXPERTS, FF, D), (FF // 4) ** -0.5, 0.25, ((0, 8), (1, 4)))
    return dict(tokens=tokens, cotangent=cotangent, block_order=block_order, segment_ids=segment_ids, valid_mask=valid_mask, routes=routes, attention_gain=attention_gain, query_weight=query_weight, key_weight=key_weight, value_weight=value_weight, out_weight=out_weight, feedforward_gain=feedforward_gain, router=router, shared_gate=shared_gate, shared_up=shared_up, shared_down=shared_down, expert_gate=expert_gate, expert_up=expert_up, expert_down=expert_down)


HIGH = lax.Precision.HIGHEST
EPS = 1e-06
NEG = -1e+30
BASE = 10000.0

@jax.custom_vjp
def low(v):
    return lax.optimization_barrier(v.astype(jnp.bfloat16)).astype(jnp.float32)

@jax.custom_vjp
def low_back(v):
    return v

def low_keep(v):
    return (low(v), None)

def low_pass(kept, grad):
    return (grad,)

def back_keep(v):
    return (v, None)

def back_low(kept, grad):
    return (low(grad),)
low.defvjp(low_keep, low_pass)
low_back.defvjp(back_keep, back_low)

def rms_norm(values, gain_vec):
    mean_sq = lax.optimization_barrier(jnp.mean(values * values, axis=-1, keepdims=True))
    return values * lax.rsqrt(mean_sq + EPS) * gain_vec

def gating(gate_pre, up_pre):
    return jax.nn.silu(gate_pre) * up_pre

def tables(positions, half_dim):
    frequency = jnp.exp(jnp.arange(half_dim, dtype=jnp.float32) * (-math.log(BASE) / half_dim))
    angles = positions.astype(jnp.float32)[:, None] * frequency[None, :]
    return (jnp.cos(angles), jnp.sin(angles))

def rotate(values, cosine, sine_table):
    total_rows = values.shape[0]
    halves = values.reshape(total_rows, HEADS, 2, HD // 2)
    first_half = halves[:, :, 0, :]
    second_half = halves[:, :, 1, :]
    cos_rows = cosine[:, None, :]
    sin_rows = sine_table[:, None, :]
    turned = jnp.stack([first_half * cos_rows - second_half * sin_rows, second_half * cos_rows + first_half * sin_rows], axis=2)
    return turned.reshape(total_rows, HEADS * HD)

def layout(order_row, segment_row, valid_row, block_len):
    group_len = segment_row.shape[0]
    stored = jnp.arange(group_len, dtype=jnp.int32)
    position = jnp.take(order_row, stored // block_len).astype(jnp.int32) * block_len + stored % block_len
    bounds = jnp.arange(NCONT + 1, dtype=jnp.int32)
    starts = lax.optimization_barrier(jnp.sum((segment_row[None, :] < bounds[:, None]).astype(jnp.int32), axis=1))
    segment = jnp.take(segment_row, position)
    rotary = position - jnp.take(starts, segment) + jnp.where(segment > 0, starts[1], 0)
    validity = jnp.take(valid_row, position)
    return (segment, rotary.astype(jnp.int32), validity)

def allowed(seg_query, rot_query, seg_keys, rot_keys, valid_keys):
    same_doc = (seg_keys[None, :] == 0) | (seg_keys[None, :] == seg_query[:, None])
    return (valid_keys[None, :] > 0) & same_doc & (rot_keys[None, :] <= rot_query[:, None])

def route_gates(logits, route_hot):
    picked = lax.optimization_barrier(jnp.sum(route_hot * logits[:, None, :], axis=-1))
    top_val = lax.optimization_barrier(jnp.max(picked, axis=-1, keepdims=True))
    exp_terms = jnp.exp(picked - top_val)
    return exp_terms / lax.optimization_barrier(jnp.sum(exp_terms, axis=-1, keepdims=True))

def slot_map(chosen_flat, experts, capacity):
    pair_count = chosen_flat.shape[0]
    expert_hot = (chosen_flat[:, None] == jnp.arange(experts, dtype=jnp.int32)[None, :]).astype(jnp.int32)
    running_count = jnp.cumsum(expert_hot, axis=0)
    slot_index = lax.optimization_barrier(jnp.sum(expert_hot * running_count, axis=1)) - 1
    flat_slot = (chosen_flat * capacity + slot_index).astype(jnp.int32)
    slot_owner = jnp.zeros((experts * capacity,), jnp.int32).at[flat_slot].add(jnp.arange(pair_count, dtype=jnp.int32) + 1)
    filled = slot_owner > 0
    pair_index = jnp.maximum(slot_owner - 1, 0).astype(jnp.int32)
    return (flat_slot, (pair_index // TOPK).astype(jnp.int32), filled, pair_index)

def group_attention(items):
    query_grp, key_grp, value_grp, seg_grp, rot_grp, valid_grp = items
    query_block = math.gcd(512, GROUP_TOK)
    block_count = GROUP_TOK // query_block

    def one_block(parts):
        query_tile, seg_query, rot_query = parts
        raw_scores = jnp.einsum('qhd,khd->hqk', query_tile, key_grp, precision=HIGH)
        scores = low_back(raw_scores * (1.0 / math.sqrt(HD)))
        key_mask = allowed(seg_query, rot_query, seg_grp, rot_grp, valid_grp)[None]
        scores = jnp.where(key_mask, scores, NEG)
        top_val = lax.optimization_barrier(jnp.max(scores, axis=-1, keepdims=True))
        exp_terms = jnp.exp(scores - top_val)
        attn_probs = low(exp_terms / lax.optimization_barrier(jnp.sum(exp_terms, axis=-1, keepdims=True)))
        mixed = jnp.einsum('hqk,khd->qhd', attn_probs, value_grp, precision=HIGH)
        return mixed.reshape(query_block, HEADS * HD)
    parts = (query_grp.reshape(block_count, query_block, HEADS, HD), seg_grp.reshape(block_count, query_block), rot_grp.reshape(block_count, query_block))
    return lax.map(jax.checkpoint(one_block), parts).reshape(GROUP_TOK, HEADS * HD)

def expert_apply(items):
    rows_in, gate_mat, up_mat, down_mat = items
    gate_pre = low_back(jnp.dot(rows_in, gate_mat, precision=HIGH))
    up_pre = low_back(jnp.dot(rows_in, up_mat, precision=HIGH))
    hidden = low(gating(gate_pre, up_pre))
    return low(low_back(jnp.dot(hidden, down_mat, precision=HIGH)))

def reference(tokens, cotangent, block_order, segment_ids, valid_mask, routes, attention_gain, query_weight, key_weight, value_weight, out_weight, feedforward_gain, router, shared_gate, shared_up, shared_down, expert_gate, expert_up, expert_down):
    block_len = GROUP_TOK // NBLK
    seg_all, rot_all, valid_all = jax.vmap(lambda order_row, segment_row, valid_row: layout(order_row, segment_row, valid_row, block_len))(block_order, segment_ids, valid_mask)
    block_total = GROUPS * N_CTX
    chosen_blocks = routes.reshape(block_total, TOK_DEV * TOPK)
    flat_slot, source_row, filled, pair_index = jax.vmap(lambda chosen_row: slot_map(chosen_row, EXPERTS, CAP))(chosen_blocks)
    route_hot = (routes.reshape(-1, TOPK)[:, :, None] == jnp.arange(EXPERTS, dtype=jnp.int32)[None, None, :]).astype(jnp.float32)
    cosine, sine_table = tables(rot_all.reshape(-1), HD // 2)
    valid_grp = valid_all.astype(jnp.float32)[:, :, None]
    params = (attention_gain.astype(jnp.float32), query_weight.astype(jnp.float32), key_weight.astype(jnp.float32), value_weight.astype(jnp.float32), out_weight.astype(jnp.float32), feedforward_gain.astype(jnp.float32), router.astype(jnp.float32), shared_gate.astype(jnp.float32), shared_up.astype(jnp.float32), shared_down.astype(jnp.float32), expert_gate.astype(jnp.float32), expert_up.astype(jnp.float32), expert_down.astype(jnp.float32))
    stream = tokens.astype(jnp.float32)

    def group_sum(values):
        return lax.optimization_barrier(jnp.sum(valid_grp * (values * values).reshape(GROUPS, GROUP_TOK, D), axis=(1, 2)))

    def forward(weights, stream_in):
        gain_first, full_query, full_key, full_value, full_out, gain_second, full_router, full_gate, full_up, full_down, whole_gate, whole_up, whole_down = weights
        flat_rows = stream_in.reshape(-1, D)
        normed = low(rms_norm(flat_rows, gain_first))
        query_rot = low(rotate(low_back(jnp.dot(normed, full_query, precision=HIGH)), cosine, sine_table))
        key_rot = low(rotate(low_back(jnp.dot(normed, full_key, precision=HIGH)), cosine, sine_table))
        value_low = low(low_back(jnp.dot(normed, full_value, precision=HIGH)))
        shaped = (GROUPS, GROUP_TOK, HEADS, HD)
        attn_mix = lax.map(group_attention, (query_rot.reshape(shaped), key_rot.reshape(shaped), value_low.reshape(shaped), seg_all, rot_all, valid_all)).reshape(-1, D)
        attn_low = low(low_back(attn_mix))
        attn_out = low_back(jnp.dot(attn_low, full_out, precision=HIGH))
        residual = flat_rows + attn_out
        normed_two = low(rms_norm(residual, gain_second))
        logits = jnp.dot(normed_two, full_router, precision=HIGH)
        gate_probs = route_gates(logits, route_hot)
        shared_gate_pre = low_back(jnp.dot(normed_two, full_gate, precision=HIGH))
        shared_up_pre = low_back(jnp.dot(normed_two, full_up, precision=HIGH))
        shared_hidden = low(gating(shared_gate_pre, shared_up_pre))
        shared_outp = jnp.dot(shared_hidden, full_down, precision=HIGH)
        block_rows = normed_two.reshape(block_total, TOK_DEV, D)
        dispatched = jax.vmap(lambda rows_in, source_idx, fill_flag: jnp.where(fill_flag[:, None], jnp.take(rows_in, source_idx, axis=0), jnp.zeros((), jnp.float32)))(block_rows, source_row, filled)
        dispatched = low_back(dispatched)
        by_expert = dispatched.reshape(block_total, EXPERTS, CAP, D).transpose(1, 0, 2, 3).reshape(EXPERTS, block_total * CAP, D)
        expert_out = lax.map(jax.checkpoint(expert_apply), (by_expert, whole_gate, whole_up, whole_down))
        back_blocks = expert_out.reshape(EXPERTS, block_total, CAP, D).transpose(1, 0, 2, 3).reshape(block_total, EXPERTS * CAP, D)
        pair_outputs = jax.vmap(lambda rows_in, slot_idx: jnp.take(rows_in, slot_idx, axis=0))(back_blocks, flat_slot).reshape(-1, TOPK, D)
        expert_mix = lax.optimization_barrier(jnp.sum(gate_probs[:, :, None] * pair_outputs, axis=1))
        mixer_out = expert_mix + shared_outp
        result = residual + mixer_out
        sums = jnp.stack([group_sum(flat_rows), group_sum(attn_out), group_sum(mixer_out), group_sum(result)], axis=1)
        return (result.reshape(GROUPS, GROUP_TOK, D), sums)
    result, pull, sums = jax.vjp(forward, params, stream, has_aux=True)
    weight_grads, input_grad = pull(cotangent.astype(jnp.float32))
    grad_gain_first, grad_query, grad_key, grad_value, grad_out, grad_gain_second, grad_router, grad_gate, grad_up, grad_down, grad_whole_gate, grad_whole_up, grad_whole_down = weight_grads
    valid_count = lax.optimization_barrier(jnp.sum(valid_mask, axis=1)).astype(jnp.float32)
    stats = jnp.sqrt(sums / (valid_count[:, None] * D))
    return (result.astype(jnp.bfloat16), input_grad, grad_gain_first, grad_query, grad_key, grad_value, grad_out, grad_gain_second, grad_router, grad_gate, grad_up, grad_down, grad_whole_gate, grad_whole_up, grad_whole_down, stats)
```

```python
import functools
import math

import jax
import jax.numpy as jnp
from jax import lax
from jax.experimental import pallas as pl
from jax.experimental.pallas import tpu as pltpu
from jax.sharding import PartitionSpec as P

D = 768
HEADS = 12
HD = 64
TOPK = 2
NCONT = 4

HIGH = lax.Precision.HIGHEST
EPS = 1e-06
NEG = -1e30
FLOOR = -5e29
BASE = 10000.0
LANES = 128
TILE = 256
GRPS = D // LANES
VMEM = 60 * 1024 * 1024

f32 = jnp.float32
bf16 = jnp.bfloat16
i32 = jnp.int32

NT = (((1,), (1,)), ((), ()))
NN = (((1,), (0,)), ((), ()))
TN = (((0,), (0,)), ((), ()))


def mm(a, b, dims=NN):
    return lax.dot_general(a, b, dims, preferred_element_type=f32)


def low_lanes(rows):
    lane = lax.broadcasted_iota(i32, (rows, LANES), 1)
    return lane % HD < HD // 2


def first_head(rows):
    return lax.broadcasted_iota(i32, (rows, LANES), 1) < HD


def turn(values, cosine, sine):
    low = low_lanes(values.shape[0])
    parts = []
    for g in range(GRPS):
        part = values[:, g * LANES : (g + 1) * LANES]
        other = jnp.where(
            low, pltpu.roll(part, LANES - HD // 2, 1), pltpu.roll(part, HD // 2, 1)
        )
        parts.append(part * cosine + other * sine)
    return jnp.concatenate(parts, axis=1)


def const_spec(shape):
    zeros = (0,) * len(shape)
    return pl.BlockSpec(shape, lambda *_: zeros)


def qkv_kernel(own, x_ref, gain_ref, wq_ref, wk_ref, wv_ref, cos_ref, sin_ref, n_ref, q_ref, k_ref, v_ref):
    x = x_ref[...].astype(f32)
    inv = lax.rsqrt(jnp.mean(x * x, axis=-1, keepdims=True) + EPS)
    n = (x * inv * gain_ref[...]).astype(bf16)
    n_ref[...] = n
    cosine = cos_ref[...]
    sine = sin_ref[...]
    k_ref[...] = turn(mm(n, wk_ref[...]), cosine, sine).astype(bf16)
    v_ref[...] = mm(n, wv_ref[...]).astype(bf16)

    @pl.when(pl.program_id(0) < own)
    def _():
        q = turn(mm(n, wq_ref[...]), cosine, sine)
        q_ref[...] = (q * (1.0 / math.sqrt(HD))).astype(bf16)


def project(x_all, gain, wq, wk, wv, cosine, sine, block, own):
    rows = x_all.shape[0]
    steps = rows // block
    row_spec = pl.BlockSpec((block, D), lambda i: (i, 0))
    tab_spec = pl.BlockSpec((block, LANES), lambda i: (i, 0))
    wide = jax.ShapeDtypeStruct((rows, D), bf16)
    return pl.pallas_call(
        functools.partial(qkv_kernel, own),
        grid=(steps,),
        in_specs=[row_spec, const_spec((1, D))] + [const_spec((D, D))] * 3 + [tab_spec] * 2,
        out_specs=[
            row_spec,
            pl.BlockSpec((block, D), lambda i: (jnp.minimum(i, own - 1), 0)),
            row_spec,
            row_spec,
        ],
        out_shape=[wide, jax.ShapeDtypeStruct((own * block, D), bf16), wide, wide],
        compiler_params=pltpu.CompilerParams(vmem_limit_bytes=VMEM),
        name="qkv",
    )(x_all, gain, wq, wk, wv, cosine, sine)


def attend_kernel(
    flag_ref, q_ref, k_ref, v_ref, sq_ref, rq_ref, sk_ref, rk_ref, vk_ref,
    o_ref, low_ref, lse_ref, m_sc, l_sc, acc_sc,
):
    i, j = pl.program_id(0), pl.program_id(1)
    count = pl.num_programs(1)
    rows = q_ref.shape[0]
    first = first_head(rows)

    @pl.when(j == 0)
    def _():
        m_sc[...] = jnp.full(m_sc.shape, FLOOR, f32)
        l_sc[...] = jnp.zeros(l_sc.shape, f32)
        acc_sc[...] = jnp.zeros(acc_sc.shape, f32)

    @pl.when(flag_ref[i * count + j] > 0)
    def _():
        sk = sk_ref[0]
        ok = (vk_ref[0] > 0) & ((sk == 0) | (sk == sq_ref[...])) & (rk_ref[0] <= rq_ref[...])
        bias = jnp.where(ok, 0.0, NEG)
        for g in range(GRPS):
            at = slice(g * LANES, (g + 1) * LANES)
            q2, k2, v2 = q_ref[:, at], k_ref[:, at], v_ref[:, at]
            mixed, scale = [], []
            for half in range(2):
                h = 2 * g + half
                mine = first if half == 0 else ~first
                s = mm(jnp.where(mine, q2, jnp.zeros((), bf16)), k2, NT) + bias
                m_old = m_sc[h]
                m_new = jnp.maximum(m_old, jnp.max(s, axis=-1, keepdims=True))
                p = jnp.exp(s - m_new)
                a = jnp.exp(m_old - m_new)
                l_sc[h] = l_sc[h] * a + jnp.sum(p, axis=-1, keepdims=True)
                m_sc[h] = m_new
                mixed.append(mm(p.astype(bf16), v2))
                scale.append(a)
            acc_sc[:, at] = acc_sc[:, at] * jnp.where(first, scale[0], scale[1]) + jnp.where(
                first, mixed[0], mixed[1]
            )

    @pl.when(j == count - 1)
    def _():
        lane = lax.broadcasted_iota(i32, (rows, LANES), 1)
        logs = jnp.zeros((rows, LANES), f32)
        for g in range(GRPS):
            at = slice(g * LANES, (g + 1) * LANES)
            inv = []
            for half in range(2):
                h = 2 * g + half
                total = jnp.maximum(l_sc[h], 1e-30)
                inv.append(1.0 / total)
                logs = jnp.where(lane == h, m_sc[h] + jnp.log(total), logs)
            o = acc_sc[:, at] * jnp.where(first, inv[0], inv[1])
            o_ref[:, at] = o
            low_ref[:, at] = o.astype(bf16)
        lse_ref[0] = logs.T[: lse_ref.shape[1]]


def attend(flags, q, k, v, seg_q, rot_q, seg_k, rot_k, val_k, block):
    rows, keys = q.shape[0], k.shape[0]
    nq, nk = rows // block, keys // block
    q_spec = pl.BlockSpec((block, D), lambda i, j, f: (i, 0))
    k_spec = pl.BlockSpec((block, D), lambda i, j, f: (j, 0))
    col_spec = pl.BlockSpec((block, 1), lambda i, j, f: (i, 0))
    row_spec = pl.BlockSpec((1, 1, block), lambda i, j, f: (j, 0, 0))
    return pl.pallas_call(
        attend_kernel,
        grid_spec=pltpu.PrefetchScalarGridSpec(
            num_scalar_prefetch=1,
            grid=(nq, nk),
            in_specs=[q_spec, k_spec, k_spec, col_spec, col_spec, row_spec, row_spec, row_spec],
            out_specs=[q_spec, q_spec, pl.BlockSpec((1, 16, block), lambda i, j, f: (i, 0, 0))],
            scratch_shapes=[
                pltpu.VMEM((HEADS, block, 1), f32),
                pltpu.VMEM((HEADS, block, 1), f32),
                pltpu.VMEM((block, D), f32),
            ],
        ),
        out_shape=[
            jax.ShapeDtypeStruct((rows, D), f32),
            jax.ShapeDtypeStruct((rows, D), bf16),
            jax.ShapeDtypeStruct((nq, 16, block), f32),
        ],
        compiler_params=pltpu.CompilerParams(vmem_limit_bytes=VMEM),
        name="attend",
    )(flags, q, k, v, seg_q, rot_q, seg_k, rot_k, val_k)


def attend_back_kernel(
    flag_ref, q_ref, do_ref, k_ref, v_ref, lse_ref, delta_ref, sq_ref, rq_ref,
    sk_ref, rk_ref, vk_ref, cosk_ref, sink_ref, cosq_ref, sinq_ref,
    dq_ref, dk_ref, dv_ref, dq_sc, dk_sc, dv_sc,
):
    j, i = pl.program_id(0), pl.program_id(1)
    nk, nq = pl.num_programs(0), pl.num_programs(1)
    rows = q_ref.shape[0]
    first = first_head(rows)
    none = jnp.zeros((), bf16)

    @pl.when(i == 0)
    def _():
        dk_sc[...] = jnp.zeros(dk_sc.shape, f32)
        dv_sc[...] = jnp.zeros(dv_sc.shape, f32)

    @pl.when(j == 0)
    def _():
        dq_sc[i] = jnp.zeros(dq_sc.shape[1:], f32)

    @pl.when(flag_ref[i * nk + j] > 0)
    def _():
        sk = sk_ref[...]
        ok = (vk_ref[...] > 0) & ((sk == 0) | (sk == sq_ref[0])) & (rk_ref[...] <= rq_ref[0])
        bias = jnp.where(ok, 0.0, NEG)
        for g in range(GRPS):
            at = slice(g * LANES, (g + 1) * LANES)
            q2, k2, v2, do2 = q_ref[:, at], k_ref[:, at], v_ref[:, at], do_ref[:, at]
            dq, dk, dv = [], [], []
            for half in range(2):
                h = 2 * g + half
                mine = first if half == 0 else ~first
                qm = jnp.where(mine, q2, none)
                dom = jnp.where(mine, do2, none)
                km = jnp.where(mine, k2, none)
                s = mm(k2, qm, NT) + bias
                p = jnp.exp(s - lse_ref[0, h : h + 1, :])
                dp = mm(v2, dom, NT)
                ds = (p * (dp - delta_ref[0, h : h + 1, :])).astype(bf16)
                dv.append(mm(p.astype(bf16), dom))
                dk.append(mm(ds, qm))
                dq.append(mm(ds, km, TN))
            dv_sc[:, at] += dv[0] + dv[1]
            dk_sc[:, at] += dk[0] + dk[1]
            dq_sc[i, :, at] += dq[0] + dq[1]

    @pl.when(i == nq - 1)
    def _():
        dk_ref[...] = turn(dk_sc[...], cosk_ref[...], -sink_ref[...]).astype(bf16)
        dv_ref[...] = dv_sc[...].astype(bf16)

    @pl.when(j == nk - 1)
    def _():
        back = turn(dq_sc[i], cosq_ref[...], -sinq_ref[...])
        dq_ref[...] = (back * (1.0 / math.sqrt(HD))).astype(bf16)


def attend_back(flags, q, d_o, k, v, lse, delta, seg_q, rot_q, seg_k, rot_k, val_k, cosine, sine, block):
    rows, keys = q.shape[0], k.shape[0]
    nq, nk = rows // block, keys // block
    q_spec = pl.BlockSpec((block, D), lambda j, i, f: (i, 0))
    k_spec = pl.BlockSpec((block, D), lambda j, i, f: (j, 0))
    stat_spec = pl.BlockSpec((1, 16, block), lambda j, i, f: (i, 0, 0))
    row_spec = pl.BlockSpec((1, 1, block), lambda j, i, f: (i, 0, 0))
    col_spec = pl.BlockSpec((block, 1), lambda j, i, f: (j, 0))
    tabk_spec = pl.BlockSpec((block, LANES), lambda j, i, f: (j, 0))
    tabq_spec = pl.BlockSpec((block, LANES), lambda j, i, f: (i, 0))
    return pl.pallas_call(
        attend_back_kernel,
        grid_spec=pltpu.PrefetchScalarGridSpec(
            num_scalar_prefetch=1,
            grid=(nk, nq),
            in_specs=[q_spec, q_spec, k_spec, k_spec, stat_spec, stat_spec, row_spec, row_spec]
            + [col_spec] * 3
            + [tabk_spec] * 2
            + [tabq_spec] * 2,
            out_specs=[
                pl.BlockSpec((block, D), lambda j, i, f: (jnp.where(j == nk - 1, i, 0), 0)),
                k_spec,
                k_spec,
            ],
            scratch_shapes=[
                pltpu.VMEM((nq, block, D), f32),
                pltpu.VMEM((block, D), f32),
                pltpu.VMEM((block, D), f32),
            ],
        ),
        out_shape=[
            jax.ShapeDtypeStruct((rows, D), bf16),
            jax.ShapeDtypeStruct((keys, D), bf16),
            jax.ShapeDtypeStruct((keys, D), bf16),
        ],
        compiler_params=pltpu.CompilerParams(vmem_limit_bytes=VMEM),
        name="attend_back",
    )(flags, q, d_o, k, v, lse, delta, seg_q, rot_q, seg_k, rot_k, val_k, cosine, sine, cosine, sine)


def unit_kernel(down_dims, chunk, x_ref, gy_ref, wg_ref, wu_ref, wd_ref, y_ref, gx_ref, he_ref, da_ref, db_ref, y_sc, gx_sc):
    f = pl.program_id(0)
    rows = x_ref.shape[0]
    wg, wu, wd = wg_ref[...].reshape(D, TILE), wu_ref[...].reshape(D, TILE), wd_ref[...]
    wd = wd.reshape(wd.shape[-2:])
    up_dims, back_dims = (NN, NT) if down_dims is NT else (NT, NN)
    for c in range(rows // chunk):
        at = slice(c * chunk, (c + 1) * chunk)
        x, gy = x_ref[at, :], gy_ref[at, :]
        ha, hb = mm(x, wg), mm(x, wu)
        dh = mm(gy, wd, up_dims)
        sg = 1.0 / (1.0 + jnp.exp(-ha))
        si = ha * sg
        he = (si * hb).astype(bf16)
        da = (dh * hb * (sg * (1.0 + ha * (1.0 - sg)))).astype(bf16)
        db = (dh * si).astype(bf16)
        he_ref[at, :] = he
        da_ref[at, :] = da
        db_ref[at, :] = db
        y = mm(he, wd, back_dims)
        gx = mm(da, wg, NT) + mm(db, wu, NT)

        @pl.when(f == 0)
        def _():
            y_sc[at, :] = y
            gx_sc[at, :] = gx

        @pl.when(f > 0)
        def _():
            y_sc[at, :] += y
            gx_sc[at, :] += gx

    @pl.when(f == pl.num_programs(0) - 1)
    def _():
        y_ref[...] = y_sc[...].astype(y_ref.dtype)
        gx_ref[...] = gx_sc[...].astype(gx_ref.dtype)


def unit(x, gy, weights, specs, down_dims, hidden, dtype, chunk):
    rows = x.shape[0]
    tile_spec = pl.BlockSpec((rows, TILE), lambda f: (0, f))
    kept = jax.ShapeDtypeStruct((rows, hidden), bf16)
    wide = jax.ShapeDtypeStruct((rows, D), dtype)
    return pl.pallas_call(
        functools.partial(unit_kernel, down_dims, chunk),
        grid=(hidden // TILE,),
        in_specs=[const_spec((rows, D))] * 2 + specs,
        out_specs=[const_spec((rows, D))] * 2 + [tile_spec] * 3,
        out_shape=[wide, wide, kept, kept, kept],
        scratch_shapes=[pltpu.VMEM((rows, D), f32), pltpu.VMEM((rows, D), f32)],
        compiler_params=pltpu.CompilerParams(vmem_limit_bytes=VMEM),
        name="unit",
    )(x, gy, *weights)


def expert_grads_kernel(xt_ref, gt_ref, he_ref, da_ref, db_ref, out_ref):
    xt = xt_ref[...]
    out_ref[0, 0] = mm(xt, da_ref[...]).astype(bf16)
    out_ref[0, 1] = mm(xt, db_ref[...]).astype(bf16)
    out_ref[0, 2] = mm(gt_ref[...], he_ref[...]).astype(bf16)


def expert_grads(xt, gt, he, da, db, shards):
    rows, hidden = he.shape
    part = hidden // shards
    per = part // TILE
    tile_spec = pl.BlockSpec((rows, TILE), lambda f: (0, f))
    return pl.pallas_call(
        expert_grads_kernel,
        grid=(hidden // TILE,),
        in_specs=[const_spec((D, rows))] * 2 + [tile_spec] * 3,
        out_specs=pl.BlockSpec((1, 3, D, TILE), lambda f: (f // per, 0, 0, f % per)),
        out_shape=jax.ShapeDtypeStruct((shards, 3, D, part), bf16),
        compiler_params=pltpu.CompilerParams(vmem_limit_bytes=VMEM),
        name="expert_grads",
    )(xt, gt, he, da, db)


EVERY = ("ctx", "fsdp")


def swap_fsdp(values):
    return lax.all_to_all(values, "fsdp", split_axis=0, concat_axis=0, tiled=True)


def peer(values, axis, size, step):
    return lax.ppermute(values, axis, [(i, i ^ step) for i in range(size)])


def scatter_sum(chunks, n_ctx, n_fsdp):
    rows, width = chunks.shape[1:]
    pairs = n_fsdp // 2
    odd = lax.axis_index("fsdp") % 2
    view = chunks.reshape(n_ctx * pairs, 2, rows, width)
    keep = jnp.where(odd == 0, view[:, 0], view[:, 1])
    give = jnp.where(odd == 0, view[:, 1], view[:, 0])
    got = peer(give, "fsdp", n_fsdp, 1)
    part = (keep.astype(f32) + got.astype(f32)).astype(bf16).reshape(n_ctx, pairs, rows, width)
    part = lax.all_to_all(part, "ctx", split_axis=0, concat_axis=0, tiled=True)
    part = jnp.sum(part.astype(f32), axis=0).astype(bf16)
    groups = [[2 * i + c for i in range(pairs)] for c in range(2)]
    part = lax.all_to_all(part, "fsdp", split_axis=0, concat_axis=0, tiled=True, axis_index_groups=groups)
    return jnp.sum(part.astype(f32), axis=0)


def norm_back(values, inv, gain, grad):
    scaled = grad * gain
    mean = jnp.mean(scaled * values, axis=-1, keepdims=True)
    return inv * scaled - values * (inv * inv * inv * mean)


def inverse_rms(values):
    return lax.rsqrt(jnp.mean(values * values, axis=-1, keepdims=True) + EPS)


def positions(order, order_rows, segment_row, valid_row, block):
    blocks = order_rows
    hot = order[:, None] == jnp.arange(blocks, dtype=i32)[None, :]

    def pick(row):
        return jnp.sum(jnp.where(hot[:, :, None], row.reshape(1, blocks, block), 0), axis=1)

    segment, valid = pick(segment_row), pick(valid_row)
    position = order[:, None] * block + jnp.arange(block, dtype=i32)[None, :]
    bounds = jnp.arange(NCONT + 1, dtype=i32)
    starts = jnp.sum((segment_row[None, :] < bounds[:, None]).astype(i32), axis=1)
    begin = jnp.sum(jnp.where(segment[:, :, None] == bounds, starts, 0), axis=-1)
    rotary = position - begin + jnp.where(segment > 0, starts[1], 0)
    return segment, rotary, valid


def local(
    n_ctx, n_fsdp,
    tokens, cotangent, block_order, segment_ids, valid_mask, routes,
    attention_gain, query_weight, key_weight, value_weight, out_weight,
    feedforward_gain, router, shared_gate, shared_up, shared_down,
    expert_gate, expert_up, expert_down,
):
    devices = n_ctx * n_fsdp
    x_low, c_low = tokens[0], cotangent[0]
    rows = x_low.shape[0]
    group = segment_ids.shape[1]
    blocks = block_order.shape[1]
    block = group // blocks
    own = rows // block
    experts = n_fsdp
    cap = 2 * rows * TOPK // experts
    slots = experts * cap
    my_ctx = lax.axis_index("ctx")
    my_fsdp = lax.axis_index("fsdp")
    shard = query_weight.shape[0]
    down_shard = shared_down.shape[0]
    hidden = shared_gate.shape[1]
    tiles = hidden // TILE
    wide = D // TILE

    misc = jnp.concatenate([router.reshape(-1), attention_gain, feedforward_gain])
    misc = jnp.pad(misc, (0, 8 * D - misc.shape[0])).reshape(8, D)
    pack = jnp.concatenate([query_weight, key_weight, value_weight, out_weight, misc], axis=0)
    dense = lax.all_gather(pack, EVERY, axis=0, tiled=False)
    wq, wk, wv, wo = (dense[:, n * shard : (n + 1) * shard].reshape(D, D) for n in range(4))
    extra = dense[:, 4 * shard]
    full_router = extra[:, : shard * experts].reshape(D, experts)
    gain_one = extra[:, shard * experts : shard * (experts + 1)].reshape(1, D).astype(f32)
    gain_two = extra[:, shard * (experts + 1) : shard * (experts + 2)].reshape(1, D).astype(f32)

    mine = jnp.stack([expert_gate[0], expert_up[0], expert_down[0].T])
    mine, _ = lax.optimization_barrier((mine, extra))
    expert_w = lax.all_gather(mine, "ctx", axis=0, tiled=False)

    def pieces(array):
        r, w = array.shape
        return array.reshape(r, w // TILE, TILE).transpose(1, 0, 2).reshape(-1, TILE)

    spack = jnp.concatenate([pieces(shared_gate), pieces(shared_up), pieces(shared_down)], axis=0)
    spack, _ = lax.optimization_barrier((spack, expert_w[0, 0, :8, :LANES]))
    shared_w = lax.all_gather(spack, EVERY, axis=0, tiled=False)
    cut = 2 * tiles * shard
    shared_gu = (
        shared_w[:, :cut].reshape(devices, 2 * tiles, shard, TILE).transpose(1, 0, 2, 3).reshape(2 * tiles, D, TILE)
    )
    shared_d = (
        shared_w[:, cut:].reshape(devices, wide, down_shard, TILE).transpose(0, 2, 1, 3).reshape(hidden, D)
    )

    x_all = jnp.concatenate(
        [x_low] + [peer(x_low, "ctx", n_ctx, step) for step in range(1, n_ctx)], axis=0
    )
    dev = my_ctx ^ jnp.arange(n_ctx, dtype=i32)
    which = (dev[:, None] * own + jnp.arange(own, dtype=i32)[None, :]).reshape(-1)
    order = jnp.sum(
        jnp.where(which[:, None] == jnp.arange(blocks, dtype=i32)[None, :], block_order[0][None, :], 0), axis=1
    )
    seg, rot, val = positions(order, blocks, segment_ids[0], valid_mask[0], block)
    seg_q, rot_q = seg[:own], rot[:own]
    allowed = (
        (val[None, :, None, :] > 0)
        & ((seg[None, :, None, :] == 0) | (seg[None, :, None, :] == seg_q[:, None, :, None]))
        & (rot[None, :, None, :] <= rot_q[:, None, :, None])
    )
    flags = jnp.any(allowed, axis=(2, 3)).astype(i32).reshape(-1)
    half = HD // 2
    lane = jnp.arange(LANES, dtype=i32)
    frequency = jnp.exp((lane % half).astype(f32) * (-math.log(BASE) / half))
    angles = rot.reshape(-1).astype(f32)[:, None] * frequency[None, :]
    cosine = jnp.cos(angles)
    sine = jnp.sin(angles) * jnp.where(lane % HD < half, -1.0, 1.0)
    rows3 = lambda a: a.reshape(-1, 1, block)
    cols = lambda a: a.reshape(-1, 1)

    chosen = routes[0]
    every = jnp.arange(experts, dtype=i32)
    hot_k = chosen[:, :, None] == every
    hot = jnp.any(hot_k, axis=1)
    before = (jnp.arange(rows)[:, None] > jnp.arange(rows)[None, :]).astype(bf16)
    rank = mm(before, hot.astype(bf16)).astype(i32)
    slot_of = jnp.where(hot, rank, -1)
    place = slot_of.T[:, None, :] == jnp.arange(cap, dtype=i32)[None, :, None]
    send = place.astype(bf16).reshape(slots, rows)
    flat = chosen * cap + jnp.sum(jnp.where(hot_k, rank[:, None, :], 0), axis=-1)
    slot_ids = jnp.arange(slots, dtype=i32)
    fetch = [(flat[:, k : k + 1] == slot_ids[None, :]) for k in range(TOPK)]

    c_slots = swap_fsdp(mm(send, c_low).astype(bf16).reshape(experts, cap, D)).reshape(slots, D)

    x_in = x_low.astype(f32)
    n_all, q, k, v = project(x_all, gain_one, wq, wk, wv, cosine, sine, block, own)
    attn, attn_low, lse = attend(
        flags, q, k, v, cols(seg_q), cols(rot_q), rows3(seg), rows3(rot), rows3(val), block
    )
    attn_out = mm(attn_low, wo)
    resid = x_in + attn_out
    inv_two = inverse_rms(resid)
    n_two = (resid * inv_two * gain_two).astype(bf16)
    logits = mm(n_two, full_router)

    picked = jnp.sum(jnp.where(hot_k, logits[:, None, :], 0.0), axis=-1)
    top = jnp.max(picked, axis=-1, keepdims=True)
    powers = jnp.exp(picked - top)
    gates = powers / jnp.sum(powers, axis=-1, keepdims=True)
    gate_of = jnp.sum(jnp.where(hot_k, gates[:, :, None], 0.0), axis=1)
    gate_slots = jnp.sum(jnp.where(place, gate_of.T[:, None, :], 0.0), axis=-1)
    gate_slots = swap_fsdp(gate_slots).reshape(slots, 1)

    x_slots = swap_fsdp(mm(send, n_two).astype(bf16).reshape(experts, cap, D)).reshape(slots, D)

    gy_slots = (gate_slots * c_slots.astype(f32)).astype(bf16)
    per = hidden // n_ctx // TILE
    e_specs = [
        pl.BlockSpec((1, 1, D, TILE), lambda f, w=w: (f // per, w, 0, f % per)) for w in range(3)
    ]
    y_slots, gx_slots, e_he, e_da, e_db = unit(
        x_slots, gy_slots, (expert_w,) * 3, e_specs, NT, hidden, bf16, rows
    )
    dg_slots = jnp.sum(c_slots.astype(f32) * y_slots.astype(f32), axis=-1).reshape(experts, cap)
    gx_back = swap_fsdp(gx_slots.reshape(experts, cap, D)).reshape(slots, D)
    dg_back = swap_fsdp(dg_slots).reshape(1, slots)
    y_back = swap_fsdp(y_slots.reshape(experts, cap, D)).reshape(slots, D)
    e_grads = expert_grads(x_slots.T, gy_slots.T, e_he, e_da, e_db, n_ctx)
    e_grads = lax.psum_scatter(e_grads, "ctx", scatter_dimension=0, tiled=False).astype(f32)

    s_specs = [
        pl.BlockSpec((1, D, TILE), lambda f: (f, 0, 0)),
        pl.BlockSpec((1, D, TILE), lambda f: (tiles + f, 0, 0)),
        pl.BlockSpec((TILE, D), lambda f: (f, 0)),
    ]
    s_out, s_dn, s_he, s_da, s_db = unit(
        n_two, c_low, (shared_gu, shared_gu, shared_d), s_specs, NN, hidden, f32, rows
    )
    n_two_t = n_two.T
    s_dgate, s_dup = mm(n_two_t, s_da).astype(bf16), mm(n_two_t, s_db).astype(bf16)
    s_ddown = mm(s_he, c_low, TN).astype(bf16)

    def to_pieces(array, part):
        w = array.shape[1] // TILE
        return array.reshape(devices, part, w, TILE).transpose(0, 2, 1, 3).reshape(devices, w * part, TILE)

    s_pack = jnp.concatenate(
        [to_pieces(s_dgate, shard), to_pieces(s_dup, shard), to_pieces(s_ddown, down_shard)], axis=1
    )
    s_grads = lax.psum_scatter(s_pack, EVERY, scatter_dimension=0, tiled=False).astype(f32)

    def from_pieces(array, part):
        return array.reshape(-1, part, TILE).transpose(1, 0, 2).reshape(part, -1)

    grad_shared_gate = from_pieces(s_grads[: tiles * shard], shard)
    grad_shared_up = from_pieces(s_grads[tiles * shard : cut], shard)
    grad_shared_down = from_pieces(s_grads[cut:], down_shard)

    pair = [mm(m.astype(bf16), y_back) for m in fetch]
    moe = sum(gates[:, n : n + 1] * pair[n] for n in range(TOPK))
    ffn = moe + s_out
    result = resid + ffn
    output = result.astype(bf16)[None]
    keep = cols(val[:own].astype(f32))
    sums = jnp.stack([jnp.sum(keep * a * a) for a in (x_in, attn_out, ffn, result)])

    d_gates = jnp.concatenate(
        [jnp.sum(jnp.where(m, dg_back, 0.0), axis=-1, keepdims=True) for m in fetch], axis=-1
    )
    d_picked = gates * (d_gates - jnp.sum(gates * d_gates, axis=-1, keepdims=True))
    d_logits = jnp.sum(jnp.where(hot_k, d_picked[:, :, None], 0.0), axis=1)
    grad_router = lax.dot_general(n_two.astype(f32), d_logits, TN, precision=HIGH, preferred_element_type=f32)
    d_two = (
        mm(send, gx_back, TN)
        + lax.dot_general(d_logits, full_router.astype(f32), NT, precision=HIGH, preferred_element_type=f32)
        + s_dn
    )
    grad_gain_two = jnp.sum(d_two * resid * inv_two, axis=0)
    d_resid = c_low.astype(f32) + norm_back(resid, inv_two, gain_two, d_two)
    d_attn = d_resid.astype(bf16)
    grad_out = mm(attn_low, d_attn, TN).astype(bf16)
    d_mix = mm(d_attn, wo, NT).astype(bf16)
    head_of = (jnp.arange(D, dtype=i32)[None, :] // HD == jnp.arange(16, dtype=i32)[:, None]).astype(f32)
    delta = lax.dot_general(
        head_of, d_mix.astype(f32) * attn, NT, precision=HIGH, preferred_element_type=f32
    )
    delta = delta.reshape(16, own, block).transpose(1, 0, 2)

    dq, dk, dv = attend_back(
        flags, q, d_mix, k, v, lse, delta, rows3(seg_q), rows3(rot_q), cols(seg), cols(rot), cols(val),
        cosine, sine, block,
    )
    d_norm = mm(dk, wk, NT) + mm(dv, wv, NT)
    d_norm_own = d_norm[:rows] + mm(dq, wq, NT)
    d_low = d_norm.astype(bf16)
    x_f = x_all.astype(f32)
    inv_all = inverse_rms(x_f)
    scaled_x = x_f * inv_all
    grad_gain_one = jnp.sum(d_norm_own * scaled_x[:rows], axis=0) + jnp.sum(
        d_norm[rows:] * scaled_x[rows:], axis=0
    )
    got = [peer(d_low[n * rows : (n + 1) * rows], "ctx", n_ctx, n) for n in range(1, n_ctx)]
    d_first = d_norm_own + sum(g.astype(f32) for g in got)
    input_grad = (d_resid + norm_back(x_in, inv_all[:rows], gain_one, d_first))[None]

    grad_query = mm(n_all[:rows], dq, TN).astype(bf16)
    grad_key = mm(n_all, dk, TN).astype(bf16)
    grad_value = mm(n_all, dv, TN).astype(bf16)
    chunks = jnp.concatenate(
        [a.reshape(devices, shard, D) for a in (grad_query, grad_key, grad_value, grad_out)], axis=1
    )
    dense_grads = scatter_sum(chunks, n_ctx, n_fsdp)
    g_query, g_key, g_value, g_out = (dense_grads[n * shard : (n + 1) * shard] for n in range(4))

    to_group = jnp.where(
        (jnp.arange(devices, dtype=i32) % n_fsdp == my_fsdp)[:, None], sums[None, :], 0.0
    )
    small = jnp.concatenate(
        [
            grad_router.reshape(devices, shard * experts),
            grad_gain_one.reshape(devices, shard),
            grad_gain_two.reshape(devices, shard),
            to_group,
        ],
        axis=1,
    )
    width = small.shape[1]
    small = jnp.pad(small, ((0, 0), (0, -width % LANES)))
    small = jnp.sum(lax.all_to_all(small, EVERY, split_axis=0, concat_axis=0, tiled=True), axis=0)
    g_router = small[: shard * experts].reshape(shard, experts)
    g_gain_one = small[shard * experts : shard * (experts + 1)]
    g_gain_two = small[shard * (experts + 1) : shard * (experts + 2)]
    group_sums = small[shard * (experts + 2) : width]
    valid_count = jnp.sum(valid_mask[0]).astype(f32)
    stats = jnp.sqrt(group_sums / (valid_count * D))[None]

    return (
        output, input_grad, g_gain_one, g_query, g_key, g_value, g_out, g_gain_two, g_router,
        grad_shared_gate, grad_shared_up, grad_shared_down,
        e_grads[0][None], e_grads[1][None], e_grads[2].T[None], stats,
    )


def solution(mesh):
    sizes = dict(mesh.shape)
    rows3 = P("fsdp", "ctx", None)
    group = P("fsdp", None)
    dense1 = P(("ctx", "fsdp"))
    dense2 = P(("ctx", "fsdp"), None)
    column = P("fsdp", None, "ctx")
    return jax.shard_map(
        functools.partial(local, sizes["ctx"], sizes["fsdp"]),
        mesh=mesh,
        in_specs=(rows3, rows3, group, group, group, rows3)
        + (dense1, dense2, dense2, dense2, dense2, dense1)
        + (dense2,) * 4
        + (column, column, rows3),
        out_specs=(rows3, rows3)
        + (dense1, dense2, dense2, dense2, dense2, dense1)
        + (dense2,) * 4
        + (column, column, rows3, group),
        check_vma=False,
    )
```

```python
import functools
import math

import jax
import jax.numpy as jnp
from jax import lax
from jax.experimental import pallas as pl
from jax.experimental.pallas import tpu as pltpu
from jax.sharding import PartitionSpec as P

D = 768
HEADS = 12
HD = 64
TOPK = 2
NCONT = 4

HIGH = lax.Precision.HIGHEST
EPS = 1e-06
NEG = -1e30
FLOOR = -5e29
BASE = 10000.0
LANES = 128
TILE = 256
GRPS = D // LANES
VMEM = 60 * 1024 * 1024

f32 = jnp.float32
bf16 = jnp.bfloat16
i32 = jnp.int32

NT = (((1,), (1,)), ((), ()))
NN = (((1,), (0,)), ((), ()))
TN = (((0,), (0,)), ((), ()))


def mm(a, b, dims=NN):
    return lax.dot_general(a, b, dims, preferred_element_type=f32)


def low_lanes(rows):
    lane = lax.broadcasted_iota(i32, (rows, LANES), 1)
    return lane % HD < HD // 2


def first_head(rows):
    return lax.broadcasted_iota(i32, (rows, LANES), 1) < HD


def turn(values, cosine, sine):
    low = low_lanes(values.shape[0])
    parts = []
    for g in range(GRPS):
        part = values[:, g * LANES : (g + 1) * LANES]
        other = jnp.where(
            low, pltpu.roll(part, LANES - HD // 2, 1), pltpu.roll(part, HD // 2, 1)
        )
        parts.append(part * cosine + other * sine)
    return jnp.concatenate(parts, axis=1)


def const_spec(shape):
    zeros = (0,) * len(shape)
    return pl.BlockSpec(shape, lambda *_: zeros)


def cost(flops, moved):
    return pl.CostEstimate(flops=int(flops), transcendentals=0, bytes_accessed=int(moved))


WIDE = D // TILE


def times(rows, pieces, out_dtype=f32):
    parts = [mm(rows, p[...].reshape(D, TILE)) for p in pieces]
    return jnp.concatenate(parts, axis=1).astype(out_dtype)


def times_back(rows, pieces):
    parts = [mm(rows[:, n * TILE : (n + 1) * TILE], p[...].reshape(D, TILE), NT) for n, p in enumerate(pieces)]
    return parts[0] + parts[1] + parts[2]


def piece_specs(held, first, count):
    groups, part = held
    return [pl.BlockSpec((groups, part, TILE), lambda *_, p=p: (0, p, 0)) for p in range(first, first + count)]


def qkv_kernel(own, x_ref, gain_ref, *refs):
    wq, wk, wv = refs[:WIDE], refs[WIDE : 2 * WIDE], refs[2 * WIDE : 3 * WIDE]
    cos_ref, sin_ref, n_ref, q_ref, k_ref, v_ref, vt_ref = refs[3 * WIDE :]
    x = x_ref[...].astype(f32)
    inv = lax.rsqrt(jnp.mean(x * x, axis=-1, keepdims=True) + EPS)
    n = (x * inv * gain_ref[...]).astype(bf16)
    n_ref[...] = n
    cosine = cos_ref[...]
    sine = sin_ref[...]
    k_ref[...] = turn(times(n, wk), cosine, sine).astype(bf16)
    v = times(n, wv, bf16)
    v_ref[...] = v
    block = vt_ref.shape[2]
    for b in range(vt_ref.shape[0]):
        vt_ref[b] = v[b * block : (b + 1) * block].T

    @pl.when(pl.program_id(0) < own)
    def _():
        q = turn(times(n, wq), cosine, sine)
        q_ref[...] = (q * (1.0 / math.sqrt(HD))).astype(bf16)


def project(x_all, gain, dense, held, cosine, sine, block, step, own):
    rows = x_all.shape[0]
    row_spec = pl.BlockSpec((step, D), lambda i: (i, 0))
    tab_spec = pl.BlockSpec((step, LANES), lambda i: (i, 0))
    wide = jax.ShapeDtypeStruct((rows, D), bf16)
    return pl.pallas_call(
        functools.partial(qkv_kernel, own),
        grid=(rows // step,),
        in_specs=[row_spec, const_spec((1, D))] + piece_specs(held, 0, 3 * WIDE) + [tab_spec] * 2,
        out_specs=[
            row_spec,
            pl.BlockSpec((step, D), lambda i: (jnp.minimum(i, own - 1), 0)),
            row_spec,
            row_spec,
            pl.BlockSpec((step // block, D, block), lambda i: (i, 0, 0)),
        ],
        out_shape=[
            wide,
            jax.ShapeDtypeStruct((own * step, D), bf16),
            wide,
            wide,
            jax.ShapeDtypeStruct((rows // block, D, block), bf16),
        ],
        compiler_params=pltpu.CompilerParams(vmem_limit_bytes=VMEM),
        cost_estimate=cost(12e9, 14 * rows * D),
        name="qkv",
    )(x_all, gain, *[dense] * (3 * WIDE), cosine, sine)


def mid_kernel(cap, o_ref, x_ref, gain_ref, slot_ref, *refs):
    wo = refs[:WIDE]
    resid_ref, n_ref, inv_ref, send_ref = refs[WIDE:]
    resid = x_ref[...].astype(f32) + times(o_ref[...], wo)
    inv = lax.rsqrt(jnp.mean(resid * resid, axis=-1, keepdims=True) + EPS)
    n = (resid * inv * gain_ref[...]).astype(bf16)
    resid_ref[...] = resid
    n_ref[...] = n
    inv_ref[...] = inv
    place = lax.broadcasted_iota(i32, (cap, n.shape[0]), 0)
    for e in range(slot_ref.shape[0]):
        hot = (slot_ref[e : e + 1, :] == place).astype(f32).astype(bf16)
        send_ref[e] = mm(hot, n).astype(bf16)


def mid(attn_low, x_low, gain, slot_rows, dense, held, cap):
    rows = x_low.shape[0]
    experts = slot_rows.shape[0]
    return pl.pallas_call(
        functools.partial(mid_kernel, cap),
        grid=(1,),
        in_specs=[const_spec((rows, D)), const_spec((rows, D)), const_spec((1, D)), const_spec((experts, rows))]
        + piece_specs(held, 3 * WIDE, WIDE),
        out_specs=[const_spec((rows, D))] * 2 + [const_spec((rows, 1)), const_spec((experts, cap, D))],
        out_shape=[
            jax.ShapeDtypeStruct((rows, D), f32),
            jax.ShapeDtypeStruct((rows, D), bf16),
            jax.ShapeDtypeStruct((rows, 1), f32),
            jax.ShapeDtypeStruct((experts, cap, D), bf16),
        ],
        compiler_params=pltpu.CompilerParams(vmem_limit_bytes=VMEM),
        cost_estimate=cost(5e9, 8 * experts * cap * D),
        name="mid",
    )(attn_low, x_low, gain, slot_rows, *[dense] * WIDE)


def mid_back_kernel(
    cap, block, gx_ref, slot_ref, sdn_ref, resid_ref, inv_ref, gain_ref, c_ref, attn_ref, *refs
):
    wo = refs[:WIDE]
    dres_ref, dattn_ref, dmix_ref, delta_ref, ggain_ref = refs[WIDE:]
    resid, inv, gain = resid_ref[...], inv_ref[...], gain_ref[...]
    rows = resid.shape[0]
    place = lax.broadcasted_iota(i32, (rows, cap), 1)
    grad = sdn_ref[...]
    for e in range(gx_ref.shape[0]):
        hot = (slot_ref[:, e : e + 1] == place).astype(f32).astype(bf16)
        grad += mm(hot, gx_ref[e])
    ggain_ref[...] = jnp.sum(grad * resid * inv, axis=0, keepdims=True)
    dres = c_ref[...].astype(f32) + norm_back(resid, inv, gain, grad)
    dres_ref[...] = dres
    dattn = dres.astype(bf16)
    dattn_ref[...] = dattn
    dmix = times_back(dattn, wo)
    dmix = dmix.astype(bf16)
    dmix_ref[...] = dmix
    prod = dmix.astype(f32) * attn_ref[...]
    high = prod.astype(bf16)
    rest = (prod - high.astype(f32)).astype(bf16)
    lane = lax.broadcasted_iota(i32, (16, D), 1)
    head = lax.broadcasted_iota(i32, (16, D), 0)
    pick = (lane // HD == head).astype(f32).astype(bf16)
    for b in range(delta_ref.shape[0]):
        at = slice(b * block, (b + 1) * block)
        delta_ref[b] = mm(pick, high[at], NT) + mm(pick, rest[at], NT)


def mid_back(gx_back, slot_cols, s_dn, resid, inv, gain, c_low, attn, dense, held, block):
    rows = resid.shape[0]
    experts, cap, _ = gx_back.shape
    row = const_spec((rows, D))
    return pl.pallas_call(
        functools.partial(mid_back_kernel, cap, block),
        grid=(1,),
        in_specs=[
            const_spec((experts, cap, D)), const_spec((rows, experts)), row, row, const_spec((rows, 1)),
            const_spec((1, D)), row, row,
        ]
        + piece_specs(held, 3 * WIDE, WIDE),
        out_specs=[row, row, row, const_spec((rows // block, 16, block)), const_spec((1, D))],
        out_shape=[
            jax.ShapeDtypeStruct((rows, D), f32),
            jax.ShapeDtypeStruct((rows, D), bf16),
            jax.ShapeDtypeStruct((rows, D), bf16),
            jax.ShapeDtypeStruct((rows // block, 16, block), f32),
            jax.ShapeDtypeStruct((1, D), f32),
        ],
        compiler_params=pltpu.CompilerParams(vmem_limit_bytes=VMEM),
        cost_estimate=cost(6e9, 8 * experts * cap * D),
        name="mid_back",
    )(gx_back, slot_cols, s_dn, resid, inv, gain, c_low, attn, *[dense] * WIDE)


def out_kernel(cap, y_ref, slot_ref, chosen_ref, n_ref, router_ref, sout_ref, resid_ref, x_ref, keep_ref, out_ref, sums_ref):
    rows = n_ref.shape[0]
    logits = mm(n_ref[...], router_ref[...])
    lane = lax.broadcasted_iota(i32, logits.shape, 1)
    first, second = chosen_ref[:, 0:1], chosen_ref[:, 1:2]
    gap = jnp.sum(jnp.where(lane == first, logits, 0.0), axis=-1, keepdims=True) - jnp.sum(
        jnp.where(lane == second, logits, 0.0), axis=-1, keepdims=True
    )
    gate_one = 1.0 / (1.0 + jnp.exp(-gap))
    gate_two = 1.0 / (1.0 + jnp.exp(gap))
    place = lax.broadcasted_iota(i32, (rows, cap), 1)
    ffn = sout_ref[...]
    for e in range(y_ref.shape[0]):
        hot = (slot_ref[:, e : e + 1] == place).astype(f32).astype(bf16)
        gate = jnp.where(first == e, gate_one, jnp.where(second == e, gate_two, 0.0))
        ffn += gate * mm(hot, y_ref[e])
    resid, x, keep = resid_ref[...], x_ref[...].astype(f32), keep_ref[...]
    result = resid + ffn
    out_ref[...] = result.astype(bf16)
    for n, a in enumerate((x, resid - x, ffn, result)):
        total = jnp.sum(keep * jnp.sum(a * a, axis=-1, keepdims=True), axis=0, keepdims=True)
        sums_ref[n : n + 1, :] = jnp.broadcast_to(total, (1, LANES))


def finish(y_back, slot_cols, chosen, n_two, router, s_out, resid, x_low, keep):
    rows = resid.shape[0]
    experts, cap, _ = y_back.shape
    row = const_spec((rows, D))
    return pl.pallas_call(
        functools.partial(out_kernel, cap),
        grid=(1,),
        in_specs=[
            const_spec((experts, cap, D)), const_spec((rows, experts)), const_spec((rows, TOPK)), row,
            const_spec((D, LANES)), row, row, row, const_spec((rows, 1)),
        ],
        out_specs=[row, const_spec((4, LANES))],
        out_shape=[jax.ShapeDtypeStruct((rows, D), bf16), jax.ShapeDtypeStruct((4, LANES), f32)],
        compiler_params=pltpu.CompilerParams(vmem_limit_bytes=VMEM),
        cost_estimate=cost(6e9, 8 * experts * cap * D),
        name="finish",
    )(y_back, slot_cols, chosen, n_two, router, s_out, resid, x_low, keep)


def tail_kernel(shard, odd_ref, n_ref, dk_ref, dv_ref, x_ref, dq_ref, o_ref, da_ref, gain_ref, *refs):
    wq, wk, wv = refs[:WIDE], refs[WIDE : 2 * WIDE], refs[2 * WIDE : 3 * WIDE]
    low_ref, own_ref, ggain_ref, grads_ref, acc = refs[3 * WIDE :]
    c = pl.program_id(0)
    dk, dv = dk_ref[...], dv_ref[...]
    dn = times_back(dk, wk) + times_back(dv, wv)
    nt = n_ref[...].T
    x = x_ref[...].astype(f32)
    scaled = x * lax.rsqrt(jnp.mean(x * x, axis=-1, keepdims=True) + EPS)
    low_ref[...] = dn.astype(bf16)

    @pl.when(c == 0)
    def _():
        own = dn + times_back(dq_ref[...], wq)
        own_ref[...] = own
        ggain_ref[...] = jnp.sum(own * scaled, axis=0, keepdims=True)
        acc[0] = mm(nt, dq_ref[...])
        acc[1] = mm(nt, dk)
        acc[2] = mm(nt, dv)
        acc[3] = mm(o_ref[...], da_ref[...], TN)

    @pl.when(c > 0)
    def _():
        ggain_ref[...] += jnp.sum(dn * scaled, axis=0, keepdims=True)
        acc[1] += mm(nt, dk)
        acc[2] += mm(nt, dv)

    @pl.when(c == pl.num_programs(0) - 1)
    def _():
        for n in range(4):
            if grads_ref.shape[0] == 1:
                grads_ref[0, n * D : (n + 1) * D, :] = acc[n].astype(bf16)
            else:
                grads_ref[:, n * shard : (n + 1) * shard, :] = acc[n].reshape(D // shard, shard, D).astype(bf16)


def tail(odd, n_all, dk, dv, x_all, dq, attn_low, d_attn, gain, dense, held, shard):
    keys, rows = n_all.shape[0], dq.shape[0]
    step = pl.BlockSpec((rows, D), lambda c, o: (c, 0))
    row = const_spec((rows, D))
    return pl.pallas_call(
        functools.partial(tail_kernel, shard),
        grid_spec=pltpu.PrefetchScalarGridSpec(
            num_scalar_prefetch=1,
            grid=(keys // rows,),
            in_specs=[step] * 4 + [row] * 3 + [const_spec((1, D))] + piece_specs(held, 0, 3 * WIDE),
            out_specs=[step, row, const_spec((1, D)), const_spec((held[0], 4 * held[1], D))],
            scratch_shapes=[pltpu.VMEM((4, D, D), f32)],
        ),
        out_shape=[
            jax.ShapeDtypeStruct((keys, D), bf16),
            jax.ShapeDtypeStruct((rows, D), f32),
            jax.ShapeDtypeStruct((1, D), f32),
            jax.ShapeDtypeStruct((held[0], 4 * held[1], D), bf16),
        ],
        compiler_params=pltpu.CompilerParams(vmem_limit_bytes=VMEM),
        cost_estimate=cost(25e9, 12 * keys * D),
        name="tail",
    )(odd, n_all, dk, dv, x_all, dq, attn_low, d_attn, gain, *[dense] * (3 * WIDE))


def split_heads(dst, values, first):
    none = jnp.zeros((), bf16)
    for g in range(GRPS):
        part = values[:, g * LANES : (g + 1) * LANES]
        dst[2 * g] = jnp.where(first, part, none)
        dst[2 * g + 1] = jnp.where(first, none, part)


def pair_lanes(h):
    return slice(h // 2 * LANES, (h // 2 + 1) * LANES)


def head_rows(h):
    return slice(h * HD, (h + 1) * HD)


def key_bias(sk_ref, rk_ref, sq_ref, rq_ref):
    sk = sk_ref[...]
    ok = ((sk == 0) | (sk == sq_ref[0])) & (rk_ref[...] <= rq_ref[0])
    return jnp.where(ok, 0.0, NEG)


def attend_kernel(
    flag_ref, q_ref, k_ref, vt_ref, sq_ref, rq_ref, sk_ref, rk_ref,
    o_ref, low_ref, lse_ref, qm_sc, m_sc, l_sc, acc_sc,
):
    i, j = pl.program_id(0), pl.program_id(1)
    count = pl.num_programs(1)

    @pl.when(j == 0)
    def _():
        m_sc[...] = jnp.full(m_sc.shape, FLOOR, f32)
        l_sc[...] = jnp.zeros(l_sc.shape, f32)
        acc_sc[...] = jnp.zeros(acc_sc.shape, f32)
        split_heads(qm_sc, q_ref[...], first_head(q_ref.shape[0]))

    @pl.when(flag_ref[i * count + j] > 0)
    def _():
        bias = key_bias(sk_ref, rk_ref, sq_ref, rq_ref)
        scores = [mm(k_ref[:, pair_lanes(h)], qm_sc[h], NT) + bias for h in range(HEADS)]
        m_old = m_sc[:HEADS]
        tops = [jnp.max(s, axis=0, keepdims=True) for s in scores]
        m_new = jnp.maximum(m_old, jnp.concatenate(tops, axis=0))
        a = jnp.exp(m_old - m_new)
        m_sc[:HEADS] = m_new
        probs = [jnp.exp(s - m_new[h : h + 1]) for h, s in enumerate(scores)]
        sums = [jnp.sum(p, axis=0, keepdims=True) for p in probs]
        l_sc[:HEADS] = l_sc[:HEADS] * a + jnp.concatenate(sums, axis=0)
        for h, p in enumerate(probs):
            at = head_rows(h)
            acc_sc[at] = acc_sc[at] * a[h : h + 1] + mm(vt_ref[0, at], p.astype(bf16))

    @pl.when(j == count - 1)
    def _():
        total = jnp.maximum(l_sc[...], 1e-30)
        lse_ref[0] = m_sc[...] + jnp.log(total)
        inv = 1.0 / total
        for h in range(HEADS):
            at = head_rows(h)
            acc_sc[at] = acc_sc[at] * inv[h : h + 1]
        o = acc_sc[...].T
        o_ref[...] = o
        low_ref[...] = o.astype(bf16)


def attend(flags, q, k, vt, seg_q, rot_q, seg_k, rot_k, block):
    rows, keys = q.shape[0], k.shape[0]
    nq, nk = rows // block, keys // block
    q_spec = pl.BlockSpec((block, D), lambda i, j, f: (i, 0))
    k_spec = pl.BlockSpec((block, D), lambda i, j, f: (j, 0))
    vt_spec = pl.BlockSpec((1, D, block), lambda i, j, f: (j, 0, 0))
    row_spec = pl.BlockSpec((1, 1, block), lambda i, j, f: (i, 0, 0))
    col_spec = pl.BlockSpec((block, 1), lambda i, j, f: (j, 0))
    return pl.pallas_call(
        attend_kernel,
        grid_spec=pltpu.PrefetchScalarGridSpec(
            num_scalar_prefetch=1,
            grid=(nq, nk),
            in_specs=[q_spec, k_spec, vt_spec, row_spec, row_spec, col_spec, col_spec],
            out_specs=[q_spec, q_spec, pl.BlockSpec((1, 16, block), lambda i, j, f: (i, 0, 0))],
            scratch_shapes=[
                pltpu.VMEM((HEADS, block, LANES), bf16),
                pltpu.VMEM((16, block), f32),
                pltpu.VMEM((16, block), f32),
                pltpu.VMEM((D, block), f32),
            ],
        ),
        out_shape=[
            jax.ShapeDtypeStruct((rows, D), f32),
            jax.ShapeDtypeStruct((rows, D), bf16),
            jax.ShapeDtypeStruct((nq, 16, block), f32),
        ],
        compiler_params=pltpu.CompilerParams(vmem_limit_bytes=VMEM),
        cost_estimate=cost(16e9, 6 * keys * D),
        name="attend",
    )(flags, q, k, vt, seg_q, rot_q, seg_k, rot_k)


def attend_back_kernel(
    flag_ref, q_ref, do_ref, k_ref, v_ref, lse_ref, delta_ref, sq_ref, rq_ref,
    sk_ref, rk_ref, cosk_ref, sink_ref, cosq_ref, sinq_ref,
    dq_ref, dk_ref, dv_ref, dq_sc, dk_sc, dv_sc, qm_sc, dom_sc,
):
    j, i = pl.program_id(0), pl.program_id(1)
    nk, nq = pl.num_programs(0), pl.num_programs(1)

    @pl.when(i == 0)
    def _():
        dk_sc[...] = jnp.zeros(dk_sc.shape, f32)
        dv_sc[...] = jnp.zeros(dv_sc.shape, f32)

    @pl.when(j == 0)
    def _():
        first = first_head(q_ref.shape[0])
        dq_sc[i] = jnp.zeros(dq_sc.shape[1:], f32)
        split_heads(qm_sc.at[i], q_ref[...], first)
        split_heads(dom_sc.at[i], do_ref[...], first)

    @pl.when(flag_ref[i * nk + j] > 0)
    def _():
        bias = key_bias(sk_ref, rk_ref, sq_ref, rq_ref)
        kt = k_ref[...].T
        heads = range(HEADS)
        scores = [mm(k_ref[:, pair_lanes(h)], qm_sc[i, h], NT) + bias for h in heads]
        dps = [mm(v_ref[:, pair_lanes(h)], dom_sc[i, h], NT) for h in heads]
        probs = [jnp.exp(scores[h] - lse_ref[0, h : h + 1, :]) for h in heads]
        ds = [(probs[h] * (dps[h] - delta_ref[0, h : h + 1, :])).astype(bf16) for h in heads]
        low = [p.astype(bf16) for p in probs]
        for h in range(0, HEADS, 2):
            at = pair_lanes(h)
            dv_sc[:, at] += mm(low[h], dom_sc[i, h]) + mm(low[h + 1], dom_sc[i, h + 1])
            dk_sc[:, at] += mm(ds[h], qm_sc[i, h]) + mm(ds[h + 1], qm_sc[i, h + 1])
        for h in heads:
            at = head_rows(h)
            dq_sc[i, at, :] += mm(kt[at], ds[h])

    @pl.when(i == nq - 1)
    def _():
        dk_ref[...] = turn(dk_sc[...], cosk_ref[...], -sink_ref[...]).astype(bf16)
        dv_ref[...] = dv_sc[...].astype(bf16)

    @pl.when(j == nk - 1)
    def _():
        back = turn(dq_sc[i].T, cosq_ref[...], -sinq_ref[...])
        dq_ref[...] = (back * (1.0 / math.sqrt(HD))).astype(bf16)


def attend_back(flags, q, d_o, k, v, lse, delta, seg_q, rot_q, seg_k, rot_k, cosine, sine, block):
    rows, keys = q.shape[0], k.shape[0]
    nq, nk = rows // block, keys // block
    q_spec = pl.BlockSpec((block, D), lambda j, i, f: (i, 0))
    k_spec = pl.BlockSpec((block, D), lambda j, i, f: (j, 0))
    stat_spec = pl.BlockSpec((1, 16, block), lambda j, i, f: (i, 0, 0))
    row_spec = pl.BlockSpec((1, 1, block), lambda j, i, f: (i, 0, 0))
    col_spec = pl.BlockSpec((block, 1), lambda j, i, f: (j, 0))
    tabk_spec = pl.BlockSpec((block, LANES), lambda j, i, f: (j, 0))
    tabq_spec = pl.BlockSpec((block, LANES), lambda j, i, f: (i, 0))
    return pl.pallas_call(
        attend_back_kernel,
        grid_spec=pltpu.PrefetchScalarGridSpec(
            num_scalar_prefetch=1,
            grid=(nk, nq),
            in_specs=[q_spec, q_spec, k_spec, k_spec, stat_spec, stat_spec, row_spec, row_spec]
            + [col_spec] * 2
            + [tabk_spec] * 2
            + [tabq_spec] * 2,
            out_specs=[
                pl.BlockSpec((block, D), lambda j, i, f: (jnp.where(j == nk - 1, i, 0), 0)),
                k_spec,
                k_spec,
            ],
            scratch_shapes=[
                pltpu.VMEM((nq, D, block), f32),
                pltpu.VMEM((block, D), f32),
                pltpu.VMEM((block, D), f32),
                pltpu.VMEM((nq, HEADS, block, LANES), bf16),
                pltpu.VMEM((nq, HEADS, block, LANES), bf16),
            ],
        ),
        out_shape=[
            jax.ShapeDtypeStruct((rows, D), bf16),
            jax.ShapeDtypeStruct((keys, D), bf16),
            jax.ShapeDtypeStruct((keys, D), bf16),
        ],
        compiler_params=pltpu.CompilerParams(vmem_limit_bytes=VMEM),
        cost_estimate=cost(25e9, 10 * keys * D),
        name="attend_back",
    )(flags, q, d_o, k, v, lse, delta, seg_q, rot_q, seg_k, rot_k, cosine, sine, cosine, sine)


def hidden_back(ha, hb, dh):
    sg = 1.0 / (1.0 + jnp.exp(-ha))
    si = ha * sg
    he = (si * hb).astype(bf16)
    da = (dh * hb * (sg * (1.0 + ha * (1.0 - sg)))).astype(bf16)
    return he, da, (dh * si).astype(bf16)


def shared_kernel(x_ref, gy_ref, wg_ref, wu_ref, wd_ref, y_ref, gx_ref, gg_ref, gu_ref, gd_ref, xt_sc):
    f = pl.program_id(0)

    @pl.when(f == 0)
    def _():
        y_ref[...] = jnp.zeros(y_ref.shape, f32)
        gx_ref[...] = jnp.zeros(gx_ref.shape, f32)
        xt_sc[...] = x_ref[...].T

    wg, wu = wg_ref[...].reshape(D, TILE), wu_ref[...].reshape(D, TILE)
    part = wd_ref.shape[1] // WIDE
    wd = [wd_ref[:, n * part : (n + 1) * part, :].reshape(TILE, TILE) for n in range(WIDE)]
    x, gy = x_ref[...], gy_ref[...]
    cut = [slice(n * TILE, (n + 1) * TILE) for n in range(WIDE)]
    ha, hb = mm(x, wg), mm(x, wu)
    dh = sum(mm(gy[:, cut[n]], wd[n], NT) for n in range(WIDE))
    he, da, db = hidden_back(ha, hb, dh)
    for n in range(WIDE):
        y_ref[:, cut[n]] += mm(he, wd[n])
    gx_ref[...] += mm(da, wg, NT) + mm(db, wu, NT)
    xt = xt_sc[...]
    gg_ref[...] = mm(xt, da).astype(bf16).reshape(gg_ref.shape)
    gu_ref[...] = mm(xt, db).astype(bf16).reshape(gu_ref.shape)
    down = mm(he, gy, TN).astype(bf16)
    for n in range(WIDE):
        gd_ref[:, n * part : (n + 1) * part, :] = down[:, cut[n]].reshape(gd_ref.shape[0], part, TILE)


def shared_unit(x, gy, w_gu, held, w_d, down_at, down_shard):
    rows = x.shape[0]
    devices = w_d.shape[0]
    hidden = devices * down_shard
    tiles = hidden // TILE
    groups, part = held
    wide = jax.ShapeDtypeStruct((rows, D), f32)
    many = TILE // down_shard
    piece = lambda first: pl.BlockSpec((groups, part, TILE), lambda f: (0, first + f, 0))
    grads = jax.ShapeDtypeStruct((groups, tiles * part, TILE), bf16)
    return pl.pallas_call(
        shared_kernel,
        grid=(tiles,),
        in_specs=[
            const_spec((rows, D)),
            const_spec((rows, D)),
            piece(0),
            piece(tiles),
            pl.BlockSpec((many, WIDE * down_shard, TILE), lambda f: (f, down_at, 0)),
        ],
        out_specs=[
            const_spec((rows, D)),
            const_spec((rows, D)),
            piece(0),
            piece(0),
            pl.BlockSpec((many, WIDE * down_shard, TILE), lambda f: (f, 0, 0)),
        ],
        out_shape=[wide, wide, grads, grads, jax.ShapeDtypeStruct((devices, WIDE * down_shard, TILE), bf16)],
        scratch_shapes=[pltpu.VMEM((D, rows), bf16)],
        compiler_params=pltpu.CompilerParams(vmem_limit_bytes=VMEM),
        cost_estimate=cost(20e9, 14 * D * hidden),
        name="shared_unit",
    )(x, gy, w_gu, w_gu, w_d)


def expert_kernel(
    chunk, x_ref, c_ref, other_ref, mine_ref, router_ref, wg_ref, wu_ref, wd_ref,
    y_ref, gx_ref, gr_ref, he_ref, da_ref, db_ref, xt_ref, gt_ref, y_sc, gx_sc, gy_sc, gap_sc,
):
    f = pl.program_id(0)

    def apart():
        lane = lax.broadcasted_iota(i32, (x_ref.shape[0], LANES), 1)
        return mine_ref[...] - jnp.where(lane == other_ref[...], 1.0, 0.0)

    @pl.when(f == 0)
    def _():
        gap = jnp.sum(mm(x_ref[...], router_ref[...]) * apart(), axis=-1, keepdims=True)
        gap_sc[...] = gap
        gate = 1.0 / (1.0 + jnp.exp(-gap))
        gy = (c_ref[...].astype(f32) * gate).astype(bf16)
        gy_sc[...] = gy
        xt_ref[...] = x_ref[...].T
        gt_ref[...] = gy.T
        y_sc[...] = jnp.zeros(y_sc.shape, f32)
        gx_sc[...] = jnp.zeros(gx_sc.shape, f32)

    wg, wu, wd = wg_ref[0, 0], wu_ref[0, 0], wd_ref[0, 0]
    for c in range(x_ref.shape[0] // chunk):
        at = slice(c * chunk, (c + 1) * chunk)
        x, gy = x_ref[at], gy_sc[at]
        he, da, db = hidden_back(mm(x, wg), mm(x, wu), mm(gy, wd))
        he_ref[at] = he
        da_ref[at] = da
        db_ref[at] = db
        y_sc[at] += mm(he, wd, NT)
        gx_sc[at] += mm(da, wg, NT) + mm(db, wu, NT)

    @pl.when(f == pl.num_programs(0) - 1)
    def _():
        y = y_sc[...].astype(bf16)
        y_ref[...] = y
        dgate = jnp.sum(c_ref[...].astype(f32) * y.astype(f32), axis=-1, keepdims=True)
        gap = gap_sc[...]
        slope = dgate / (1.0 + jnp.exp(-gap)) / (1.0 + jnp.exp(gap))
        d_logits = slope * apart()
        high = d_logits.astype(bf16)
        rest = (d_logits - high.astype(f32)).astype(bf16)
        router = router_ref[...]
        gx_ref[...] = (gx_sc[...] + mm(high, router, NT) + mm(rest, router, NT)).astype(bf16)
        gr_ref[...] = mm(xt_ref[...], high) + mm(xt_ref[...], rest)


def expert_unit(x, c, other, mine, router, weights):
    rows = x.shape[0]
    shards, _, _, part = weights.shape
    hidden = shards * part
    per = part // TILE
    specs = [pl.BlockSpec((1, 1, D, TILE), lambda f, w=w: (f // per, w, 0, f % per)) for w in range(3)]
    tile_spec = pl.BlockSpec((rows, TILE), lambda f: (0, f))
    kept = jax.ShapeDtypeStruct((rows, hidden), bf16)
    wide = jax.ShapeDtypeStruct((rows, D), bf16)
    tall = jax.ShapeDtypeStruct((D, rows), bf16)
    row_spec = const_spec((rows, D))
    return pl.pallas_call(
        functools.partial(expert_kernel, rows // 2),
        grid=(hidden // TILE,),
        in_specs=[row_spec, row_spec, const_spec((rows, 1)), const_spec((1, LANES)), const_spec((D, LANES))] + specs,
        out_specs=[row_spec] * 2 + [const_spec((D, LANES))] + [tile_spec] * 3 + [const_spec((D, rows))] * 2,
        out_shape=[wide, wide, jax.ShapeDtypeStruct((D, LANES), f32), kept, kept, kept, tall, tall],
        scratch_shapes=[
            pltpu.VMEM((rows, D), f32),
            pltpu.VMEM((rows, D), f32),
            pltpu.VMEM((rows, D), bf16),
            pltpu.VMEM((rows, 1), f32),
        ],
        compiler_params=pltpu.CompilerParams(vmem_limit_bytes=VMEM),
        cost_estimate=cost(50e9, 6 * rows * hidden),
        name="expert_unit",
    )(x, c, other, mine, router, weights, weights, weights)


def expert_grads_kernel(xt_ref, gt_ref, he_ref, da_ref, db_ref, out_ref):
    xt = xt_ref[...]
    out_ref[0, 0] = mm(xt, da_ref[...]).astype(bf16)
    out_ref[0, 1] = mm(xt, db_ref[...]).astype(bf16)
    out_ref[0, 2] = mm(gt_ref[...], he_ref[...]).astype(bf16)


def expert_grads(xt, gt, he, da, db, shards):
    rows, hidden = he.shape
    part = hidden // shards
    per = part // TILE
    tile_spec = pl.BlockSpec((rows, TILE), lambda f: (0, f))
    return pl.pallas_call(
        expert_grads_kernel,
        grid=(hidden // TILE,),
        in_specs=[const_spec((D, rows))] * 2 + [tile_spec] * 3,
        out_specs=pl.BlockSpec((1, 3, D, TILE), lambda f: (f // per, 0, 0, f % per)),
        out_shape=jax.ShapeDtypeStruct((shards, 3, D, part), bf16),
        compiler_params=pltpu.CompilerParams(vmem_limit_bytes=VMEM),
        cost_estimate=cost(20e9, 6 * rows * hidden),
        name="expert_grads",
    )(xt, gt, he, da, db)


EVERY = ("ctx", "fsdp")


def swap_fsdp(values):
    return lax.all_to_all(values, "fsdp", split_axis=0, concat_axis=0, tiled=True)


def peer(values, axis, size, step):
    return lax.ppermute(values, axis, [(i, i ^ step) for i in range(size)])


def scatter_sum(chunks, n_ctx, n_fsdp):
    rows, width = chunks.shape[1:]
    pairs = n_fsdp // 2
    odd = lax.axis_index("fsdp") % 2
    view = chunks.reshape(n_ctx * pairs, 2, rows, width)
    keep = jnp.where(odd == 0, view[:, 0], view[:, 1])
    give = jnp.where(odd == 0, view[:, 1], view[:, 0])
    got = peer(give, "fsdp", n_fsdp, 1)
    part = (keep.astype(f32) + got.astype(f32)).astype(bf16).reshape(n_ctx, pairs, rows, width)
    part = lax.all_to_all(part, "ctx", split_axis=0, concat_axis=0, tiled=True)
    part = jnp.sum(part.astype(f32), axis=0).astype(bf16)
    groups = [[2 * i + c for i in range(pairs)] for c in range(2)]
    part = lax.all_to_all(part, "fsdp", split_axis=0, concat_axis=0, tiled=True, axis_index_groups=groups)
    return jnp.sum(part.astype(f32), axis=0)


def norm_back(values, inv, gain, grad):
    scaled = grad * gain
    mean = jnp.mean(scaled * values, axis=-1, keepdims=True)
    return inv * scaled - values * (inv * inv * inv * mean)


def inverse_rms(values):
    return lax.rsqrt(jnp.mean(values * values, axis=-1, keepdims=True) + EPS)


def positions(order, order_rows, segment_row, valid_row, block):
    blocks = order_rows
    hot = order[:, None] == jnp.arange(blocks, dtype=i32)[None, :]

    def pick(row):
        return jnp.sum(jnp.where(hot[:, :, None], row.reshape(1, blocks, block), 0), axis=1)

    segment, valid = pick(segment_row), pick(valid_row)
    position = order[:, None] * block + jnp.arange(block, dtype=i32)[None, :]
    bounds = jnp.arange(NCONT + 1, dtype=i32)
    starts = jnp.sum((segment_row[None, :] < bounds[:, None]).astype(i32), axis=1)
    begin = jnp.sum(jnp.where(segment[:, :, None] == bounds, starts, 0), axis=-1)
    rotary = position - begin + jnp.where(segment > 0, starts[1], 0)
    return segment, rotary, valid


def local(
    n_ctx, n_fsdp,
    tokens, cotangent, block_order, segment_ids, valid_mask, routes,
    attention_gain, query_weight, key_weight, value_weight, out_weight,
    feedforward_gain, router, shared_gate, shared_up, shared_down,
    expert_gate, expert_up, expert_down,
):
    devices = n_ctx * n_fsdp
    x_low, c_low = tokens[0], cotangent[0]
    rows = x_low.shape[0]
    group = segment_ids.shape[1]
    blocks = block_order.shape[1]
    block = group // blocks
    own = rows // block
    experts = n_fsdp
    cap = 2 * rows * TOPK // experts
    slots = experts * cap
    my_ctx = lax.axis_index("ctx")
    my_fsdp = lax.axis_index("fsdp")
    shard = query_weight.shape[0]
    down_shard = shared_down.shape[0]
    hidden = shared_gate.shape[1]
    tiles = hidden // TILE
    tie = lax.optimization_barrier

    def pieces(array):
        r, w = array.shape
        return array.reshape(r, w // TILE, TILE).transpose(1, 0, 2).reshape(-1, TILE)

    misc = jnp.concatenate([router.reshape(-1), attention_gain, feedforward_gain])
    misc = jnp.pad(misc, (0, 8 * TILE - misc.shape[0])).reshape(8, TILE)
    square = [pieces(w) for w in (query_weight, key_weight, value_weight, out_weight)]
    dense = lax.all_gather(jnp.concatenate(square + [misc], axis=0), EVERY, axis=0, tiled=False)

    x_all = jnp.concatenate(
        [x_low] + [peer(x_low, "ctx", n_ctx, step) for step in range(1, n_ctx)], axis=0
    )
    dev = my_ctx ^ jnp.arange(n_ctx, dtype=i32)
    which = (dev[:, None] * own + jnp.arange(own, dtype=i32)[None, :]).reshape(-1)
    order = jnp.sum(
        jnp.where(which[:, None] == jnp.arange(blocks, dtype=i32)[None, :], block_order[0][None, :], 0), axis=1
    )
    seg, rot, val = positions(order, blocks, segment_ids[0], valid_mask[0], block)
    seg_q, rot_q = seg[:own], rot[:own]
    seg_k = jnp.where(val > 0, seg, -1)
    allowed = (
        (seg_k[None, :, None, :] == 0) | (seg_k[None, :, None, :] == seg_q[:, None, :, None])
    ) & (rot[None, :, None, :] <= rot_q[:, None, :, None])
    flags = jnp.any(allowed, axis=(2, 3)).astype(i32).reshape(-1)
    half = HD // 2
    lane = jnp.arange(LANES, dtype=i32)
    frequency = jnp.exp((lane % half).astype(f32) * (-math.log(BASE) / half))
    angles = rot.reshape(-1).astype(f32)[:, None] * frequency[None, :]
    cosine = jnp.cos(angles)
    sine = jnp.sin(angles) * jnp.where(lane % HD < half, -1.0, 1.0)
    seg_rows, rot_rows = seg_q.reshape(own, 1, block), rot_q.reshape(own, 1, block)
    seg_cols, rot_cols = seg_k.reshape(-1, 1), rot.reshape(-1, 1)
    keep = val[:own].reshape(-1, 1).astype(f32)

    chosen = routes[0]
    every = jnp.arange(experts, dtype=i32)
    hot = jnp.any(chosen[:, :, None] == every, axis=1)
    before = (jnp.arange(rows)[:, None] > jnp.arange(rows)[None, :]).astype(bf16)
    rank = mm(before, hot.astype(bf16)).astype(i32)
    slot_cols = jnp.where(hot, rank, -1)
    slot_rows = slot_cols.T
    place = slot_rows[:, None, :] == jnp.arange(cap, dtype=i32)[None, :, None]
    other = jnp.sum(chosen, axis=-1)[None, :] - every[:, None]
    other = jnp.sum(jnp.where(place, other[:, None, :], 0), axis=-1)
    other = swap_fsdp(other).reshape(slots, 1)
    c_send = mm(place.astype(bf16).reshape(slots, rows), c_low).astype(bf16).reshape(experts, cap, D)

    c_slots = swap_fsdp(c_send).reshape(slots, D)
    early = (dense, x_all, flags, cosine, sine, seg_rows, rot_rows, seg_cols, rot_cols, slot_cols, slot_rows, other, c_slots, keep)
    (dense, x_all, flags, cosine, sine, seg_rows, rot_rows, seg_cols, rot_cols, slot_cols, slot_rows, other, c_slots, keep) = tie(early)

    mine = jnp.stack([expert_gate[0], expert_up[0], expert_down[0].T])
    mine, dense = tie((mine, dense))
    expert_w = lax.all_gather(mine, "ctx", axis=0, tiled=False)

    at = 4 * WIDE * shard
    extra = dense[:, at : at + 8].reshape(devices, 8 * TILE)
    full_router = extra[:, : shard * experts].reshape(D, experts)
    full_router = jnp.pad(full_router, ((0, 0), (0, LANES - experts)))
    gain_one = extra[:, shard * experts : shard * (experts + 1)].reshape(1, D).astype(f32)
    gain_two = extra[:, shard * (experts + 1) : shard * (experts + 2)].reshape(1, D).astype(f32)
    cut = 2 * tiles * shard
    if shard % 8 == 0:
        held = (devices, shard)
    else:
        held = (1, D)
        dense = dense[:, :at].reshape(devices, 4 * WIDE, shard, TILE).transpose(1, 0, 2, 3).reshape(1, -1, TILE)

    n_all, q, k, v, vt = project(x_all, gain_one, dense, held, cosine, sine, block, rows, 1)
    attn, attn_low, lse = attend(flags, q, k, vt, seg_rows, rot_rows, seg_cols, rot_cols, block)
    resid, n_two, inv_two, x_send = mid(attn_low, x_low, gain_two, slot_rows, dense, held, cap)
    x_slots = swap_fsdp(x_send).reshape(slots, D)

    spack = jnp.concatenate([pieces(shared_gate), pieces(shared_up), pieces(shared_down)], axis=0)
    spack, n_two = tie((spack, n_two))
    shared_w = lax.all_gather(spack, EVERY, axis=0, tiled=False)
    if shard % 8 == 0:
        shared_gu = shared_w
    else:
        shared_gu = shared_w[:, :cut].reshape(devices, 2 * tiles, shard, TILE).transpose(1, 0, 2, 3).reshape(1, -1, TILE)

    is_mine = (lane == my_fsdp).astype(f32)[None, :]
    y_slots, gx_slots, grad_router, e_he, e_da, e_db, e_xt, e_gt = expert_unit(
        x_slots, c_slots, other, is_mine, full_router, expert_w
    )
    gx_slots, n_shared = tie((gx_slots, n_two))
    gx_back = swap_fsdp(gx_slots.reshape(experts, cap, D))
    s_out, s_dn, s_gg, s_gu, s_gd = shared_unit(
        n_shared, c_low, shared_gu, held, shared_w, cut // (WIDE * down_shard), down_shard
    )
    if held[0] == 1:
        s_gg, s_gu = (
            g.reshape(tiles, devices, shard, TILE).transpose(1, 0, 2, 3).reshape(devices, -1, TILE) for g in (s_gg, s_gu)
        )
    s_out, e_xt = tie((s_out, e_xt))
    e_grads = expert_grads(e_xt, e_gt, e_he, e_da, e_db, n_ctx)
    e_grads = lax.psum_scatter(e_grads, "ctx", scatter_dimension=0, tiled=False).astype(f32)
    s_pack = jnp.concatenate([s_gg, s_gu, s_gd], axis=1)
    s_grads = scatter_sum(s_pack, n_ctx, n_fsdp)

    d_resid, d_attn, d_mix, delta, grad_gain_two = mid_back(
        gx_back, slot_cols, s_dn, resid, inv_two, gain_two, c_low, attn, dense, held, block
    )
    dq, dk, dv = attend_back(
        flags, q, d_mix, k, v, lse, delta, seg_rows, rot_rows, seg_cols, rot_cols, cosine, sine, block
    )
    odd = (my_fsdp % 2).reshape(1)
    d_low, d_own, grad_gain_one, grads = tail(
        odd, n_all, dk, dv, x_all, dq, attn_low, d_attn, gain_one, dense, held, shard
    )
    if held[0] == 1:
        grads = grads.reshape(4, devices, shard, D).transpose(1, 0, 2, 3).reshape(devices, 4 * shard, D)
    dense_grads = scatter_sum(grads, n_ctx, n_fsdp)
    g_query, g_key, g_value, g_out = (dense_grads[n * shard : (n + 1) * shard] for n in range(4))
    got = [peer(d_low[n * rows : (n + 1) * rows], "ctx", n_ctx, n) for n in range(1, n_ctx)]
    d_first = d_own + sum(g.astype(f32) for g in got)
    x_in = x_low.astype(f32)
    input_grad = (d_resid + norm_back(x_in, inverse_rms(x_in), gain_one, d_first))[None]

    y_back = swap_fsdp(y_slots.reshape(experts, cap, D))
    late = slot_cols + (dk[0, 0].astype(f32) * 0.0).astype(i32)
    output, sums = finish(y_back, late, chosen, n_two, full_router, s_out, resid, x_low, keep)
    sums = sums[:, 0]

    def from_pieces(array, part):
        return array.reshape(-1, part, TILE).transpose(1, 0, 2).reshape(part, -1)

    grad_shared_gate = from_pieces(s_grads[: tiles * shard], shard)
    grad_shared_up = from_pieces(s_grads[tiles * shard : cut], shard)
    grad_shared_down = from_pieces(s_grads[cut:], down_shard)

    to_group = jnp.where(
        (jnp.arange(devices, dtype=i32) % n_fsdp == my_fsdp)[:, None], sums[None, :], 0.0
    )
    small = jnp.concatenate(
        [
            grad_router[:, :experts].reshape(devices, shard * experts),
            grad_gain_one.reshape(devices, shard),
            grad_gain_two.reshape(devices, shard),
            to_group,
        ],
        axis=1,
    )
    width = small.shape[1]
    small = jnp.pad(small, ((0, 0), (0, -width % LANES)))
    small = jnp.sum(lax.all_to_all(small, EVERY, split_axis=0, concat_axis=0, tiled=True), axis=0)
    g_router = small[: shard * experts].reshape(shard, experts)
    g_gain_one = small[shard * experts : shard * (experts + 1)]
    g_gain_two = small[shard * (experts + 1) : shard * (experts + 2)]
    group_sums = small[shard * (experts + 2) : width]
    valid_count = jnp.sum(valid_mask[0]).astype(f32)
    stats = jnp.sqrt(group_sums / (valid_count * D))[None]

    return (
        output[None], input_grad, g_gain_one, g_query, g_key, g_value, g_out, g_gain_two, g_router,
        grad_shared_gate, grad_shared_up, grad_shared_down,
        e_grads[0][None], e_grads[1][None], e_grads[2].T[None], stats,
    )


def solution(mesh):
    sizes = dict(mesh.shape)
    rows3 = P("fsdp", "ctx", None)
    group = P("fsdp", None)
    dense1 = P(("ctx", "fsdp"))
    dense2 = P(("ctx", "fsdp"), None)
    column = P("fsdp", None, "ctx")
    return jax.shard_map(
        functools.partial(local, sizes["ctx"], sizes["fsdp"]),
        mesh=mesh,
        in_specs=(rows3, rows3, group, group, group, rows3)
        + (dense1, dense2, dense2, dense2, dense2, dense1)
        + (dense2,) * 4
        + (column, column, rows3),
        out_specs=(rows3, rows3)
        + (dense1, dense2, dense2, dense2, dense2, dense1)
        + (dense2,) * 4
        + (column, column, rows3, group),
        check_vma=False,
    )
```

```python
import functools
import math

import jax
import jax.numpy as jnp
from jax import lax
from jax.experimental import pallas as pl
from jax.experimental.pallas import tpu as pltpu
from jax.sharding import PartitionSpec as P

D = 768
HEADS = 12
HD = 64
TOPK = 2
NCONT = 4

HIGH = lax.Precision.HIGHEST
EPS = 1e-06
NEG = -1e30
FLOOR = -5e29
BASE = 10000.0
LANES = 128
TILE = 256
GRPS = D // LANES
VMEM = 60 * 1024 * 1024

f32 = jnp.float32
bf16 = jnp.bfloat16
i32 = jnp.int32

NT = (((1,), (1,)), ((), ()))
NN = (((1,), (0,)), ((), ()))
TN = (((0,), (0,)), ((), ()))


def mm(a, b, dims=NN):
    return lax.dot_general(a, b, dims, preferred_element_type=f32)


def low_lanes(rows):
    lane = lax.broadcasted_iota(i32, (rows, LANES), 1)
    return lane % HD < HD // 2


def first_head(rows):
    return lax.broadcasted_iota(i32, (rows, LANES), 1) < HD


def turn(values, cosine, sine):
    low = low_lanes(values.shape[0])
    parts = []
    for g in range(GRPS):
        part = values[:, g * LANES : (g + 1) * LANES]
        other = jnp.where(
            low, pltpu.roll(part, LANES - HD // 2, 1), pltpu.roll(part, HD // 2, 1)
        )
        parts.append(part * cosine + other * sine)
    return jnp.concatenate(parts, axis=1)


def const_spec(shape):
    zeros = (0,) * len(shape)
    return pl.BlockSpec(shape, lambda *_: zeros)


BRIEF = pl.CostEstimate(flops=10**9, transcendentals=0, bytes_accessed=10**6)
WIDE = D // TILE
LAST = 4 * WIDE


def times(rows, pieces, out_dtype=f32):
    parts = [mm(rows, p[...].reshape(D, TILE)) for p in pieces]
    return jnp.concatenate(parts, axis=1).astype(out_dtype)


def times_back(rows, pieces):
    parts = [mm(rows[:, n * TILE : (n + 1) * TILE], p[...].reshape(D, TILE), NT) for n, p in enumerate(pieces)]
    return parts[0] + parts[1] + parts[2]


def piece_specs(held, first, count):
    groups, part, base = held
    first = first + base
    return [pl.BlockSpec((groups, part, TILE), lambda *_, p=p: (0, p, 0)) for p in range(first, first + count)]


def pack_kernel(with_last, *refs):
    out_ref = refs[-1]
    at = 0
    for ref in refs[:-3] if with_last else refs[:-1]:
        rows = ref.shape[0]
        for n in range(ref.shape[1] // TILE):
            out_ref[at : at + rows, :] = ref[:, n * TILE : (n + 1) * TILE]
            at += rows
    if with_last:
        router_ref, gains_ref = refs[-3:-1]
        rows, experts = router_ref.shape
        rest = jnp.zeros((rows, TILE - experts - 2), f32)
        last = [router_ref[...].astype(f32), gains_ref[...].astype(f32), rest]
        out_ref[at : at + rows, :] = jnp.concatenate(last, axis=1).astype(bf16)


def pack_weights(weights, last):
    operands = (*weights, *last)
    if weights[-1].shape[0] % 8:
        flat = [a.reshape(a.shape[0], -1, TILE).transpose(1, 0, 2).reshape(-1, TILE) for a in weights]
        if last:
            both = jnp.concatenate(last, axis=1)
            flat.append(jnp.pad(both, ((0, 0), (0, TILE - both.shape[1]))))
        return jnp.concatenate(flat, axis=0)
    rows = sum(a.shape[0] * (a.shape[1] // TILE) for a in weights) + (last[0].shape[0] if last else 0)
    return pl.pallas_call(
        functools.partial(pack_kernel, bool(last)),
        out_shape=jax.ShapeDtypeStruct((rows, TILE), bf16),
        compiler_params=pltpu.CompilerParams(vmem_limit_bytes=VMEM),
        cost_estimate=BRIEF,
        name="pack",
    )(*operands)


def in_pieces(dense, first, count, shard):
    if shard % 8 == 0:
        return dense, (dense.shape[0], shard, first // shard)
    square = dense[:, first : first + count * shard].reshape(dense.shape[0], count, shard, TILE)
    return square.transpose(1, 0, 2, 3).reshape(1, -1, TILE), (1, D, 0)


def qkv_kernel(own, experts, x_ref, last_ref, *refs):
    wq, wk, wv = refs[:WIDE], refs[WIDE : 2 * WIDE], refs[2 * WIDE : 3 * WIDE]
    cos_ref, sin_ref, n_ref, q_ref, k_ref, v_ref, vt_ref, gain_ref = refs[3 * WIDE :]

    @pl.when(pl.program_id(0) == 0)
    def _():
        last = last_ref[...].reshape(D, TILE)[:, :LANES].astype(f32).T
        gain_ref[...] = last[experts : experts + 2]

    x = x_ref[...].astype(f32)
    inv = lax.rsqrt(jnp.mean(x * x, axis=-1, keepdims=True) + EPS)
    n = (x * inv * gain_ref[0:1, :]).astype(bf16)
    n_ref[...] = n
    cosine = cos_ref[...]
    sine = sin_ref[...]
    k_ref[...] = turn(times(n, wk), cosine, sine).astype(bf16)
    v = times(n, wv, bf16)
    v_ref[...] = v
    block = vt_ref.shape[2]
    for b in range(vt_ref.shape[0]):
        vt_ref[b] = v[b * block : (b + 1) * block].T

    @pl.when(pl.program_id(0) < own)
    def _():
        q = turn(times(n, wq), cosine, sine)
        q_ref[...] = (q * (1.0 / math.sqrt(HD))).astype(bf16)


def project(x_all, experts, dense, held, cosine, sine, block, step, own):
    rows = x_all.shape[0]
    row_spec = pl.BlockSpec((step, D), lambda i: (i, 0))
    tab_spec = pl.BlockSpec((step, LANES), lambda i: (i, 0))
    wide = jax.ShapeDtypeStruct((rows, D), bf16)
    return pl.pallas_call(
        functools.partial(qkv_kernel, own, experts),
        grid=(rows // step,),
        in_specs=[row_spec] + piece_specs(held, LAST, 1) + piece_specs(held, 0, 3 * WIDE) + [tab_spec] * 2,
        out_specs=[
            row_spec,
            pl.BlockSpec((step, D), lambda i: (jnp.minimum(i, own - 1), 0)),
            row_spec,
            row_spec,
            pl.BlockSpec((step // block, D, block), lambda i: (i, 0, 0)),
            const_spec((2, D)),
        ],
        out_shape=[
            wide,
            jax.ShapeDtypeStruct((own * step, D), bf16),
            wide,
            wide,
            jax.ShapeDtypeStruct((rows // block, D, block), bf16),
            jax.ShapeDtypeStruct((2, D), f32),
        ],
        compiler_params=pltpu.CompilerParams(vmem_limit_bytes=VMEM),
        cost_estimate=BRIEF,
        name="qkv",
    )(x_all, *[dense] * (3 * WIDE + 1), cosine, sine)


def mid_kernel(cap, o_ref, x_ref, gain_ref, slot_ref, *refs):
    wo = refs[:WIDE]
    resid_ref, n_ref, inv_ref, send_ref = refs[WIDE:]
    resid = x_ref[...].astype(f32) + times(o_ref[...], wo)
    inv = lax.rsqrt(jnp.mean(resid * resid, axis=-1, keepdims=True) + EPS)
    n = (resid * inv * gain_ref[1:2, :]).astype(bf16)
    resid_ref[...] = resid
    n_ref[...] = n
    inv_ref[...] = inv
    place = lax.broadcasted_iota(i32, (cap, n.shape[0]), 0)
    for e in range(slot_ref.shape[0]):
        hot = (slot_ref[e : e + 1, :] == place).astype(f32).astype(bf16)
        send_ref[e] = mm(hot, n).astype(bf16)


def mid(attn_low, x_low, gain, slot_rows, dense, held, cap):
    rows = x_low.shape[0]
    experts = slot_rows.shape[0]
    return pl.pallas_call(
        functools.partial(mid_kernel, cap),
        grid=(1,),
        in_specs=[const_spec((rows, D)), const_spec((rows, D)), const_spec((2, D)), const_spec((experts, rows))]
        + piece_specs(held, 3 * WIDE, WIDE),
        out_specs=[const_spec((rows, D))] * 2 + [const_spec((rows, 1)), const_spec((experts, cap, D))],
        out_shape=[
            jax.ShapeDtypeStruct((rows, D), f32),
            jax.ShapeDtypeStruct((rows, D), bf16),
            jax.ShapeDtypeStruct((rows, 1), f32),
            jax.ShapeDtypeStruct((experts, cap, D), bf16),
        ],
        compiler_params=pltpu.CompilerParams(vmem_limit_bytes=VMEM),
        cost_estimate=BRIEF,
        name="mid",
    )(attn_low, x_low, gain, slot_rows, *[dense] * WIDE)


def mid_back_kernel(
    cap, block, gx_ref, slot_ref, sdn_ref, resid_ref, inv_ref, gain_ref, c_ref, attn_ref, *refs
):
    wo = refs[:WIDE]
    dres_ref, dattn_ref, dmix_ref, delta_ref, ggain_ref = refs[WIDE:]
    resid, inv, gain = resid_ref[...], inv_ref[...], gain_ref[1:2, :]
    rows = resid.shape[0]
    place = lax.broadcasted_iota(i32, (rows, cap), 1)
    grad = sdn_ref[...]
    for e in range(gx_ref.shape[0]):
        hot = (slot_ref[:, e : e + 1] == place).astype(f32).astype(bf16)
        grad += mm(hot, gx_ref[e])
    ggain_ref[...] = jnp.sum(grad * resid * inv, axis=0, keepdims=True)
    dres = c_ref[...].astype(f32) + norm_back(resid, inv, gain, grad)
    dres_ref[...] = dres
    dattn = dres.astype(bf16)
    dattn_ref[...] = dattn
    dmix = times_back(dattn, wo)
    dmix = dmix.astype(bf16)
    dmix_ref[...] = dmix
    prod = dmix.astype(f32) * attn_ref[...]
    high = prod.astype(bf16)
    rest = (prod - high.astype(f32)).astype(bf16)
    lane = lax.broadcasted_iota(i32, (16, D), 1)
    head = lax.broadcasted_iota(i32, (16, D), 0)
    pick = (lane // HD == head).astype(f32).astype(bf16)
    for b in range(delta_ref.shape[0]):
        at = slice(b * block, (b + 1) * block)
        delta_ref[b] = mm(pick, high[at], NT) + mm(pick, rest[at], NT)


def mid_back(gx_back, slot_cols, s_dn, resid, inv, gain, c_low, attn, dense, held, block):
    rows = resid.shape[0]
    experts, cap, _ = gx_back.shape
    row = const_spec((rows, D))
    return pl.pallas_call(
        functools.partial(mid_back_kernel, cap, block),
        grid=(1,),
        in_specs=[
            const_spec((experts, cap, D)), const_spec((rows, experts)), row, row, const_spec((rows, 1)),
            const_spec((2, D)), row, row,
        ]
        + piece_specs(held, 3 * WIDE, WIDE),
        out_specs=[row, row, row, const_spec((rows // block, 16, block)), const_spec((1, D))],
        out_shape=[
            jax.ShapeDtypeStruct((rows, D), f32),
            jax.ShapeDtypeStruct((rows, D), bf16),
            jax.ShapeDtypeStruct((rows, D), bf16),
            jax.ShapeDtypeStruct((rows // block, 16, block), f32),
            jax.ShapeDtypeStruct((1, D), f32),
        ],
        compiler_params=pltpu.CompilerParams(vmem_limit_bytes=VMEM),
        cost_estimate=BRIEF,
        name="mid_back",
    )(gx_back, slot_cols, s_dn, resid, inv, gain, c_low, attn, *[dense] * WIDE)


def out_kernel(cap, y_ref, slot_ref, chosen_ref, n_ref, last_ref, sout_ref, resid_ref, x_ref, keep_ref, out_ref, sums_ref):
    rows = n_ref.shape[0]
    logits = mm(n_ref[...], last_ref[...].reshape(D, TILE)[:, :LANES])
    lane = lax.broadcasted_iota(i32, logits.shape, 1)
    first, second = chosen_ref[:, 0:1], chosen_ref[:, 1:2]
    gap = jnp.sum(jnp.where(lane == first, logits, 0.0), axis=-1, keepdims=True) - jnp.sum(
        jnp.where(lane == second, logits, 0.0), axis=-1, keepdims=True
    )
    gate_one = 1.0 / (1.0 + jnp.exp(-gap))
    gate_two = 1.0 / (1.0 + jnp.exp(gap))
    place = lax.broadcasted_iota(i32, (rows, cap), 1)
    ffn = sout_ref[...]
    for e in range(y_ref.shape[0]):
        hot = (slot_ref[:, e : e + 1] == place).astype(f32).astype(bf16)
        gate = jnp.where(first == e, gate_one, jnp.where(second == e, gate_two, 0.0))
        ffn += gate * mm(hot, y_ref[e])
    resid, x, keep = resid_ref[...], x_ref[...].astype(f32), keep_ref[...]
    result = resid + ffn
    out_ref[...] = result.astype(bf16)
    for n, a in enumerate((x, resid - x, ffn, result)):
        total = jnp.sum(keep * jnp.sum(a * a, axis=-1, keepdims=True), axis=0, keepdims=True)
        sums_ref[n : n + 1, :] = jnp.broadcast_to(total, (1, LANES))


def finish(y_back, slot_cols, chosen, n_two, dense, held, s_out, resid, x_low, keep):
    rows = resid.shape[0]
    experts, cap, _ = y_back.shape
    row = const_spec((rows, D))
    return pl.pallas_call(
        functools.partial(out_kernel, cap),
        grid=(1,),
        in_specs=[
            const_spec((experts, cap, D)), const_spec((rows, experts)), const_spec((rows, TOPK)), row,
        ]
        + piece_specs(held, LAST, 1)
        + [row, row, row, const_spec((rows, 1))],
        out_specs=[row, const_spec((4, LANES))],
        out_shape=[jax.ShapeDtypeStruct((rows, D), bf16), jax.ShapeDtypeStruct((4, LANES), f32)],
        compiler_params=pltpu.CompilerParams(vmem_limit_bytes=VMEM),
        cost_estimate=BRIEF,
        name="finish",
    )(y_back, slot_cols, chosen, n_two, dense, s_out, resid, x_low, keep)


def tail_kernel(
    shard, n_ctx, experts, place_ref, n_ref, dk_ref, dv_ref, x_ref, dq_ref, o_ref, da_ref, router_ref, second_ref, *refs
):
    wq, wk, wv = refs[:WIDE], refs[WIDE : 2 * WIDE], refs[2 * WIDE : 3 * WIDE]
    low_ref, own_ref, *outs, acc, ggain_ref, last_sc = refs[3 * WIDE :]
    c = pl.program_id(0)
    dk, dv = dk_ref[...], dv_ref[...]
    dn = times_back(dk, wk) + times_back(dv, wv)
    nt = n_ref[...].T
    x = x_ref[...].astype(f32)
    scaled = x * lax.rsqrt(jnp.mean(x * x, axis=-1, keepdims=True) + EPS)
    low_ref[...] = dn.astype(bf16)

    @pl.when(c == 0)
    def _():
        own = times_back(dq_ref[...], wq)
        own_ref[...] = own
        ggain_ref[...] = jnp.sum((own + dn) * scaled, axis=0, keepdims=True)
        acc[0] = mm(nt, dq_ref[...])
        acc[1] = mm(nt, dk)
        acc[2] = mm(nt, dv)
        acc[3] = mm(o_ref[...], da_ref[...], TN)

    @pl.when(c > 0)
    def _():
        ggain_ref[...] += jnp.sum(dn * scaled, axis=0, keepdims=True)
        acc[1] += mm(nt, dk)
        acc[2] += mm(nt, dv)

    @pl.when(c == pl.num_programs(0) - 1)
    def _():
        lane = lax.broadcasted_iota(i32, (D, LANES), 1)
        columns = [jnp.broadcast_to(g[...], (8, D)).T[:, :1] for g in (ggain_ref, second_ref)]
        last = jnp.where(lane == experts, columns[0], router_ref[...])
        last = jnp.where(lane == experts + 1, columns[1], last)
        last_sc[...] = jnp.concatenate([last, jnp.zeros((D, TILE - LANES), f32)], axis=1)
        if shard == D:
            for n in range(4):
                outs[0][0, n * D : (n + 1) * D, :] = acc[n].astype(bf16)
            outs[1][...] = last_sc[...].astype(bf16)
            return
        me, odd = place_ref[0], place_ref[1] > 0
        span = D // n_ctx
        keep_ref, give_ref = outs
        for step in range(n_ctx):
            start = pl.multiple_of((me ^ step) * span, span)
            for n in range(4):
                view = acc[n, pl.ds(start, span), :].reshape(span // shard // 2, 2, shard, D)
                mine = jnp.where(odd, view[:, 1], view[:, 0]).astype(bf16)
                other = jnp.where(odd, view[:, 0], view[:, 1]).astype(bf16)
                for p in range(WIDE):
                    at = slice((n * WIDE + p) * shard, (n * WIDE + p + 1) * shard)
                    cols = slice(p * TILE, (p + 1) * TILE)
                    keep_ref[step, :, at, :] = mine[:, :, cols]
                    give_ref[step, :, at, :] = other[:, :, cols]
            view = last_sc[pl.ds(start, span), :].reshape(span // shard // 2, 2, shard, TILE)
            at = slice(LAST * shard, (LAST + 1) * shard)
            keep_ref[step, :, at, :] = jnp.where(odd, view[:, 1], view[:, 0]).astype(bf16)
            give_ref[step, :, at, :] = jnp.where(odd, view[:, 0], view[:, 1]).astype(bf16)


def tail(place, n_all, dk, dv, x_all, dq, attn_low, d_attn, g_router, g_second, dense, held, n_ctx, experts):
    keys, rows = n_all.shape[0], dq.shape[0]
    groups, shard, _ = held
    step = pl.BlockSpec((rows, D), lambda c, o: (c, 0))
    row = const_spec((rows, D))
    parts = [(n_ctx, groups // 2 // n_ctx, (LAST + 1) * shard, TILE)] * 2
    if groups == 1:
        parts = [(1, 4 * D, D), (D, TILE)]
    return pl.pallas_call(
        functools.partial(tail_kernel, shard, n_ctx, experts),
        grid_spec=pltpu.PrefetchScalarGridSpec(
            num_scalar_prefetch=1,
            grid=(keys // rows,),
            in_specs=[step] * 4
            + [row] * 3
            + [const_spec((D, LANES)), const_spec((1, D))]
            + piece_specs(held, 0, 3 * WIDE),
            out_specs=[pl.BlockSpec((rows, D), lambda c, o: (c ^ o[0], 0)), row]
            + [const_spec(p) for p in parts],
            scratch_shapes=[pltpu.VMEM((4, D, D), f32), pltpu.VMEM((1, D), f32), pltpu.VMEM((D, TILE), f32)],
        ),
        out_shape=[
            jax.ShapeDtypeStruct((keys, D), bf16),
            jax.ShapeDtypeStruct((rows, D), f32),
        ]
        + [jax.ShapeDtypeStruct(p, bf16) for p in parts],
        compiler_params=pltpu.CompilerParams(vmem_limit_bytes=VMEM),
        cost_estimate=BRIEF,
        name="tail",
    )(place, n_all, dk, dv, x_all, dq, attn_low, d_attn, g_router, g_second, *[dense] * (3 * WIDE))


def split_heads(dst, values, first):
    none = jnp.zeros((), bf16)
    for g in range(GRPS):
        part = values[:, g * LANES : (g + 1) * LANES]
        dst[2 * g] = jnp.where(first, part, none)
        dst[2 * g + 1] = jnp.where(first, none, part)


def pair_lanes(h):
    return slice(h // 2 * LANES, (h // 2 + 1) * LANES)


def head_rows(h):
    return slice(h * HD, (h + 1) * HD)


def key_bias(sk_ref, rk_ref, sq_ref, rq_ref):
    sk = sk_ref[...]
    ok = ((sk == 0) | (sk == sq_ref[0])) & (rk_ref[...] <= rq_ref[0])
    return jnp.where(ok, 0.0, NEG)


def attend_kernel(
    flag_ref, q_ref, k_ref, vt_ref, sq_ref, rq_ref, sk_ref, rk_ref,
    o_ref, low_ref, lse_ref, qm_sc, m_sc, l_sc, acc_sc,
):
    i, j = pl.program_id(0), pl.program_id(1)
    count = pl.num_programs(1)

    @pl.when(j == 0)
    def _():
        m_sc[...] = jnp.full(m_sc.shape, FLOOR, f32)
        l_sc[...] = jnp.zeros(l_sc.shape, f32)
        acc_sc[...] = jnp.zeros(acc_sc.shape, f32)
        split_heads(qm_sc, q_ref[...], first_head(q_ref.shape[0]))

    @pl.when(flag_ref[i * count + j] > 0)
    def _():
        bias = key_bias(sk_ref, rk_ref, sq_ref, rq_ref)
        scores = [mm(k_ref[:, pair_lanes(h)], qm_sc[h], NT) + bias for h in range(HEADS)]
        m_old = m_sc[:HEADS]
        tops = [jnp.max(s, axis=0, keepdims=True) for s in scores]
        m_new = jnp.maximum(m_old, jnp.concatenate(tops, axis=0))
        a = jnp.exp(m_old - m_new)
        m_sc[:HEADS] = m_new
        probs = [jnp.exp(s - m_new[h : h + 1]) for h, s in enumerate(scores)]
        sums = [jnp.sum(p, axis=0, keepdims=True) for p in probs]
        l_sc[:HEADS] = l_sc[:HEADS] * a + jnp.concatenate(sums, axis=0)
        for h, p in enumerate(probs):
            at = head_rows(h)
            acc_sc[at] = acc_sc[at] * a[h : h + 1] + mm(vt_ref[0, at], p.astype(bf16))

    @pl.when(j == count - 1)
    def _():
        total = jnp.maximum(l_sc[...], 1e-30)
        lse_ref[0] = m_sc[...] + jnp.log(total)
        inv = 1.0 / total
        for h in range(HEADS):
            at = head_rows(h)
            acc_sc[at] = acc_sc[at] * inv[h : h + 1]
        o = acc_sc[...].T
        o_ref[...] = o
        low_ref[...] = o.astype(bf16)


def attend(flags, q, k, vt, seg_q, rot_q, seg_k, rot_k, block):
    rows, keys = q.shape[0], k.shape[0]
    nq, nk = rows // block, keys // block
    q_spec = pl.BlockSpec((block, D), lambda i, j, f: (i, 0))
    k_spec = pl.BlockSpec((block, D), lambda i, j, f: (j, 0))
    vt_spec = pl.BlockSpec((1, D, block), lambda i, j, f: (j, 0, 0))
    row_spec = pl.BlockSpec((1, 1, block), lambda i, j, f: (i, 0, 0))
    col_spec = pl.BlockSpec((block, 1), lambda i, j, f: (j, 0))
    return pl.pallas_call(
        attend_kernel,
        grid_spec=pltpu.PrefetchScalarGridSpec(
            num_scalar_prefetch=1,
            grid=(nq, nk),
            in_specs=[q_spec, k_spec, vt_spec, row_spec, row_spec, col_spec, col_spec],
            out_specs=[q_spec, q_spec, pl.BlockSpec((1, 16, block), lambda i, j, f: (i, 0, 0))],
            scratch_shapes=[
                pltpu.VMEM((HEADS, block, LANES), bf16),
                pltpu.VMEM((16, block), f32),
                pltpu.VMEM((16, block), f32),
                pltpu.VMEM((D, block), f32),
            ],
        ),
        out_shape=[
            jax.ShapeDtypeStruct((rows, D), f32),
            jax.ShapeDtypeStruct((rows, D), bf16),
            jax.ShapeDtypeStruct((nq, 16, block), f32),
        ],
        compiler_params=pltpu.CompilerParams(vmem_limit_bytes=VMEM),
        cost_estimate=BRIEF,
        name="attend",
    )(flags, q, k, vt, seg_q, rot_q, seg_k, rot_k)


def attend_back_kernel(
    flag_ref, q_ref, do_ref, k_ref, v_ref, lse_ref, delta_ref, sq_ref, rq_ref,
    sk_ref, rk_ref, cosk_ref, sink_ref, cosq_ref, sinq_ref,
    dq_ref, dk_ref, dv_ref, dq_sc, dk_sc, dv_sc, qm_sc, dom_sc,
):
    j, i = pl.program_id(0), pl.program_id(1)
    nk, nq = pl.num_programs(0), pl.num_programs(1)

    @pl.when(i == 0)
    def _():
        dk_sc[...] = jnp.zeros(dk_sc.shape, f32)
        dv_sc[...] = jnp.zeros(dv_sc.shape, f32)

    @pl.when(j == 0)
    def _():
        first = first_head(q_ref.shape[0])
        dq_sc[i] = jnp.zeros(dq_sc.shape[1:], f32)
        split_heads(qm_sc.at[i], q_ref[...], first)
        split_heads(dom_sc.at[i], do_ref[...], first)

    @pl.when(flag_ref[i * nk + j] > 0)
    def _():
        bias = key_bias(sk_ref, rk_ref, sq_ref, rq_ref)
        kt = k_ref[...].T
        heads = range(HEADS)
        scores = [mm(k_ref[:, pair_lanes(h)], qm_sc[i, h], NT) + bias for h in heads]
        dps = [mm(v_ref[:, pair_lanes(h)], dom_sc[i, h], NT) for h in heads]
        probs = [jnp.exp(scores[h] - lse_ref[0, h : h + 1, :]) for h in heads]
        ds = [(probs[h] * (dps[h] - delta_ref[0, h : h + 1, :])).astype(bf16) for h in heads]
        low = [p.astype(bf16) for p in probs]
        for h in range(0, HEADS, 2):
            at = pair_lanes(h)
            dv_sc[:, at] += mm(low[h], dom_sc[i, h]) + mm(low[h + 1], dom_sc[i, h + 1])
            dk_sc[:, at] += mm(ds[h], qm_sc[i, h]) + mm(ds[h + 1], qm_sc[i, h + 1])
        for h in heads:
            at = head_rows(h)
            dq_sc[i, at, :] += mm(kt[at], ds[h])

    @pl.when(i == nq - 1)
    def _():
        dk_ref[...] = turn(dk_sc[...], cosk_ref[...], -sink_ref[...]).astype(bf16)
        dv_ref[...] = dv_sc[...].astype(bf16)

    @pl.when(j == nk - 1)
    def _():
        back = turn(dq_sc[i].T, cosq_ref[...], -sinq_ref[...])
        dq_ref[...] = (back * (1.0 / math.sqrt(HD))).astype(bf16)


def attend_back(flags, q, d_o, k, v, lse, delta, seg_q, rot_q, seg_k, rot_k, cosine, sine, block):
    rows, keys = q.shape[0], k.shape[0]
    nq, nk = rows // block, keys // block
    q_spec = pl.BlockSpec((block, D), lambda j, i, f: (i, 0))
    k_spec = pl.BlockSpec((block, D), lambda j, i, f: (j, 0))
    stat_spec = pl.BlockSpec((1, 16, block), lambda j, i, f: (i, 0, 0))
    row_spec = pl.BlockSpec((1, 1, block), lambda j, i, f: (i, 0, 0))
    col_spec = pl.BlockSpec((block, 1), lambda j, i, f: (j, 0))
    tabk_spec = pl.BlockSpec((block, LANES), lambda j, i, f: (j, 0))
    tabq_spec = pl.BlockSpec((block, LANES), lambda j, i, f: (i, 0))
    return pl.pallas_call(
        attend_back_kernel,
        grid_spec=pltpu.PrefetchScalarGridSpec(
            num_scalar_prefetch=1,
            grid=(nk, nq),
            in_specs=[q_spec, q_spec, k_spec, k_spec, stat_spec, stat_spec, row_spec, row_spec]
            + [col_spec] * 2
            + [tabk_spec] * 2
            + [tabq_spec] * 2,
            out_specs=[
                pl.BlockSpec((block, D), lambda j, i, f: (jnp.where(j == nk - 1, i, 0), 0)),
                k_spec,
                k_spec,
            ],
            scratch_shapes=[
                pltpu.VMEM((nq, D, block), f32),
                pltpu.VMEM((block, D), f32),
                pltpu.VMEM((block, D), f32),
                pltpu.VMEM((nq, HEADS, block, LANES), bf16),
                pltpu.VMEM((nq, HEADS, block, LANES), bf16),
            ],
        ),
        out_shape=[
            jax.ShapeDtypeStruct((rows, D), bf16),
            jax.ShapeDtypeStruct((keys, D), bf16),
            jax.ShapeDtypeStruct((keys, D), bf16),
        ],
        compiler_params=pltpu.CompilerParams(vmem_limit_bytes=VMEM),
        cost_estimate=BRIEF,
        name="attend_back",
    )(flags, q, d_o, k, v, lse, delta, seg_q, rot_q, seg_k, rot_k, cosine, sine, cosine, sine)


def input_kernel(own_ref, dres_ref, x_ref, gain_ref, got_ref, out_ref):
    grad = own_ref[...]
    for n in range(got_ref.shape[0]):
        grad += got_ref[n].astype(f32)
    x = x_ref[...].astype(f32)
    inv = lax.rsqrt(jnp.mean(x * x, axis=-1, keepdims=True) + EPS)
    out_ref[...] = dres_ref[...] + norm_back(x, inv, gain_ref[0:1, :], grad)


def input_back(own, d_resid, x_low, gain, got):
    rows = x_low.shape[0]
    row = const_spec((rows, D))
    return pl.pallas_call(
        input_kernel,
        grid=(1,),
        in_specs=[row, row, row, const_spec((2, D)), const_spec(got.shape)],
        out_specs=row,
        out_shape=jax.ShapeDtypeStruct((rows, D), f32),
        compiler_params=pltpu.CompilerParams(vmem_limit_bytes=VMEM),
        cost_estimate=BRIEF,
        name="input_back",
    )(own, d_resid, x_low, gain, got)


def hidden_back(ha, hb, dh):
    sg = 1.0 / (1.0 + jnp.exp(-ha))
    si = ha * sg
    he = (si * hb).astype(bf16)
    da = (dh * hb * (sg * (1.0 + ha * (1.0 - sg)))).astype(bf16)
    return he, da, (dh * si).astype(bf16)


def shared_kernel(
    fast, odd_ref, x_ref, gy_ref, wg_ref, wu_ref, wd_ref, y_ref, gx_ref, *refs
):
    f = pl.program_id(0)
    xt_sc = refs[-1]

    @pl.when(f == 0)
    def _():
        y_ref[...] = jnp.zeros(y_ref.shape, f32)
        gx_ref[...] = jnp.zeros(gx_ref.shape, f32)
        xt_sc[...] = x_ref[...].T

    wg, wu = wg_ref[...].reshape(D, TILE), wu_ref[...].reshape(D, TILE)
    part = wd_ref.shape[1] // WIDE
    many = wd_ref.shape[0]
    wd = [wd_ref[:, n * part : (n + 1) * part, :].reshape(TILE, TILE) for n in range(WIDE)]
    x, gy = x_ref[...], gy_ref[...]
    cut = [slice(n * TILE, (n + 1) * TILE) for n in range(WIDE)]
    ha, hb = mm(x, wg), mm(x, wu)
    dh = sum(mm(gy[:, cut[n]], wd[n], NT) for n in range(WIDE))
    he, da, db = hidden_back(ha, hb, dh)
    for n in range(WIDE):
        y_ref[:, cut[n]] += mm(he, wd[n])
    gx_ref[...] += mm(da, wg, NT) + mm(db, wu, NT)
    xt = xt_sc[...]
    gate, up = mm(xt, da), mm(xt, db)
    down = mm(he, gy, TN)
    if not fast:
        gg_ref, gu_ref, gd_ref = refs[:3]
        gg_ref[0] = gate.astype(bf16)
        gu_ref[0] = up.astype(bf16)
        for n in range(WIDE):
            gd_ref[:, n * part : (n + 1) * part, :] = down[:, cut[n]].astype(bf16).reshape(many, part, TILE)
        return

    keep_ref, give_ref, up_sc, down_sc, sem = refs[:5]
    pairs, shard = up_sc.shape[2:4]
    odd = odd_ref[0] > 0
    last = pl.num_programs(0) - 1

    def copies(tile):
        out = []
        for n, dst in enumerate((keep_ref, give_ref)):
            for m in range(2):
                rows = pl.ds((m * (last + 1) + tile) * shard, shard)
                out.append(pltpu.make_async_copy(up_sc.at[n, m], dst.at[:, rows, :], sem.at[n, m]))
            where = dst.at[pl.ds(tile * (many // 2), many // 2), pl.ds(2 * (last + 1) * shard, WIDE * part), :]
            out.append(pltpu.make_async_copy(down_sc.at[n], where, sem.at[n, 2]))
        return out

    @pl.when(f > 0)
    def _():
        for copy in copies(f - 1):
            copy.wait()

    for m, grad in enumerate((gate, up)):
        view = grad.reshape(pairs, 2, shard, TILE)
        up_sc[0, m] = jnp.where(odd, view[:, 1], view[:, 0]).astype(bf16)
        up_sc[1, m] = jnp.where(odd, view[:, 0], view[:, 1]).astype(bf16)
    for n in range(WIDE):
        view = down[:, cut[n]].reshape(many // 2, 2, part, TILE)
        at = slice(n * part, (n + 1) * part)
        down_sc[0, :, at, :] = jnp.where(odd, view[:, 1], view[:, 0]).astype(bf16)
        down_sc[1, :, at, :] = jnp.where(odd, view[:, 0], view[:, 1]).astype(bf16)
    for copy in copies(f):
        copy.start()

    @pl.when(f == last)
    def _():
        for copy in copies(f):
            copy.wait()


def shared_unit(odd, x, gy, w_gu, held, w_d, down_shard):
    rows = x.shape[0]
    devices = w_d.shape[0]
    hidden = devices * down_shard
    tiles = hidden // TILE
    groups, part, base = held
    fast = groups > 1
    wide = jax.ShapeDtypeStruct((rows, D), f32)
    many = TILE // down_shard
    piece = lambda first: pl.BlockSpec((groups, part, TILE), lambda f, o: (0, first + f, 0))
    down = pl.BlockSpec((many, WIDE * down_shard, TILE), lambda f, o: (f, 0, 0))
    if fast:
        total = 2 * tiles * part + WIDE * down_shard
        grads = [jax.ShapeDtypeStruct((devices // 2, total, TILE), bf16)] * 2
        specs = [pl.BlockSpec(memory_space=pl.ANY)] * 2
        scratch = [
            pltpu.VMEM((2, 2, devices // 2, part, TILE), bf16),
            pltpu.VMEM((2, many // 2, WIDE * down_shard, TILE), bf16),
            pltpu.SemaphoreType.DMA((2, 3)),
        ]
    else:
        grads = [jax.ShapeDtypeStruct((groups, tiles * part, TILE), bf16)] * 2
        grads.append(jax.ShapeDtypeStruct((devices, WIDE * down_shard, TILE), bf16))
        specs = [piece(0), piece(0), down]
        scratch = []
    row = const_spec((rows, D))
    outs = pl.pallas_call(
        functools.partial(shared_kernel, fast),
        grid_spec=pltpu.PrefetchScalarGridSpec(
            num_scalar_prefetch=1,
            grid=(tiles,),
            in_specs=[row, row, piece(base), piece(base + tiles), down],
            out_specs=[row, row] + specs,
            scratch_shapes=scratch + [pltpu.VMEM((D, rows), bf16)],
        ),
        out_shape=[wide, wide] + grads,
        compiler_params=pltpu.CompilerParams(vmem_limit_bytes=VMEM),
        cost_estimate=BRIEF,
        name="shared_unit",
    )(odd, x, gy, w_gu, w_gu, w_d)
    if fast:
        return outs
    y, gx, g_gate, g_up, g_down = outs
    shard = D // devices
    g_gate, g_up = (
        g.reshape(tiles, devices, shard, TILE).transpose(1, 0, 2, 3).reshape(devices, -1, TILE) for g in (g_gate, g_up)
    )
    return (y, gx) + split_cores(jnp.concatenate([g_gate, g_up, g_down], axis=1))


def expert_kernel(
    chunk, x_ref, c_ref, other_ref, mine_ref, last_ref, wg_ref, wu_ref, wd_ref,
    y_ref, gx_ref, gr_ref, he_ref, da_ref, db_ref, xt_ref, gt_ref, y_sc, gx_sc, gy_sc, gap_sc,
):
    f = pl.program_id(0)

    def apart():
        sources, cap = other_ref.shape
        lane = lax.broadcasted_iota(i32, (cap, LANES), 1)
        other = other_ref[...].astype(f32).T.astype(i32)
        parts = [jnp.where(lane == other[:, e : e + 1], 1.0, 0.0) for e in range(sources)]
        return mine_ref[...] - jnp.concatenate(parts, axis=0)

    @pl.when(f == 0)
    def _():
        router = last_ref[...].reshape(D, TILE)[:, :LANES]
        gap = jnp.sum(mm(x_ref[...], router) * apart(), axis=-1, keepdims=True)
        gap_sc[...] = gap
        gate = 1.0 / (1.0 + jnp.exp(-gap))
        gy = (c_ref[...].astype(f32) * gate).astype(bf16)
        gy_sc[...] = gy
        xt_ref[...] = x_ref[...].T
        gt_ref[...] = gy.T
        y_sc[...] = jnp.zeros(y_sc.shape, f32)
        gx_sc[...] = jnp.zeros(gx_sc.shape, f32)

    wg, wu, wd = wg_ref[0, 0], wu_ref[0, 0], wd_ref[0, 0]
    for c in range(x_ref.shape[0] // chunk):
        at = slice(c * chunk, (c + 1) * chunk)
        x, gy = x_ref[at], gy_sc[at]
        he, da, db = hidden_back(mm(x, wg), mm(x, wu), mm(gy, wd))
        he_ref[at] = he
        da_ref[at] = da
        db_ref[at] = db
        y_sc[at] += mm(he, wd, NT)
        gx_sc[at] += mm(da, wg, NT) + mm(db, wu, NT)

    @pl.when(f == pl.num_programs(0) - 1)
    def _():
        y = y_sc[...].astype(bf16)
        y_ref[...] = y
        dgate = jnp.sum(c_ref[...].astype(f32) * y.astype(f32), axis=-1, keepdims=True)
        gap = gap_sc[...]
        slope = dgate / (1.0 + jnp.exp(-gap)) / (1.0 + jnp.exp(gap))
        d_logits = slope * apart()
        high = d_logits.astype(bf16)
        rest = (d_logits - high.astype(f32)).astype(bf16)
        router = last_ref[...].reshape(D, TILE)[:, :LANES]
        gx_ref[...] = (gx_sc[...] + mm(high, router, NT) + mm(rest, router, NT)).astype(bf16)
        gr_ref[...] = mm(xt_ref[...], high) + mm(xt_ref[...], rest)


def expert_unit(x, c, other, mine, dense, held, weights):
    rows = x.shape[0]
    shards, _, _, part = weights.shape
    hidden = shards * part
    per = part // TILE
    specs = [pl.BlockSpec((1, 1, D, TILE), lambda f, w=w: (f // per, w, 0, f % per)) for w in range(3)]
    tile_spec = pl.BlockSpec((rows, TILE), lambda f: (0, f))
    kept = jax.ShapeDtypeStruct((rows, hidden), bf16)
    wide = jax.ShapeDtypeStruct((rows, D), bf16)
    tall = jax.ShapeDtypeStruct((D, rows), bf16)
    row_spec = const_spec((rows, D))
    return pl.pallas_call(
        functools.partial(expert_kernel, rows // 2),
        grid=(hidden // TILE,),
        in_specs=[row_spec, row_spec, const_spec(other.shape), const_spec((1, LANES))]
        + piece_specs(held, LAST, 1)
        + specs,
        out_specs=[row_spec] * 2 + [const_spec((D, LANES))] + [tile_spec] * 3 + [const_spec((D, rows))] * 2,
        out_shape=[wide, wide, jax.ShapeDtypeStruct((D, LANES), f32), kept, kept, kept, tall, tall],
        scratch_shapes=[
            pltpu.VMEM((rows, D), f32),
            pltpu.VMEM((rows, D), f32),
            pltpu.VMEM((rows, D), bf16),
            pltpu.VMEM((rows, 1), f32),
        ],
        compiler_params=pltpu.CompilerParams(vmem_limit_bytes=VMEM),
        cost_estimate=BRIEF,
        name="expert_unit",
    )(x, c, other, mine, dense, weights, weights, weights)


def expert_grads_kernel(xt_ref, gt_ref, he_ref, da_ref, db_ref, out_ref):
    xt = xt_ref[...]
    out_ref[0, 0] = mm(xt, da_ref[...]).astype(bf16)
    out_ref[0, 1] = mm(xt, db_ref[...]).astype(bf16)
    out_ref[0, 2] = mm(gt_ref[...], he_ref[...]).astype(bf16)


def expert_grads(xt, gt, he, da, db, shards):
    rows, hidden = he.shape
    part = hidden // shards
    per = part // TILE
    tile_spec = pl.BlockSpec((rows, TILE), lambda f: (0, f))
    return pl.pallas_call(
        expert_grads_kernel,
        grid=(hidden // TILE,),
        in_specs=[const_spec((D, rows))] * 2 + [tile_spec] * 3,
        out_specs=pl.BlockSpec((1, 3, D, TILE), lambda f: (f // per, 0, 0, f % per)),
        out_shape=jax.ShapeDtypeStruct((shards, 3, D, part), bf16),
        compiler_params=pltpu.CompilerParams(vmem_limit_bytes=VMEM),
        cost_estimate=BRIEF,
        name="expert_grads",
    )(xt, gt, he, da, db)


EVERY = ("ctx", "fsdp")


def swap_fsdp(values):
    return lax.all_to_all(values, "fsdp", split_axis=0, concat_axis=0, tiled=True)


def peer(values, axis, size, step):
    return lax.ppermute(values, axis, [(i, i ^ step) for i in range(size)])


def block_of(array, index):
    return lax.dynamic_index_in_dim(array, index, 0, keepdims=False)


def by_step(array, n_ctx):
    array = array.reshape((n_ctx, array.shape[0] // n_ctx) + array.shape[1:])
    me = lax.axis_index("ctx")
    return [block_of(array, me ^ step) for step in range(n_ctx)]


def meet_core(keep, got):
    parts = [mine.astype(f32) + other.astype(f32) for mine, other in zip(keep, got)]
    return parts[:1] + [p.astype(bf16) for p in parts[1:]]


def meet_ctx(parts, n_ctx):
    return list(parts[:1]) + [peer(parts[step], "ctx", n_ctx, step) for step in range(1, n_ctx)]


def add_up(parts):
    total = sum(p.astype(f32) for p in parts)
    return total, total.astype(bf16)


def meet_far(total, low, n_fsdp):
    me = lax.axis_index("fsdp") // 2
    out = block_of(total, me)
    for step in range(1, n_fsdp // 2):
        out += peer(block_of(low, me ^ step), "fsdp", n_fsdp, 2 * step).astype(f32)
    return out


def meet_far_once(low, n_fsdp):
    groups = [[2 * i + c for i in range(n_fsdp // 2)] for c in range(2)]
    got = lax.all_to_all(low, "fsdp", split_axis=0, concat_axis=0, tiled=True, axis_index_groups=groups)
    return jnp.sum(got.astype(f32), axis=0)


def split_cores(chunks):
    odd = lax.axis_index("fsdp") % 2
    view = chunks.reshape((chunks.shape[0] // 2, 2) + chunks.shape[1:])
    return jnp.where(odd == 0, view[:, 0], view[:, 1]), jnp.where(odd == 0, view[:, 1], view[:, 0])


def norm_back(values, inv, gain, grad):
    scaled = grad * gain
    mean = jnp.mean(scaled * values, axis=-1, keepdims=True)
    return inv * scaled - values * (inv * inv * inv * mean)


def positions(order, order_rows, segment_row, valid_row, block):
    blocks = order_rows
    hot = order[:, None] == jnp.arange(blocks, dtype=i32)[None, :]

    def pick(row):
        return jnp.sum(jnp.where(hot[:, :, None], row.reshape(1, blocks, block), 0), axis=1)

    segment, valid = pick(segment_row), pick(valid_row)
    position = order[:, None] * block + jnp.arange(block, dtype=i32)[None, :]
    bounds = jnp.arange(NCONT + 1, dtype=i32)
    starts = jnp.sum((segment_row[None, :] < bounds[:, None]).astype(i32), axis=1)
    begin = jnp.sum(jnp.where(segment[:, :, None] == bounds, starts, 0), axis=-1)
    rotary = position - begin + jnp.where(segment > 0, starts[1], 0)
    return segment, rotary, valid


def local(
    n_ctx, n_fsdp,
    tokens, cotangent, block_order, segment_ids, valid_mask, routes,
    attention_gain, query_weight, key_weight, value_weight, out_weight,
    feedforward_gain, router, shared_gate, shared_up, shared_down,
    expert_gate, expert_up, expert_down,
):
    devices = n_ctx * n_fsdp
    x_low, c_low = tokens[0], cotangent[0]
    rows = x_low.shape[0]
    group = segment_ids.shape[1]
    blocks = block_order.shape[1]
    block = group // blocks
    own = rows // block
    experts = n_fsdp
    cap = 2 * rows * TOPK // experts
    slots = experts * cap
    my_ctx = lax.axis_index("ctx")
    my_fsdp = lax.axis_index("fsdp")
    shard = query_weight.shape[0]
    down_shard = shared_down.shape[0]
    hidden = shared_gate.shape[1]
    tiles = hidden // TILE
    tie = lax.optimization_barrier

    gains = jnp.stack([attention_gain, feedforward_gain], axis=1)
    squares = (query_weight, key_weight, value_weight, out_weight)
    dense = lax.all_gather(pack_weights(squares, (router, gains)), EVERY, axis=0, tiled=False)

    x_all = jnp.concatenate(
        [x_low] + [peer(x_low, "ctx", n_ctx, step) for step in range(1, n_ctx)], axis=0
    )
    dev = my_ctx ^ jnp.arange(n_ctx, dtype=i32)
    which = (dev[:, None] * own + jnp.arange(own, dtype=i32)[None, :]).reshape(-1)
    order = jnp.sum(
        jnp.where(which[:, None] == jnp.arange(blocks, dtype=i32)[None, :], block_order[0][None, :], 0), axis=1
    )
    seg, rot, val = positions(order, blocks, segment_ids[0], valid_mask[0], block)
    seg_q, rot_q = seg[:own], rot[:own]
    seg_k = jnp.where(val > 0, seg, -1)
    allowed = (
        (seg_k[None, :, None, :] == 0) | (seg_k[None, :, None, :] == seg_q[:, None, :, None])
    ) & (rot[None, :, None, :] <= rot_q[:, None, :, None])
    flags = jnp.any(allowed, axis=(2, 3)).astype(i32).reshape(-1)
    half = HD // 2
    lane = jnp.arange(LANES, dtype=i32)
    frequency = jnp.exp((lane % half).astype(f32) * (-math.log(BASE) / half))
    angles = rot.reshape(-1).astype(f32)[:, None] * frequency[None, :]
    cosine = jnp.cos(angles)
    sine = jnp.sin(angles) * jnp.where(lane % HD < half, -1.0, 1.0)
    seg_rows, rot_rows = seg_q.reshape(own, 1, block), rot_q.reshape(own, 1, block)
    seg_cols, rot_cols = seg_k.reshape(-1, 1), rot.reshape(-1, 1)
    keep = val[:own].reshape(-1, 1).astype(f32)

    chosen = routes[0]
    every = jnp.arange(experts, dtype=i32)
    hot = jnp.any(chosen[:, :, None] == every, axis=1)
    before = (jnp.arange(rows)[:, None] > jnp.arange(rows)[None, :]).astype(bf16)
    rank = mm(before, hot.astype(bf16)).astype(i32)
    slot_cols = jnp.where(hot, rank, -1)
    slot_rows = slot_cols.T
    place = slot_rows[:, None, :] == jnp.arange(cap, dtype=i32)[None, :, None]
    other = jnp.sum(chosen, axis=-1)[None, :] - every[:, None]
    other = jnp.sum(jnp.where(place, other[:, None, :], 0), axis=-1)
    other = swap_fsdp(other)
    c_send = mm(place.astype(bf16).reshape(slots, rows), c_low).astype(bf16).reshape(experts, cap, D)

    early = (dense, x_all, flags, cosine, sine, seg_rows, rot_rows, seg_cols, rot_cols, slot_cols, slot_rows, other, c_send, keep)
    (dense, x_all, flags, cosine, sine, seg_rows, rot_rows, seg_cols, rot_cols, slot_cols, slot_rows, other, c_send, keep) = tie(early)

    mine = jnp.stack([expert_gate[0], expert_up[0], expert_down[0].T])
    mine, dense = tie((mine, dense))
    expert_w = lax.all_gather(mine, "ctx", axis=0, tiled=False)
    c_slots = swap_fsdp(c_send).reshape(slots, D)

    cut = 2 * tiles * shard
    square, held = in_pieces(dense, 0, LAST + 1, shard)

    n_all, q, k, v, vt, gains = project(x_all, experts, square, held, cosine, sine, block, rows, 1)
    attn, attn_low, lse = attend(flags, q, k, vt, seg_rows, rot_rows, seg_cols, rot_cols, block)
    attn_low, c_slots = tie((attn_low, c_slots))
    resid, n_two, inv_two, x_send = mid(attn_low, x_low, gains, slot_rows, square, held, cap)
    x_slots = swap_fsdp(x_send).reshape(slots, D)

    shared_pack = pack_weights((shared_down, shared_gate, shared_up), ())
    shared_pack, n_two = tie((shared_pack, n_two))
    shared_w = lax.all_gather(shared_pack, EVERY, axis=0, tiled=False)
    shared_sq, shared_held = in_pieces(shared_w, WIDE * down_shard, 2 * tiles, shard)

    is_mine = (lane == my_fsdp).astype(f32)[None, :]
    y_slots, gx_slots, grad_router, e_he, e_da, e_db, e_xt, e_gt = expert_unit(
        x_slots, c_slots, other, is_mine, square, held, expert_w
    )
    gx_slots, n_shared = tie((gx_slots, n_two))
    gx_back = swap_fsdp(gx_slots.reshape(experts, cap, D))
    e_grads = expert_grads(e_xt, e_gt, e_he, e_da, e_db, n_ctx)

    e_grads, n_shared = tie((e_grads, n_shared))
    odd = (my_fsdp % 2).reshape(1)
    s_out, s_dn, s_keep, s_give = shared_unit(odd, n_shared, c_low, shared_sq, shared_held, shared_w, down_shard)
    s_got = [peer(g, "fsdp", n_fsdp, 1) for g in by_step(s_give, n_ctx)]
    s_parts = meet_core(by_step(s_keep, n_ctx), s_got)
    e_grads, gx_back, *s_parts = tie((e_grads, gx_back, *s_parts))
    e_sums = lax.psum_scatter(e_grads, "ctx", scatter_dimension=0, tiled=False).astype(f32)
    s_parts = meet_ctx(s_parts, n_ctx)

    d_resid, d_attn, d_mix, delta, grad_gain_two = mid_back(
        gx_back, slot_cols, s_dn, resid, inv_two, gains, c_low, attn, square, held, block
    )
    d_mix, y_slots = tie((d_mix, y_slots))
    y_back = swap_fsdp(y_slots.reshape(experts, cap, D))
    dq, dk, dv = attend_back(
        flags, q, d_mix, k, v, lse, delta, seg_rows, rot_rows, seg_cols, rot_cols, cosine, sine, block
    )
    where = jnp.stack([my_ctx, my_fsdp % 2])
    d_low, d_own, *halves = tail(
        where, n_all, dk, dv, x_all, dq, attn_low, d_attn, grad_router, grad_gain_two, square, held, n_ctx, experts
    )
    if held[0] == 1:
        g_all = halves[0].reshape(4, devices, shard, WIDE, TILE).transpose(1, 0, 3, 2, 4)
        g_all = g_all.reshape(devices, 4 * WIDE * shard, TILE)
        g_all = jnp.concatenate([g_all, halves[1].reshape(devices, shard, TILE)], axis=1)
        g_keep, g_give = (jnp.stack(by_step(h, n_ctx)) for h in split_cores(g_all))
    else:
        g_keep, g_give = halves
    g_give, *s_parts = tie((g_give, *s_parts))
    s_low = add_up(s_parts)[1]
    s_grads = meet_far_once(s_low, n_fsdp)
    g_parts = meet_core(g_keep, peer(g_give, "fsdp", n_fsdp, 1))
    y_back, *g_parts = tie((y_back, *g_parts))
    g_parts = meet_ctx(g_parts, n_ctx)

    output, sums = finish(y_back, slot_cols, chosen, n_two, square, held, s_out, resid, x_low, keep)

    group_sums = sums
    for bit in range(n_ctx.bit_length() - 1):
        group_sums = group_sums + peer(group_sums, "ctx", n_ctx, 1 << bit)
    valid_count = jnp.sum(valid_mask[0]).astype(f32)
    stats = jnp.sqrt(group_sums[:, 0] / (valid_count * D))[None]

    e_outs = (e_sums[0][None], e_sums[1][None], e_sums[2].T[None])
    d_low, e_outs, s_grads, output, stats, *g_parts = tie((d_low, e_outs, s_grads, output, stats, *g_parts))
    g_total, g_low = add_up(g_parts)
    dense_grads = meet_far(g_total, g_low, n_fsdp)

    def from_pieces(array, part):
        return array.reshape(-1, part, TILE).transpose(1, 0, 2).reshape(part, -1)

    grad_shared_gate = from_pieces(s_grads[: tiles * shard], shard)
    grad_shared_up = from_pieces(s_grads[tiles * shard : cut], shard)
    grad_shared_down = from_pieces(s_grads[cut:], down_shard)
    span = WIDE * shard
    g_query, g_key, g_value, g_out = (from_pieces(dense_grads[n * span : (n + 1) * span], shard) for n in range(4))
    got = lax.all_to_all(d_low.reshape(n_ctx, rows, D), "ctx", split_axis=0, concat_axis=0, tiled=True)
    input_grad = input_back(d_own, d_resid, x_low, gains, got)[None]

    last = dense_grads[LAST * shard :]
    g_router, g_gain_one, g_gain_two = last[:, :experts], last[:, experts], last[:, experts + 1]

    return (
        output[None], input_grad, g_gain_one, g_query, g_key, g_value, g_out, g_gain_two, g_router,
        grad_shared_gate, grad_shared_up, grad_shared_down,
        *e_outs, stats,
    )


def solution(mesh):
    sizes = dict(mesh.shape)
    rows3 = P("fsdp", "ctx", None)
    group = P("fsdp", None)
    dense1 = P(("ctx", "fsdp"))
    dense2 = P(("ctx", "fsdp"), None)
    column = P("fsdp", None, "ctx")
    return jax.shard_map(
        functools.partial(local, sizes["ctx"], sizes["fsdp"]),
        mesh=mesh,
        in_specs=(rows3, rows3, group, group, group, rows3)
        + (dense1, dense2, dense2, dense2, dense2, dense1)
        + (dense2,) * 4
        + (column, column, rows3),
        out_specs=(rows3, rows3)
        + (dense1, dense2, dense2, dense2, dense2, dense1)
        + (dense2,) * 4
        + (column, column, rows3, group),
        check_vma=False,
    )
```

```python
import functools
import math

import jax
import jax.numpy as jnp
from jax import lax
from jax.experimental import pallas as pl
from jax.experimental.pallas import tpu as pltpu
from jax.sharding import PartitionSpec as P

D = 768
HEADS = 12
HD = 64
TOPK = 2
NCONT = 4

HIGH = lax.Precision.HIGHEST
EPS = 1e-06
NEG = -1e30
FLOOR = -5e29
BASE = 10000.0
LANES = 128
TILE = 256
GRPS = D // LANES
VMEM = 60 * 1024 * 1024

f32 = jnp.float32
bf16 = jnp.bfloat16
i32 = jnp.int32

NT = (((1,), (1,)), ((), ()))
NN = (((1,), (0,)), ((), ()))
TN = (((0,), (0,)), ((), ()))


def mm(a, b, dims=NN):
    return lax.dot_general(a, b, dims, preferred_element_type=f32)


def low_lanes(rows):
    lane = lax.broadcasted_iota(i32, (rows, LANES), 1)
    return lane % HD < HD // 2


def first_head(rows):
    return lax.broadcasted_iota(i32, (rows, LANES), 1) < HD


def turn(values, cosine, sine):
    low = low_lanes(values.shape[0])
    parts = []
    for g in range(GRPS):
        part = values[:, g * LANES : (g + 1) * LANES]
        other = jnp.where(
            low, pltpu.roll(part, LANES - HD // 2, 1), pltpu.roll(part, HD // 2, 1)
        )
        parts.append(part * cosine + other * sine)
    return jnp.concatenate(parts, axis=1)


def const_spec(shape):
    zeros = (0,) * len(shape)
    return pl.BlockSpec(shape, lambda *_: zeros)


BRIEF = pl.CostEstimate(flops=10**9, transcendentals=0, bytes_accessed=10**6)
WIDE = D // TILE
LAST = 4 * WIDE


def times(rows, pieces, out_dtype=f32):
    parts = [mm(rows, p[...].reshape(D, TILE)) for p in pieces]
    return jnp.concatenate(parts, axis=1).astype(out_dtype)


def times_back(rows, pieces):
    parts = [mm(rows[:, n * TILE : (n + 1) * TILE], p[...].reshape(D, TILE), NT) for n, p in enumerate(pieces)]
    return parts[0] + parts[1] + parts[2]


def piece_specs(held, first, count):
    groups, part, base = held
    first = first + base
    return [pl.BlockSpec((groups, part, TILE), lambda *_, p=p: (0, p, 0)) for p in range(first, first + count)]


def pack_kernel(with_last, *refs):
    out_ref = refs[-1]
    at = 0
    for ref in refs[:-3] if with_last else refs[:-1]:
        rows = ref.shape[0]
        for n in range(ref.shape[1] // TILE):
            out_ref[at : at + rows, :] = ref[:, n * TILE : (n + 1) * TILE]
            at += rows
    if with_last:
        router_ref, gains_ref = refs[-3:-1]
        rows, experts = router_ref.shape
        rest = jnp.zeros((rows, TILE - experts - 2), f32)
        last = [router_ref[...].astype(f32), gains_ref[...].astype(f32), rest]
        out_ref[at : at + rows, :] = jnp.concatenate(last, axis=1).astype(bf16)


def pack_weights(weights, last):
    operands = (*weights, *last)
    if weights[-1].shape[0] % 8:
        flat = [a.reshape(a.shape[0], -1, TILE).transpose(1, 0, 2).reshape(-1, TILE) for a in weights]
        if last:
            both = jnp.concatenate(last, axis=1)
            flat.append(jnp.pad(both, ((0, 0), (0, TILE - both.shape[1]))))
        return jnp.concatenate(flat, axis=0)
    rows = sum(a.shape[0] * (a.shape[1] // TILE) for a in weights) + (last[0].shape[0] if last else 0)
    return pl.pallas_call(
        functools.partial(pack_kernel, bool(last)),
        out_shape=jax.ShapeDtypeStruct((rows, TILE), bf16),
        compiler_params=pltpu.CompilerParams(vmem_limit_bytes=VMEM),
        cost_estimate=BRIEF,
        name="pack",
    )(*operands)


def in_pieces(dense, first, count, shard):
    if shard % 8 == 0:
        return dense, (dense.shape[0], shard, first // shard)
    square = dense[:, first : first + count * shard].reshape(dense.shape[0], count, shard, TILE)
    return square.transpose(1, 0, 2, 3).reshape(1, -1, TILE), (1, D, 0)


def qkv_kernel(own, experts, x_ref, last_ref, *refs):
    wq, wk, wv = refs[:WIDE], refs[WIDE : 2 * WIDE], refs[2 * WIDE : 3 * WIDE]
    cos_ref, sin_ref, n_ref, q_ref, k_ref, v_ref, vt_ref, gain_ref = refs[3 * WIDE :]

    @pl.when(pl.program_id(0) == 0)
    def _():
        last = last_ref[...].reshape(D, TILE)[:, :LANES].astype(f32).T
        gain_ref[...] = last[experts : experts + 2]

    x = x_ref[...].astype(f32)
    inv = lax.rsqrt(jnp.mean(x * x, axis=-1, keepdims=True) + EPS)
    n = (x * inv * gain_ref[0:1, :]).astype(bf16)
    n_ref[...] = n
    cosine = cos_ref[...]
    sine = sin_ref[...]
    k_ref[...] = turn(times(n, wk), cosine, sine).astype(bf16)
    v = times(n, wv, bf16)
    v_ref[...] = v
    block = vt_ref.shape[2]
    for b in range(vt_ref.shape[0]):
        vt_ref[b] = v[b * block : (b + 1) * block].T

    @pl.when(pl.program_id(0) < own)
    def _():
        q = turn(times(n, wq), cosine, sine)
        q_ref[...] = (q * (1.0 / math.sqrt(HD))).astype(bf16)


def project(x_all, experts, dense, held, cosine, sine, block, step, own):
    rows = x_all.shape[0]
    row_spec = pl.BlockSpec((step, D), lambda i: (i, 0))
    tab_spec = pl.BlockSpec((step, LANES), lambda i: (i, 0))
    wide = jax.ShapeDtypeStruct((rows, D), bf16)
    return pl.pallas_call(
        functools.partial(qkv_kernel, own, experts),
        grid=(rows // step,),
        in_specs=[row_spec] + piece_specs(held, LAST, 1) + piece_specs(held, 0, 3 * WIDE) + [tab_spec] * 2,
        out_specs=[
            row_spec,
            pl.BlockSpec((step, D), lambda i: (jnp.minimum(i, own - 1), 0)),
            row_spec,
            row_spec,
            pl.BlockSpec((step // block, D, block), lambda i: (i, 0, 0)),
            const_spec((2, D)),
        ],
        out_shape=[
            wide,
            jax.ShapeDtypeStruct((own * step, D), bf16),
            wide,
            wide,
            jax.ShapeDtypeStruct((rows // block, D, block), bf16),
            jax.ShapeDtypeStruct((2, D), f32),
        ],
        compiler_params=pltpu.CompilerParams(vmem_limit_bytes=VMEM),
        cost_estimate=BRIEF,
        name="qkv",
    )(x_all, *[dense] * (3 * WIDE + 1), cosine, sine)


def mid_kernel(cap, o_ref, x_ref, gain_ref, slot_ref, *refs):
    wo = refs[:WIDE]
    resid_ref, n_ref, inv_ref, send_ref = refs[WIDE:]
    resid = x_ref[...].astype(f32) + times(o_ref[...], wo)
    inv = lax.rsqrt(jnp.mean(resid * resid, axis=-1, keepdims=True) + EPS)
    n = (resid * inv * gain_ref[1:2, :]).astype(bf16)
    resid_ref[...] = resid
    n_ref[...] = n
    inv_ref[...] = inv
    place = lax.broadcasted_iota(i32, (cap, n.shape[0]), 0)
    for e in range(slot_ref.shape[0]):
        hot = (slot_ref[e : e + 1, :] == place).astype(f32).astype(bf16)
        send_ref[e] = mm(hot, n).astype(bf16)


def mid(attn_low, x_low, gain, slot_rows, dense, held, cap):
    rows = x_low.shape[0]
    experts = slot_rows.shape[0]
    return pl.pallas_call(
        functools.partial(mid_kernel, cap),
        grid=(1,),
        in_specs=[const_spec((rows, D)), const_spec((rows, D)), const_spec((2, D)), const_spec((experts, rows))]
        + piece_specs(held, 3 * WIDE, WIDE),
        out_specs=[const_spec((rows, D))] * 2 + [const_spec((rows, 1)), const_spec((experts, cap, D))],
        out_shape=[
            jax.ShapeDtypeStruct((rows, D), f32),
            jax.ShapeDtypeStruct((rows, D), bf16),
            jax.ShapeDtypeStruct((rows, 1), f32),
            jax.ShapeDtypeStruct((experts, cap, D), bf16),
        ],
        compiler_params=pltpu.CompilerParams(vmem_limit_bytes=VMEM),
        cost_estimate=BRIEF,
        name="mid",
    )(attn_low, x_low, gain, slot_rows, *[dense] * WIDE)


def mid_back_kernel(
    cap, block, gx_ref, slot_ref, sdn_ref, resid_ref, inv_ref, gain_ref, c_ref, attn_ref, *refs
):
    wo = refs[:WIDE]
    dres_ref, dattn_ref, dmix_ref, delta_ref, ggain_ref = refs[WIDE:]
    resid, inv, gain = resid_ref[...], inv_ref[...], gain_ref[1:2, :]
    rows = resid.shape[0]
    place = lax.broadcasted_iota(i32, (rows, cap), 1)
    grad = sdn_ref[...]
    for e in range(gx_ref.shape[0]):
        hot = (slot_ref[:, e : e + 1] == place).astype(f32).astype(bf16)
        grad += mm(hot, gx_ref[e])
    ggain_ref[...] = jnp.sum(grad * resid * inv, axis=0, keepdims=True)
    dres = c_ref[...].astype(f32) + norm_back(resid, inv, gain, grad)
    dres_ref[...] = dres
    dattn = dres.astype(bf16)
    dattn_ref[...] = dattn
    dmix = times_back(dattn, wo)
    dmix = dmix.astype(bf16)
    dmix_ref[...] = dmix
    prod = dmix.astype(f32) * attn_ref[...]
    high = prod.astype(bf16)
    rest = (prod - high.astype(f32)).astype(bf16)
    lane = lax.broadcasted_iota(i32, (16, D), 1)
    head = lax.broadcasted_iota(i32, (16, D), 0)
    pick = (lane // HD == head).astype(f32).astype(bf16)
    for b in range(delta_ref.shape[0]):
        at = slice(b * block, (b + 1) * block)
        delta_ref[b] = mm(pick, high[at], NT) + mm(pick, rest[at], NT)


def mid_back(gx_back, slot_cols, s_dn, resid, inv, gain, c_low, attn, dense, held, block):
    rows = resid.shape[0]
    experts, cap, _ = gx_back.shape
    row = const_spec((rows, D))
    return pl.pallas_call(
        functools.partial(mid_back_kernel, cap, block),
        grid=(1,),
        in_specs=[
            const_spec((experts, cap, D)), const_spec((rows, experts)), row, row, const_spec((rows, 1)),
            const_spec((2, D)), row, row,
        ]
        + piece_specs(held, 3 * WIDE, WIDE),
        out_specs=[row, row, row, const_spec((rows // block, 16, block)), const_spec((1, D))],
        out_shape=[
            jax.ShapeDtypeStruct((rows, D), f32),
            jax.ShapeDtypeStruct((rows, D), bf16),
            jax.ShapeDtypeStruct((rows, D), bf16),
            jax.ShapeDtypeStruct((rows // block, 16, block), f32),
            jax.ShapeDtypeStruct((1, D), f32),
        ],
        compiler_params=pltpu.CompilerParams(vmem_limit_bytes=VMEM),
        cost_estimate=BRIEF,
        name="mid_back",
    )(gx_back, slot_cols, s_dn, resid, inv, gain, c_low, attn, *[dense] * WIDE)


def out_kernel(cap, y_ref, slot_ref, chosen_ref, n_ref, last_ref, sout_ref, resid_ref, x_ref, keep_ref, out_ref, sums_ref):
    rows = n_ref.shape[0]
    logits = mm(n_ref[...], last_ref[...].reshape(D, TILE)[:, :LANES])
    lane = lax.broadcasted_iota(i32, logits.shape, 1)
    first, second = chosen_ref[:, 0:1], chosen_ref[:, 1:2]
    gap = jnp.sum(jnp.where(lane == first, logits, 0.0), axis=-1, keepdims=True) - jnp.sum(
        jnp.where(lane == second, logits, 0.0), axis=-1, keepdims=True
    )
    gate_one = 1.0 / (1.0 + jnp.exp(-gap))
    gate_two = 1.0 / (1.0 + jnp.exp(gap))
    place = lax.broadcasted_iota(i32, (rows, cap), 1)
    ffn = sout_ref[...]
    for e in range(y_ref.shape[0]):
        hot = (slot_ref[:, e : e + 1] == place).astype(f32).astype(bf16)
        gate = jnp.where(first == e, gate_one, jnp.where(second == e, gate_two, 0.0))
        ffn += gate * mm(hot, y_ref[e])
    resid, x, keep = resid_ref[...], x_ref[...].astype(f32), keep_ref[...]
    result = resid + ffn
    out_ref[...] = result.astype(bf16)
    for n, a in enumerate((x, resid - x, ffn, result)):
        total = jnp.sum(keep * jnp.sum(a * a, axis=-1, keepdims=True), axis=0, keepdims=True)
        sums_ref[n : n + 1, :] = jnp.broadcast_to(total, (1, LANES))


def finish(y_back, slot_cols, chosen, n_two, dense, held, s_out, resid, x_low, keep):
    rows = resid.shape[0]
    experts, cap, _ = y_back.shape
    row = const_spec((rows, D))
    return pl.pallas_call(
        functools.partial(out_kernel, cap),
        grid=(1,),
        in_specs=[
            const_spec((experts, cap, D)), const_spec((rows, experts)), const_spec((rows, TOPK)), row,
        ]
        + piece_specs(held, LAST, 1)
        + [row, row, row, const_spec((rows, 1))],
        out_specs=[row, const_spec((4, LANES))],
        out_shape=[jax.ShapeDtypeStruct((rows, D), bf16), jax.ShapeDtypeStruct((4, LANES), f32)],
        compiler_params=pltpu.CompilerParams(vmem_limit_bytes=VMEM),
        cost_estimate=BRIEF,
        name="finish",
    )(y_back, slot_cols, chosen, n_two, dense, s_out, resid, x_low, keep)


def tail_kernel(
    shard, n_ctx, experts, place_ref, n_ref, dk_ref, dv_ref, x_ref, dq_ref, o_ref, da_ref, router_ref, second_ref, *refs
):
    wq, wk, wv = refs[:WIDE], refs[WIDE : 2 * WIDE], refs[2 * WIDE : 3 * WIDE]
    low_ref, own_ref, *outs, acc, ggain_ref, last_sc = refs[3 * WIDE :]
    c = pl.program_id(0)
    dk, dv = dk_ref[...], dv_ref[...]
    dn = times_back(dk, wk) + times_back(dv, wv)
    nt = n_ref[...].T
    x = x_ref[...].astype(f32)
    scaled = x * lax.rsqrt(jnp.mean(x * x, axis=-1, keepdims=True) + EPS)
    low_ref[...] = dn.astype(bf16)

    @pl.when(c == 0)
    def _():
        own = times_back(dq_ref[...], wq)
        own_ref[...] = own
        ggain_ref[...] = jnp.sum((own + dn) * scaled, axis=0, keepdims=True)
        acc[0] = mm(nt, dq_ref[...])
        acc[1] = mm(nt, dk)
        acc[2] = mm(nt, dv)
        acc[3] = mm(o_ref[...], da_ref[...], TN)

    @pl.when(c > 0)
    def _():
        ggain_ref[...] += jnp.sum(dn * scaled, axis=0, keepdims=True)
        acc[1] += mm(nt, dk)
        acc[2] += mm(nt, dv)

    @pl.when(c == pl.num_programs(0) - 1)
    def _():
        lane = lax.broadcasted_iota(i32, (D, LANES), 1)
        columns = [jnp.broadcast_to(g[...], (8, D)).T[:, :1] for g in (ggain_ref, second_ref)]
        last = jnp.where(lane == experts, columns[0], router_ref[...])
        last = jnp.where(lane == experts + 1, columns[1], last)
        last_sc[...] = jnp.concatenate([last, jnp.zeros((D, TILE - LANES), f32)], axis=1)
        if shard == D:
            for n in range(4):
                outs[0][0, n * D : (n + 1) * D, :] = acc[n].astype(bf16)
            outs[1][...] = last_sc[...].astype(bf16)
            return
        me, odd = place_ref[0], place_ref[1] > 0
        span = D // n_ctx
        keep_ref, give_ref = outs
        for step in range(n_ctx):
            start = pl.multiple_of((me ^ step) * span, span)
            for n in range(4):
                view = acc[n, pl.ds(start, span), :].reshape(span // shard // 2, 2, shard, D)
                mine = jnp.where(odd, view[:, 1], view[:, 0]).astype(bf16)
                other = jnp.where(odd, view[:, 0], view[:, 1]).astype(bf16)
                for p in range(WIDE):
                    at = slice((n * WIDE + p) * shard, (n * WIDE + p + 1) * shard)
                    cols = slice(p * TILE, (p + 1) * TILE)
                    keep_ref[step, :, at, :] = mine[:, :, cols]
                    give_ref[step, :, at, :] = other[:, :, cols]
            view = last_sc[pl.ds(start, span), :].reshape(span // shard // 2, 2, shard, TILE)
            at = slice(LAST * shard, (LAST + 1) * shard)
            keep_ref[step, :, at, :] = jnp.where(odd, view[:, 1], view[:, 0]).astype(bf16)
            give_ref[step, :, at, :] = jnp.where(odd, view[:, 0], view[:, 1]).astype(bf16)


def tail(place, n_all, dk, dv, x_all, dq, attn_low, d_attn, g_router, g_second, dense, held, n_ctx, experts):
    keys, rows = n_all.shape[0], dq.shape[0]
    groups, shard, _ = held
    step = pl.BlockSpec((rows, D), lambda c, o: (c, 0))
    row = const_spec((rows, D))
    parts = [(n_ctx, groups // 2 // n_ctx, (LAST + 1) * shard, TILE)] * 2
    if groups == 1:
        parts = [(1, 4 * D, D), (D, TILE)]
    return pl.pallas_call(
        functools.partial(tail_kernel, shard, n_ctx, experts),
        grid_spec=pltpu.PrefetchScalarGridSpec(
            num_scalar_prefetch=1,
            grid=(keys // rows,),
            in_specs=[step] * 4
            + [row] * 3
            + [const_spec((D, LANES)), const_spec((1, D))]
            + piece_specs(held, 0, 3 * WIDE),
            out_specs=[pl.BlockSpec((rows, D), lambda c, o: (c ^ o[0], 0)), row]
            + [const_spec(p) for p in parts],
            scratch_shapes=[pltpu.VMEM((4, D, D), f32), pltpu.VMEM((1, D), f32), pltpu.VMEM((D, TILE), f32)],
        ),
        out_shape=[
            jax.ShapeDtypeStruct((keys, D), bf16),
            jax.ShapeDtypeStruct((rows, D), f32),
        ]
        + [jax.ShapeDtypeStruct(p, bf16) for p in parts],
        compiler_params=pltpu.CompilerParams(vmem_limit_bytes=VMEM),
        cost_estimate=BRIEF,
        name="tail",
    )(place, n_all, dk, dv, x_all, dq, attn_low, d_attn, g_router, g_second, *[dense] * (3 * WIDE))


def split_heads(dst, values, first):
    none = jnp.zeros((), bf16)
    for g in range(GRPS):
        part = values[:, g * LANES : (g + 1) * LANES]
        dst[2 * g] = jnp.where(first, part, none)
        dst[2 * g + 1] = jnp.where(first, none, part)


def pair_lanes(h):
    return slice(h // 2 * LANES, (h // 2 + 1) * LANES)


def head_rows(h):
    return slice(h * HD, (h + 1) * HD)


def key_bias(sk_ref, rk_ref, sq_ref, rq_ref):
    sk = sk_ref[...]
    ok = ((sk == 0) | (sk == sq_ref[0])) & (rk_ref[...] <= rq_ref[0])
    return jnp.where(ok, 0.0, NEG)


def attend_kernel(
    flag_ref, q_ref, k_ref, vt_ref, sq_ref, rq_ref, sk_ref, rk_ref,
    o_ref, low_ref, lse_ref, qm_sc, m_sc, l_sc, acc_sc,
):
    i, j = pl.program_id(0), pl.program_id(1)
    count = pl.num_programs(1)

    @pl.when(j == 0)
    def _():
        m_sc[...] = jnp.full(m_sc.shape, FLOOR, f32)
        l_sc[...] = jnp.zeros(l_sc.shape, f32)
        acc_sc[...] = jnp.zeros(acc_sc.shape, f32)
        split_heads(qm_sc, q_ref[...], first_head(q_ref.shape[0]))

    @pl.when(flag_ref[i * count + j] > 0)
    def _():
        bias = key_bias(sk_ref, rk_ref, sq_ref, rq_ref)
        scores = [mm(k_ref[:, pair_lanes(h)], qm_sc[h], NT) + bias for h in range(HEADS)]
        m_old = m_sc[:HEADS]
        tops = [jnp.max(s, axis=0, keepdims=True) for s in scores]
        m_new = jnp.maximum(m_old, jnp.concatenate(tops, axis=0))
        a = jnp.exp(m_old - m_new)
        m_sc[:HEADS] = m_new
        probs = [jnp.exp(s - m_new[h : h + 1]) for h, s in enumerate(scores)]
        sums = [jnp.sum(p, axis=0, keepdims=True) for p in probs]
        l_sc[:HEADS] = l_sc[:HEADS] * a + jnp.concatenate(sums, axis=0)
        for h, p in enumerate(probs):
            at = head_rows(h)
            acc_sc[at] = acc_sc[at] * a[h : h + 1] + mm(vt_ref[0, at], p.astype(bf16))

    @pl.when(j == count - 1)
    def _():
        total = jnp.maximum(l_sc[...], 1e-30)
        lse_ref[0] = m_sc[...] + jnp.log(total)
        inv = 1.0 / total
        for h in range(HEADS):
            at = head_rows(h)
            acc_sc[at] = acc_sc[at] * inv[h : h + 1]
        o = acc_sc[...].T
        o_ref[...] = o
        low_ref[...] = o.astype(bf16)


def attend(flags, q, k, vt, seg_q, rot_q, seg_k, rot_k, block):
    rows, keys = q.shape[0], k.shape[0]
    nq, nk = rows // block, keys // block
    q_spec = pl.BlockSpec((block, D), lambda i, j, f: (i, 0))
    k_spec = pl.BlockSpec((block, D), lambda i, j, f: (j, 0))
    vt_spec = pl.BlockSpec((1, D, block), lambda i, j, f: (j, 0, 0))
    row_spec = pl.BlockSpec((1, 1, block), lambda i, j, f: (i, 0, 0))
    col_spec = pl.BlockSpec((block, 1), lambda i, j, f: (j, 0))
    return pl.pallas_call(
        attend_kernel,
        grid_spec=pltpu.PrefetchScalarGridSpec(
            num_scalar_prefetch=1,
            grid=(nq, nk),
            in_specs=[q_spec, k_spec, vt_spec, row_spec, row_spec, col_spec, col_spec],
            out_specs=[q_spec, q_spec, pl.BlockSpec((1, 16, block), lambda i, j, f: (i, 0, 0))],
            scratch_shapes=[
                pltpu.VMEM((HEADS, block, LANES), bf16),
                pltpu.VMEM((16, block), f32),
                pltpu.VMEM((16, block), f32),
                pltpu.VMEM((D, block), f32),
            ],
        ),
        out_shape=[
            jax.ShapeDtypeStruct((rows, D), f32),
            jax.ShapeDtypeStruct((rows, D), bf16),
            jax.ShapeDtypeStruct((nq, 16, block), f32),
        ],
        compiler_params=pltpu.CompilerParams(vmem_limit_bytes=VMEM),
        cost_estimate=BRIEF,
        name="attend",
    )(flags, q, k, vt, seg_q, rot_q, seg_k, rot_k)


def attend_back_kernel(
    flag_ref, q_ref, do_ref, k_ref, v_ref, lse_ref, delta_ref, sq_ref, rq_ref,
    sk_ref, rk_ref, cosk_ref, sink_ref, cosq_ref, sinq_ref,
    dq_ref, dk_ref, dv_ref, dq_sc, dk_sc, dv_sc, qm_sc, dom_sc,
):
    j, i = pl.program_id(0), pl.program_id(1)
    nk, nq = pl.num_programs(0), pl.num_programs(1)

    @pl.when(i == 0)
    def _():
        dk_sc[...] = jnp.zeros(dk_sc.shape, f32)
        dv_sc[...] = jnp.zeros(dv_sc.shape, f32)

    @pl.when(j == 0)
    def _():
        first = first_head(q_ref.shape[0])
        dq_sc[i] = jnp.zeros(dq_sc.shape[1:], f32)
        split_heads(qm_sc.at[i], q_ref[...], first)
        split_heads(dom_sc.at[i], do_ref[...], first)

    @pl.when(flag_ref[i * nk + j] > 0)
    def _():
        bias = key_bias(sk_ref, rk_ref, sq_ref, rq_ref)
        kt = k_ref[...].T
        heads = range(HEADS)
        scores = [mm(k_ref[:, pair_lanes(h)], qm_sc[i, h], NT) + bias for h in heads]
        dps = [mm(v_ref[:, pair_lanes(h)], dom_sc[i, h], NT) for h in heads]
        probs = [jnp.exp(scores[h] - lse_ref[0, h : h + 1, :]) for h in heads]
        ds = [(probs[h] * (dps[h] - delta_ref[0, h : h + 1, :])).astype(bf16) for h in heads]
        low = [p.astype(bf16) for p in probs]
        for h in range(0, HEADS, 2):
            at = pair_lanes(h)
            dv_sc[:, at] += mm(low[h], dom_sc[i, h]) + mm(low[h + 1], dom_sc[i, h + 1])
            dk_sc[:, at] += mm(ds[h], qm_sc[i, h]) + mm(ds[h + 1], qm_sc[i, h + 1])
        for h in heads:
            at = head_rows(h)
            dq_sc[i, at, :] += mm(kt[at], ds[h])

    @pl.when(i == nq - 1)
    def _():
        dk_ref[...] = turn(dk_sc[...], cosk_ref[...], -sink_ref[...]).astype(bf16)
        dv_ref[...] = dv_sc[...].astype(bf16)

    @pl.when(j == nk - 1)
    def _():
        back = turn(dq_sc[i].T, cosq_ref[...], -sinq_ref[...])
        dq_ref[...] = (back * (1.0 / math.sqrt(HD))).astype(bf16)


def attend_back(flags, q, d_o, k, v, lse, delta, seg_q, rot_q, seg_k, rot_k, cosine, sine, block):
    rows, keys = q.shape[0], k.shape[0]
    nq, nk = rows // block, keys // block
    q_spec = pl.BlockSpec((block, D), lambda j, i, f: (i, 0))
    k_spec = pl.BlockSpec((block, D), lambda j, i, f: (j, 0))
    stat_spec = pl.BlockSpec((1, 16, block), lambda j, i, f: (i, 0, 0))
    row_spec = pl.BlockSpec((1, 1, block), lambda j, i, f: (i, 0, 0))
    col_spec = pl.BlockSpec((block, 1), lambda j, i, f: (j, 0))
    tabk_spec = pl.BlockSpec((block, LANES), lambda j, i, f: (j, 0))
    tabq_spec = pl.BlockSpec((block, LANES), lambda j, i, f: (i, 0))
    return pl.pallas_call(
        attend_back_kernel,
        grid_spec=pltpu.PrefetchScalarGridSpec(
            num_scalar_prefetch=1,
            grid=(nk, nq),
            in_specs=[q_spec, q_spec, k_spec, k_spec, stat_spec, stat_spec, row_spec, row_spec]
            + [col_spec] * 2
            + [tabk_spec] * 2
            + [tabq_spec] * 2,
            out_specs=[
                pl.BlockSpec((block, D), lambda j, i, f: (jnp.where(j == nk - 1, i, 0), 0)),
                k_spec,
                k_spec,
            ],
            scratch_shapes=[
                pltpu.VMEM((nq, D, block), f32),
                pltpu.VMEM((block, D), f32),
                pltpu.VMEM((block, D), f32),
                pltpu.VMEM((nq, HEADS, block, LANES), bf16),
                pltpu.VMEM((nq, HEADS, block, LANES), bf16),
            ],
        ),
        out_shape=[
            jax.ShapeDtypeStruct((rows, D), bf16),
            jax.ShapeDtypeStruct((keys, D), bf16),
            jax.ShapeDtypeStruct((keys, D), bf16),
        ],
        compiler_params=pltpu.CompilerParams(vmem_limit_bytes=VMEM),
        cost_estimate=BRIEF,
        name="attend_back",
    )(flags, q, d_o, k, v, lse, delta, seg_q, rot_q, seg_k, rot_k, cosine, sine, cosine, sine)


def input_kernel(own_ref, dres_ref, x_ref, gain_ref, got_ref, out_ref):
    grad = own_ref[...]
    for n in range(got_ref.shape[0]):
        grad += got_ref[n].astype(f32)
    x = x_ref[...].astype(f32)
    inv = lax.rsqrt(jnp.mean(x * x, axis=-1, keepdims=True) + EPS)
    out_ref[...] = dres_ref[...] + norm_back(x, inv, gain_ref[0:1, :], grad)


def input_back(own, d_resid, x_low, gain, got):
    rows = x_low.shape[0]
    row = const_spec((rows, D))
    return pl.pallas_call(
        input_kernel,
        grid=(1,),
        in_specs=[row, row, row, const_spec((2, D)), const_spec(got.shape)],
        out_specs=row,
        out_shape=jax.ShapeDtypeStruct((rows, D), f32),
        compiler_params=pltpu.CompilerParams(vmem_limit_bytes=VMEM),
        cost_estimate=BRIEF,
        name="input_back",
    )(own, d_resid, x_low, gain, got)


def hidden_back(ha, hb, dh):
    sg = 1.0 / (1.0 + jnp.exp(-ha))
    si = ha * sg
    he = (si * hb).astype(bf16)
    da = (dh * hb * (sg * (1.0 + ha * (1.0 - sg)))).astype(bf16)
    return he, da, (dh * si).astype(bf16)


def shared_kernel(
    fast, odd_ref, x_ref, gy_ref, wg_ref, wu_ref, wd_ref, y_ref, gx_ref, *refs
):
    f = pl.program_id(0)
    xt_sc = refs[-1]

    @pl.when(f == 0)
    def _():
        y_ref[...] = jnp.zeros(y_ref.shape, f32)
        gx_ref[...] = jnp.zeros(gx_ref.shape, f32)
        xt_sc[...] = x_ref[...].T

    wg, wu = wg_ref[...].reshape(D, TILE), wu_ref[...].reshape(D, TILE)
    part = wd_ref.shape[1] // WIDE
    many = wd_ref.shape[0]
    wd = [wd_ref[:, n * part : (n + 1) * part, :].reshape(TILE, TILE) for n in range(WIDE)]
    x, gy = x_ref[...], gy_ref[...]
    cut = [slice(n * TILE, (n + 1) * TILE) for n in range(WIDE)]
    ha, hb = mm(x, wg), mm(x, wu)
    dh = sum(mm(gy[:, cut[n]], wd[n], NT) for n in range(WIDE))
    he, da, db = hidden_back(ha, hb, dh)
    for n in range(WIDE):
        y_ref[:, cut[n]] += mm(he, wd[n])
    gx_ref[...] += mm(da, wg, NT) + mm(db, wu, NT)
    xt = xt_sc[...]
    gate, up = mm(xt, da), mm(xt, db)
    down = mm(he, gy, TN)
    if not fast:
        gg_ref, gu_ref, gd_ref = refs[:3]
        gg_ref[0] = gate.astype(bf16)
        gu_ref[0] = up.astype(bf16)
        for n in range(WIDE):
            gd_ref[:, n * part : (n + 1) * part, :] = down[:, cut[n]].astype(bf16).reshape(many, part, TILE)
        return

    keep_ref, give_ref, up_sc, down_sc, sem = refs[:5]
    pairs, shard = up_sc.shape[2:4]
    odd = odd_ref[0] > 0
    last = pl.num_programs(0) - 1

    def copies(tile):
        out = []
        for n, dst in enumerate((keep_ref, give_ref)):
            for m in range(2):
                rows = pl.ds((m * (last + 1) + tile) * shard, shard)
                out.append(pltpu.make_async_copy(up_sc.at[n, m], dst.at[:, rows, :], sem.at[n, m]))
            where = dst.at[pl.ds(tile * (many // 2), many // 2), pl.ds(2 * (last + 1) * shard, WIDE * part), :]
            out.append(pltpu.make_async_copy(down_sc.at[n], where, sem.at[n, 2]))
        return out

    @pl.when(f > 0)
    def _():
        for copy in copies(f - 1):
            copy.wait()

    for m, grad in enumerate((gate, up)):
        view = grad.reshape(pairs, 2, shard, TILE)
        up_sc[0, m] = jnp.where(odd, view[:, 1], view[:, 0]).astype(bf16)
        up_sc[1, m] = jnp.where(odd, view[:, 0], view[:, 1]).astype(bf16)
    for n in range(WIDE):
        view = down[:, cut[n]].reshape(many // 2, 2, part, TILE)
        at = slice(n * part, (n + 1) * part)
        down_sc[0, :, at, :] = jnp.where(odd, view[:, 1], view[:, 0]).astype(bf16)
        down_sc[1, :, at, :] = jnp.where(odd, view[:, 0], view[:, 1]).astype(bf16)
    for copy in copies(f):
        copy.start()

    @pl.when(f == last)
    def _():
        for copy in copies(f):
            copy.wait()


def shared_unit(odd, x, gy, w_gu, held, w_d, down_shard):
    rows = x.shape[0]
    devices = w_d.shape[0]
    hidden = devices * down_shard
    tiles = hidden // TILE
    groups, part, base = held
    fast = groups > 1
    wide = jax.ShapeDtypeStruct((rows, D), f32)
    many = TILE // down_shard
    piece = lambda first: pl.BlockSpec((groups, part, TILE), lambda f, o: (0, first + f, 0))
    down = pl.BlockSpec((many, WIDE * down_shard, TILE), lambda f, o: (f, 0, 0))
    if fast:
        total = 2 * tiles * part + WIDE * down_shard
        grads = [jax.ShapeDtypeStruct((devices // 2, total, TILE), bf16)] * 2
        specs = [pl.BlockSpec(memory_space=pl.ANY)] * 2
        scratch = [
            pltpu.VMEM((2, 2, devices // 2, part, TILE), bf16),
            pltpu.VMEM((2, many // 2, WIDE * down_shard, TILE), bf16),
            pltpu.SemaphoreType.DMA((2, 3)),
        ]
    else:
        grads = [jax.ShapeDtypeStruct((groups, tiles * part, TILE), bf16)] * 2
        grads.append(jax.ShapeDtypeStruct((devices, WIDE * down_shard, TILE), bf16))
        specs = [piece(0), piece(0), down]
        scratch = []
    row = const_spec((rows, D))
    outs = pl.pallas_call(
        functools.partial(shared_kernel, fast),
        grid_spec=pltpu.PrefetchScalarGridSpec(
            num_scalar_prefetch=1,
            grid=(tiles,),
            in_specs=[row, row, piece(base), piece(base + tiles), down],
            out_specs=[row, row] + specs,
            scratch_shapes=scratch + [pltpu.VMEM((D, rows), bf16)],
        ),
        out_shape=[wide, wide] + grads,
        compiler_params=pltpu.CompilerParams(vmem_limit_bytes=VMEM),
        cost_estimate=BRIEF,
        name="shared_unit",
    )(odd, x, gy, w_gu, w_gu, w_d)
    if fast:
        return outs
    y, gx, g_gate, g_up, g_down = outs
    shard = D // devices
    g_gate, g_up = (
        g.reshape(tiles, devices, shard, TILE).transpose(1, 0, 2, 3).reshape(devices, -1, TILE) for g in (g_gate, g_up)
    )
    return (y, gx) + split_cores(jnp.concatenate([g_gate, g_up, g_down], axis=1))


def expert_kernel(
    chunk, x_ref, c_ref, other_ref, mine_ref, last_ref, wg_ref, wu_ref, wd_ref,
    y_ref, gx_ref, gr_ref, he_ref, da_ref, db_ref, xt_ref, gt_ref, y_sc, gx_sc, gy_sc, gap_sc,
):
    f = pl.program_id(0)

    def apart():
        sources, cap = other_ref.shape
        lane = lax.broadcasted_iota(i32, (cap, LANES), 1)
        other = other_ref[...].astype(f32).T.astype(i32)
        parts = [jnp.where(lane == other[:, e : e + 1], 1.0, 0.0) for e in range(sources)]
        return mine_ref[...] - jnp.concatenate(parts, axis=0)

    @pl.when(f == 0)
    def _():
        router = last_ref[...].reshape(D, TILE)[:, :LANES]
        gap = jnp.sum(mm(x_ref[...], router) * apart(), axis=-1, keepdims=True)
        gap_sc[...] = gap
        gate = 1.0 / (1.0 + jnp.exp(-gap))
        gy = (c_ref[...].astype(f32) * gate).astype(bf16)
        gy_sc[...] = gy
        xt_ref[...] = x_ref[...].T
        gt_ref[...] = gy.T
        y_sc[...] = jnp.zeros(y_sc.shape, f32)
        gx_sc[...] = jnp.zeros(gx_sc.shape, f32)

    wg, wu, wd = wg_ref[0, 0], wu_ref[0, 0], wd_ref[0, 0]
    for c in range(x_ref.shape[0] // chunk):
        at = slice(c * chunk, (c + 1) * chunk)
        x, gy = x_ref[at], gy_sc[at]
        he, da, db = hidden_back(mm(x, wg), mm(x, wu), mm(gy, wd))
        he_ref[at] = he
        da_ref[at] = da
        db_ref[at] = db
        y_sc[at] += mm(he, wd, NT)
        gx_sc[at] += mm(da, wg, NT) + mm(db, wu, NT)

    @pl.when(f == pl.num_programs(0) - 1)
    def _():
        y = y_sc[...].astype(bf16)
        y_ref[...] = y
        dgate = jnp.sum(c_ref[...].astype(f32) * y.astype(f32), axis=-1, keepdims=True)
        gap = gap_sc[...]
        slope = dgate / (1.0 + jnp.exp(-gap)) / (1.0 + jnp.exp(gap))
        d_logits = slope * apart()
        high = d_logits.astype(bf16)
        rest = (d_logits - high.astype(f32)).astype(bf16)
        router = last_ref[...].reshape(D, TILE)[:, :LANES]
        gx_ref[...] = (gx_sc[...] + mm(high, router, NT) + mm(rest, router, NT)).astype(bf16)
        gr_ref[...] = mm(xt_ref[...], high) + mm(xt_ref[...], rest)


def expert_unit(x, c, other, mine, dense, held, weights):
    rows = x.shape[0]
    shards, _, _, part = weights.shape
    hidden = shards * part
    per = part // TILE
    specs = [pl.BlockSpec((1, 1, D, TILE), lambda f, w=w: (f // per, w, 0, f % per)) for w in range(3)]
    tile_spec = pl.BlockSpec((rows, TILE), lambda f: (0, f))
    kept = jax.ShapeDtypeStruct((rows, hidden), bf16)
    wide = jax.ShapeDtypeStruct((rows, D), bf16)
    tall = jax.ShapeDtypeStruct((D, rows), bf16)
    row_spec = const_spec((rows, D))
    return pl.pallas_call(
        functools.partial(expert_kernel, rows // 2),
        grid=(hidden // TILE,),
        in_specs=[row_spec, row_spec, const_spec(other.shape), const_spec((1, LANES))]
        + piece_specs(held, LAST, 1)
        + specs,
        out_specs=[row_spec] * 2 + [const_spec((D, LANES))] + [tile_spec] * 3 + [const_spec((D, rows))] * 2,
        out_shape=[wide, wide, jax.ShapeDtypeStruct((D, LANES), f32), kept, kept, kept, tall, tall],
        scratch_shapes=[
            pltpu.VMEM((rows, D), f32),
            pltpu.VMEM((rows, D), f32),
            pltpu.VMEM((rows, D), bf16),
            pltpu.VMEM((rows, 1), f32),
        ],
        compiler_params=pltpu.CompilerParams(vmem_limit_bytes=VMEM),
        cost_estimate=BRIEF,
        name="expert_unit",
    )(x, c, other, mine, dense, weights, weights, weights)


def expert_grads_kernel(left_ref, *refs):
    left = left_ref[...]
    for n, ref in enumerate(refs[:-1]):
        refs[-1][0, n] = mm(left, ref[...]).astype(bf16)


def expert_grads(left, rights, shards):
    rows, hidden = rights[0].shape
    part = hidden // shards
    per = part // TILE
    count = len(rights)
    return pl.pallas_call(
        expert_grads_kernel,
        grid=(hidden // TILE,),
        in_specs=[const_spec((D, rows))] + [pl.BlockSpec((rows, TILE), lambda f: (0, f))] * count,
        out_specs=pl.BlockSpec((1, count, D, TILE), lambda f: (f // per, 0, 0, f % per)),
        out_shape=jax.ShapeDtypeStruct((shards, count, D, part), bf16),
        compiler_params=pltpu.CompilerParams(vmem_limit_bytes=VMEM),
        cost_estimate=BRIEF,
        name="expert_grads",
    )(left, *rights)


EVERY = ("ctx", "fsdp")


def swap_fsdp(values):
    return lax.all_to_all(values, "fsdp", split_axis=0, concat_axis=0, tiled=True)


def peer(values, axis, size, step):
    return lax.ppermute(values, axis, [(i, i ^ step) for i in range(size)])


def block_of(array, index):
    return lax.dynamic_index_in_dim(array, index, 0, keepdims=False)


def by_step(array, n_ctx):
    array = array.reshape((n_ctx, array.shape[0] // n_ctx) + array.shape[1:])
    me = lax.axis_index("ctx")
    return [block_of(array, me ^ step) for step in range(n_ctx)]


def meet_core(keep, got):
    parts = [mine.astype(f32) + other.astype(f32) for mine, other in zip(keep, got)]
    return parts[:1] + [p.astype(bf16) for p in parts[1:]]


def meet_ctx(parts, n_ctx):
    return list(parts[:1]) + [peer(parts[step], "ctx", n_ctx, step) for step in range(1, n_ctx)]


def add_up(parts):
    total = sum(p.astype(f32) for p in parts)
    return total, total.astype(bf16)


def meet_far(total, low, n_fsdp):
    me = lax.axis_index("fsdp") // 2
    out = block_of(total, me)
    for step in range(1, n_fsdp // 2):
        out += peer(block_of(low, me ^ step), "fsdp", n_fsdp, 2 * step).astype(f32)
    return out


def meet_far_once(low, n_fsdp):
    groups = [[2 * i + c for i in range(n_fsdp // 2)] for c in range(2)]
    got = lax.all_to_all(low, "fsdp", split_axis=0, concat_axis=0, tiled=True, axis_index_groups=groups)
    return jnp.sum(got.astype(f32), axis=0)


def split_cores(chunks):
    odd = lax.axis_index("fsdp") % 2
    view = chunks.reshape((chunks.shape[0] // 2, 2) + chunks.shape[1:])
    return jnp.where(odd == 0, view[:, 0], view[:, 1]), jnp.where(odd == 0, view[:, 1], view[:, 0])


def norm_back(values, inv, gain, grad):
    scaled = grad * gain
    mean = jnp.mean(scaled * values, axis=-1, keepdims=True)
    return inv * scaled - values * (inv * inv * inv * mean)


def positions(order, order_rows, segment_row, valid_row, block):
    blocks = order_rows
    hot = order[:, None] == jnp.arange(blocks, dtype=i32)[None, :]

    def pick(row):
        return jnp.sum(jnp.where(hot[:, :, None], row.reshape(1, blocks, block), 0), axis=1)

    segment, valid = pick(segment_row), pick(valid_row)
    position = order[:, None] * block + jnp.arange(block, dtype=i32)[None, :]
    bounds = jnp.arange(NCONT + 1, dtype=i32)
    starts = jnp.sum((segment_row[None, :] < bounds[:, None]).astype(i32), axis=1)
    begin = jnp.sum(jnp.where(segment[:, :, None] == bounds, starts, 0), axis=-1)
    rotary = position - begin + jnp.where(segment > 0, starts[1], 0)
    return segment, rotary, valid


def local(
    n_ctx, n_fsdp,
    tokens, cotangent, block_order, segment_ids, valid_mask, routes,
    attention_gain, query_weight, key_weight, value_weight, out_weight,
    feedforward_gain, router, shared_gate, shared_up, shared_down,
    expert_gate, expert_up, expert_down,
):
    devices = n_ctx * n_fsdp
    x_low, c_low = tokens[0], cotangent[0]
    rows = x_low.shape[0]
    group = segment_ids.shape[1]
    blocks = block_order.shape[1]
    block = group // blocks
    own = rows // block
    experts = n_fsdp
    cap = 2 * rows * TOPK // experts
    slots = experts * cap
    my_ctx = lax.axis_index("ctx")
    my_fsdp = lax.axis_index("fsdp")
    shard = query_weight.shape[0]
    down_shard = shared_down.shape[0]
    hidden = shared_gate.shape[1]
    tiles = hidden // TILE
    tie = lax.optimization_barrier

    gains = jnp.stack([attention_gain, feedforward_gain], axis=1)
    squares = (query_weight, key_weight, value_weight, out_weight)
    dense = lax.all_gather(pack_weights(squares, (router, gains)), EVERY, axis=0, tiled=False)

    x_all = jnp.concatenate(
        [x_low] + [peer(x_low, "ctx", n_ctx, step) for step in range(1, n_ctx)], axis=0
    )
    dev = my_ctx ^ jnp.arange(n_ctx, dtype=i32)
    which = (dev[:, None] * own + jnp.arange(own, dtype=i32)[None, :]).reshape(-1)
    order = jnp.sum(
        jnp.where(which[:, None] == jnp.arange(blocks, dtype=i32)[None, :], block_order[0][None, :], 0), axis=1
    )
    seg, rot, val = positions(order, blocks, segment_ids[0], valid_mask[0], block)
    seg_q, rot_q = seg[:own], rot[:own]
    seg_k = jnp.where(val > 0, seg, -1)
    allowed = (
        (seg_k[None, :, None, :] == 0) | (seg_k[None, :, None, :] == seg_q[:, None, :, None])
    ) & (rot[None, :, None, :] <= rot_q[:, None, :, None])
    flags = jnp.any(allowed, axis=(2, 3)).astype(i32).reshape(-1)
    half = HD // 2
    lane = jnp.arange(LANES, dtype=i32)
    frequency = jnp.exp((lane % half).astype(f32) * (-math.log(BASE) / half))
    angles = rot.reshape(-1).astype(f32)[:, None] * frequency[None, :]
    cosine = jnp.cos(angles)
    sine = jnp.sin(angles) * jnp.where(lane % HD < half, -1.0, 1.0)
    seg_rows, rot_rows = seg_q.reshape(own, 1, block), rot_q.reshape(own, 1, block)
    seg_cols, rot_cols = seg_k.reshape(-1, 1), rot.reshape(-1, 1)
    keep = val[:own].reshape(-1, 1).astype(f32)

    chosen = routes[0]
    every = jnp.arange(experts, dtype=i32)
    hot = jnp.any(chosen[:, :, None] == every, axis=1)
    before = (jnp.arange(rows)[:, None] > jnp.arange(rows)[None, :]).astype(bf16)
    rank = mm(before, hot.astype(bf16)).astype(i32)
    slot_cols = jnp.where(hot, rank, -1)
    slot_rows = slot_cols.T
    place = slot_rows[:, None, :] == jnp.arange(cap, dtype=i32)[None, :, None]
    other = jnp.sum(chosen, axis=-1)[None, :] - every[:, None]
    other = jnp.sum(jnp.where(place, other[:, None, :], 0), axis=-1)
    other = swap_fsdp(other)
    c_send = mm(place.astype(bf16).reshape(slots, rows), c_low).astype(bf16).reshape(experts, cap, D)

    early = (dense, x_all, flags, cosine, sine, seg_rows, rot_rows, seg_cols, rot_cols, slot_cols, slot_rows, other, c_send, keep)
    (dense, x_all, flags, cosine, sine, seg_rows, rot_rows, seg_cols, rot_cols, slot_cols, slot_rows, other, c_send, keep) = tie(early)

    mine = jnp.stack([expert_gate[0], expert_up[0], expert_down[0].T])
    mine, dense = tie((mine, dense))
    expert_w = lax.all_gather(mine, "ctx", axis=0, tiled=False)
    c_slots = swap_fsdp(c_send).reshape(slots, D)

    cut = 2 * tiles * shard
    square, held = in_pieces(dense, 0, LAST + 1, shard)

    n_all, q, k, v, vt, gains = project(x_all, experts, square, held, cosine, sine, block, rows, 1)
    attn, attn_low, lse = attend(flags, q, k, vt, seg_rows, rot_rows, seg_cols, rot_cols, block)
    resid, n_two, inv_two, x_send = mid(attn_low, x_low, gains, slot_rows, square, held, cap)
    x_send, n_two, c_slots = tie((x_send, n_two, c_slots))
    x_slots = swap_fsdp(x_send).reshape(slots, D)

    shared_pack = pack_weights((shared_down, shared_gate, shared_up), ())
    shared_pack, n_two = tie((shared_pack, n_two))
    shared_w = lax.all_gather(shared_pack, EVERY, axis=0, tiled=False)
    shared_sq, shared_held = in_pieces(shared_w, WIDE * down_shard, 2 * tiles, shard)

    is_mine = (lane == my_fsdp).astype(f32)[None, :]
    y_slots, gx_slots, grad_router, e_he, e_da, e_db, e_xt, e_gt = expert_unit(
        x_slots, c_slots, other, is_mine, square, held, expert_w
    )
    gx_slots, n_shared = tie((gx_slots, n_two))
    gx_back = swap_fsdp(gx_slots.reshape(experts, cap, D))
    e_down = expert_grads(e_gt, (e_he,), n_ctx)
    e_down, e_xt = tie((e_down, e_xt))
    e_down_sums = lax.psum_scatter(e_down, "ctx", scatter_dimension=0, tiled=False).astype(f32)
    e_grads = expert_grads(e_xt, (e_da, e_db), n_ctx)

    e_grads, n_shared = tie((e_grads, n_shared))
    odd = (my_fsdp % 2).reshape(1)
    s_out, s_dn, s_keep, s_give = shared_unit(odd, n_shared, c_low, shared_sq, shared_held, shared_w, down_shard)
    s_give = s_give.reshape((n_ctx, -1) + s_give.shape[1:])
    s_got = jnp.stack([peer(s_give[n], "fsdp", n_fsdp, 1) for n in range(n_ctx)])
    s_parts = (s_keep.reshape(s_got.shape).astype(f32) + s_got.astype(f32)).astype(bf16)
    e_grads, gx_back, s_parts = tie((e_grads, gx_back, s_parts))
    s_low = lax.psum_scatter(s_parts, "ctx", scatter_dimension=0, tiled=False)

    d_resid, d_attn, d_mix, delta, grad_gain_two = mid_back(
        gx_back, slot_cols, s_dn, resid, inv_two, gains, c_low, attn, square, held, block
    )
    d_mix, y_slots, e_grads = tie((d_mix, y_slots, e_grads))
    e_sums = lax.psum_scatter(e_grads, "ctx", scatter_dimension=0, tiled=False)
    y_back = swap_fsdp(y_slots.reshape(experts, cap, D))
    dq, dk, dv = attend_back(
        flags, q, d_mix, k, v, lse, delta, seg_rows, rot_rows, seg_cols, rot_cols, cosine, sine, block
    )
    where = jnp.stack([my_ctx, my_fsdp % 2])
    d_low, d_own, *halves = tail(
        where, n_all, dk, dv, x_all, dq, attn_low, d_attn, grad_router, grad_gain_two, square, held, n_ctx, experts
    )
    if held[0] == 1:
        g_all = halves[0].reshape(4, devices, shard, WIDE, TILE).transpose(1, 0, 3, 2, 4)
        g_all = g_all.reshape(devices, 4 * WIDE * shard, TILE)
        g_all = jnp.concatenate([g_all, halves[1].reshape(devices, shard, TILE)], axis=1)
        g_keep, g_give = (jnp.stack(by_step(h, n_ctx)) for h in split_cores(g_all))
    else:
        g_keep, g_give = halves
    y_back, s_low = tie((y_back, s_low))
    s_grads = meet_far_once(s_low, n_fsdp)
    g_give, e_down_sums = tie((g_give, e_down_sums))
    g_parts = meet_core(g_keep, peer(g_give, "fsdp", n_fsdp, 1))
    y_back, *g_parts = tie((y_back, *g_parts))
    g_parts = meet_ctx(g_parts, n_ctx)

    output, sums = finish(y_back, slot_cols, chosen, n_two, square, held, s_out, resid, x_low, keep)

    e_down_out = e_down_sums[0].T[None]
    d_low, s_grads, output, *g_parts = tie((d_low, s_grads, output, *g_parts))
    g_total, g_low = add_up(g_parts)
    dense_grads = meet_far(g_total, g_low, n_fsdp)
    sums, dense_grads = tie((sums, dense_grads))
    level = [sums] + [peer(sums, "ctx", n_ctx, step) for step in range(1, n_ctx)]
    while len(level) > 1:
        level = [a + b for a, b in zip(level[0::2], level[1::2])]
    group_sums = level[0]
    valid_count = jnp.sum(valid_mask[0]).astype(f32)
    stats = jnp.sqrt(group_sums[:, 0] / (valid_count * D))[None]

    def from_pieces(array, part):
        return array.reshape(-1, part, TILE).transpose(1, 0, 2).reshape(part, -1)

    grad_shared_gate = from_pieces(s_grads[: tiles * shard], shard)
    grad_shared_up = from_pieces(s_grads[tiles * shard : cut], shard)
    grad_shared_down = from_pieces(s_grads[cut:], down_shard)
    span = WIDE * shard
    g_query, g_key, g_value, g_out = (from_pieces(dense_grads[n * span : (n + 1) * span], shard) for n in range(4))
    got = lax.all_to_all(d_low.reshape(n_ctx, rows, D), "ctx", split_axis=0, concat_axis=0, tiled=True)
    input_grad = input_back(d_own, d_resid, x_low, gains, got)[None]
    input_grad, e_sums = tie((input_grad, e_sums))
    e_sums = e_sums.astype(f32)

    last = dense_grads[LAST * shard :]
    g_router, g_gain_one, g_gain_two = last[:, :experts], last[:, experts], last[:, experts + 1]

    return (
        output[None], input_grad, g_gain_one, g_query, g_key, g_value, g_out, g_gain_two, g_router,
        grad_shared_gate, grad_shared_up, grad_shared_down,
        e_sums[0][None], e_sums[1][None], e_down_out, stats,
    )


def solution(mesh):
    sizes = dict(mesh.shape)
    rows3 = P("fsdp", "ctx", None)
    group = P("fsdp", None)
    dense1 = P(("ctx", "fsdp"))
    dense2 = P(("ctx", "fsdp"), None)
    column = P("fsdp", None, "ctx")
    return jax.shard_map(
        functools.partial(local, sizes["ctx"], sizes["fsdp"]),
        mesh=mesh,
        in_specs=(rows3, rows3, group, group, group, rows3)
        + (dense1, dense2, dense2, dense2, dense2, dense1)
        + (dense2,) * 4
        + (column, column, rows3),
        out_specs=(rows3, rows3)
        + (dense1, dense2, dense2, dense2, dense2, dense1)
        + (dense2,) * 4
        + (column, column, rows3, group),
        check_vma=False,
    )
```

```python
import functools
import math

import jax
import jax.numpy as jnp
from jax import lax
from jax.experimental import pallas as pl
from jax.experimental.pallas import tpu as pltpu
from jax.sharding import PartitionSpec as P

D = 768
HEADS = 12
HD = 64
TOPK = 2
NCONT = 4

HIGH = lax.Precision.HIGHEST
EPS = 1e-06
NEG = -1e30
FLOOR = -5e29
BASE = 10000.0
LANES = 128
TILE = 256
GRPS = D // LANES
VMEM = 60 * 1024 * 1024

f32 = jnp.float32
bf16 = jnp.bfloat16
i32 = jnp.int32

NT = (((1,), (1,)), ((), ()))
NN = (((1,), (0,)), ((), ()))
TN = (((0,), (0,)), ((), ()))


def mm(a, b, dims=NN):
    return lax.dot_general(a, b, dims, preferred_element_type=f32)


def low_lanes(rows):
    lane = lax.broadcasted_iota(i32, (rows, LANES), 1)
    return lane % HD < HD // 2


def first_head(rows):
    return lax.broadcasted_iota(i32, (rows, LANES), 1) < HD


def turn(values, cosine, sine):
    low = low_lanes(values.shape[0])
    parts = []
    for g in range(GRPS):
        part = values[:, g * LANES : (g + 1) * LANES]
        other = jnp.where(
            low, pltpu.roll(part, LANES - HD // 2, 1), pltpu.roll(part, HD // 2, 1)
        )
        parts.append(part * cosine + other * sine)
    return jnp.concatenate(parts, axis=1)


def const_spec(shape):
    zeros = (0,) * len(shape)
    return pl.BlockSpec(shape, lambda *_: zeros)


BRIEF = pl.CostEstimate(flops=10**9, transcendentals=0, bytes_accessed=10**6)
WIDE = D // TILE
LAST = 4 * WIDE


def times(rows, pieces, out_dtype=f32):
    parts = [mm(rows, p[...].reshape(D, TILE)) for p in pieces]
    return jnp.concatenate(parts, axis=1).astype(out_dtype)


def times_back(rows, pieces):
    parts = [mm(rows[:, n * TILE : (n + 1) * TILE], p[...].reshape(D, TILE), NT) for n, p in enumerate(pieces)]
    return parts[0] + parts[1] + parts[2]


def piece_specs(held, first, count):
    groups, part, base = held
    first = first + base
    return [pl.BlockSpec((groups, part, TILE), lambda *_, p=p: (0, p, 0)) for p in range(first, first + count)]


def pack_kernel(with_last, *refs):
    out_ref = refs[-1]
    at = 0
    for ref in refs[:-3] if with_last else refs[:-1]:
        rows = ref.shape[0]
        for n in range(ref.shape[1] // TILE):
            out_ref[at : at + rows, :] = ref[:, n * TILE : (n + 1) * TILE]
            at += rows
    if with_last:
        router_ref, gains_ref = refs[-3:-1]
        rows, experts = router_ref.shape
        rest = jnp.zeros((rows, TILE - experts - 2), f32)
        last = [router_ref[...].astype(f32), gains_ref[...].astype(f32), rest]
        out_ref[at : at + rows, :] = jnp.concatenate(last, axis=1).astype(bf16)


def pack_weights(weights, last):
    operands = (*weights, *last)
    if weights[-1].shape[0] % 8:
        flat = [a.reshape(a.shape[0], -1, TILE).transpose(1, 0, 2).reshape(-1, TILE) for a in weights]
        if last:
            both = jnp.concatenate(last, axis=1)
            flat.append(jnp.pad(both, ((0, 0), (0, TILE - both.shape[1]))))
        return jnp.concatenate(flat, axis=0)
    rows = sum(a.shape[0] * (a.shape[1] // TILE) for a in weights) + (last[0].shape[0] if last else 0)
    return pl.pallas_call(
        functools.partial(pack_kernel, bool(last)),
        out_shape=jax.ShapeDtypeStruct((rows, TILE), bf16),
        compiler_params=pltpu.CompilerParams(vmem_limit_bytes=VMEM),
        cost_estimate=BRIEF,
        name="pack",
    )(*operands)


def in_pieces(dense, first, count, shard):
    if shard % 8 == 0:
        return dense, (dense.shape[0], shard, first // shard)
    square = dense[:, first : first + count * shard].reshape(dense.shape[0], count, shard, TILE)
    return square.transpose(1, 0, 2, 3).reshape(1, -1, TILE), (1, D, 0)


def qkv_kernel(own, experts, x_ref, last_ref, *refs):
    wq, wk, wv = refs[:WIDE], refs[WIDE : 2 * WIDE], refs[2 * WIDE : 3 * WIDE]
    cos_ref, sin_ref, n_ref, q_ref, k_ref, v_ref, vt_ref, gain_ref = refs[3 * WIDE :]

    @pl.when(pl.program_id(0) == 0)
    def _():
        last = last_ref[...].reshape(D, TILE)[:, :LANES].astype(f32).T
        gain_ref[...] = last[experts : experts + 2]

    x = x_ref[...].astype(f32)
    inv = lax.rsqrt(jnp.mean(x * x, axis=-1, keepdims=True) + EPS)
    n = (x * inv * gain_ref[0:1, :]).astype(bf16)
    n_ref[...] = n
    cosine = cos_ref[...]
    sine = sin_ref[...]
    k_ref[...] = turn(times(n, wk), cosine, sine).astype(bf16)
    v = times(n, wv, bf16)
    v_ref[...] = v
    block = vt_ref.shape[2]
    for b in range(vt_ref.shape[0]):
        vt_ref[b] = v[b * block : (b + 1) * block].T

    @pl.when(pl.program_id(0) < own)
    def _():
        q = turn(times(n, wq), cosine, sine)
        q_ref[...] = (q * (1.0 / math.sqrt(HD))).astype(bf16)


def project(x_all, experts, dense, held, cosine, sine, block, step, own):
    rows = x_all.shape[0]
    row_spec = pl.BlockSpec((step, D), lambda i: (i, 0))
    tab_spec = pl.BlockSpec((step, LANES), lambda i: (i, 0))
    wide = jax.ShapeDtypeStruct((rows, D), bf16)
    return pl.pallas_call(
        functools.partial(qkv_kernel, own, experts),
        grid=(rows // step,),
        in_specs=[row_spec] + piece_specs(held, LAST, 1) + piece_specs(held, 0, 3 * WIDE) + [tab_spec] * 2,
        out_specs=[
            row_spec,
            pl.BlockSpec((step, D), lambda i: (jnp.minimum(i, own - 1), 0)),
            row_spec,
            row_spec,
            pl.BlockSpec((step // block, D, block), lambda i: (i, 0, 0)),
            const_spec((2, D)),
        ],
        out_shape=[
            wide,
            jax.ShapeDtypeStruct((own * step, D), bf16),
            wide,
            wide,
            jax.ShapeDtypeStruct((rows // block, D, block), bf16),
            jax.ShapeDtypeStruct((2, D), f32),
        ],
        compiler_params=pltpu.CompilerParams(vmem_limit_bytes=VMEM),
        cost_estimate=BRIEF,
        name="qkv",
    )(x_all, *[dense] * (3 * WIDE + 1), cosine, sine)


def mid_kernel(cap, o_ref, x_ref, gain_ref, slot_ref, *refs):
    wo = refs[:WIDE]
    resid_ref, n_ref, inv_ref, send_ref = refs[WIDE:]
    resid = x_ref[...].astype(f32) + times(o_ref[...], wo)
    inv = lax.rsqrt(jnp.mean(resid * resid, axis=-1, keepdims=True) + EPS)
    n = (resid * inv * gain_ref[1:2, :]).astype(bf16)
    resid_ref[...] = resid
    n_ref[...] = n
    inv_ref[...] = inv
    place = lax.broadcasted_iota(i32, (cap, n.shape[0]), 0)
    for e in range(slot_ref.shape[0]):
        hot = (slot_ref[e : e + 1, :] == place).astype(f32).astype(bf16)
        send_ref[e] = mm(hot, n).astype(bf16)


def mid(attn_low, x_low, gain, slot_rows, dense, held, cap):
    rows = x_low.shape[0]
    experts = slot_rows.shape[0]
    return pl.pallas_call(
        functools.partial(mid_kernel, cap),
        grid=(1,),
        in_specs=[const_spec((rows, D)), const_spec((rows, D)), const_spec((2, D)), const_spec((experts, rows))]
        + piece_specs(held, 3 * WIDE, WIDE),
        out_specs=[const_spec((rows, D))] * 2 + [const_spec((rows, 1)), const_spec((experts, cap, D))],
        out_shape=[
            jax.ShapeDtypeStruct((rows, D), f32),
            jax.ShapeDtypeStruct((rows, D), bf16),
            jax.ShapeDtypeStruct((rows, 1), f32),
            jax.ShapeDtypeStruct((experts, cap, D), bf16),
        ],
        compiler_params=pltpu.CompilerParams(vmem_limit_bytes=VMEM),
        cost_estimate=BRIEF,
        name="mid",
    )(attn_low, x_low, gain, slot_rows, *[dense] * WIDE)


def mid_back_kernel(
    cap, block, gx_ref, slot_ref, sdn_ref, resid_ref, inv_ref, gain_ref, c_ref, attn_ref, *refs
):
    wo = refs[:WIDE]
    dres_ref, dattn_ref, dmix_ref, delta_ref, ggain_ref = refs[WIDE:]
    resid, inv, gain = resid_ref[...], inv_ref[...], gain_ref[1:2, :]
    rows = resid.shape[0]
    place = lax.broadcasted_iota(i32, (rows, cap), 1)
    grad = sdn_ref[...]
    for e in range(gx_ref.shape[0]):
        hot = (slot_ref[:, e : e + 1] == place).astype(f32).astype(bf16)
        grad += mm(hot, gx_ref[e])
    ggain_ref[...] = jnp.sum(grad * resid * inv, axis=0, keepdims=True)
    dres = c_ref[...].astype(f32) + norm_back(resid, inv, gain, grad)
    dres_ref[...] = dres
    dattn = dres.astype(bf16)
    dattn_ref[...] = dattn
    dmix = times_back(dattn, wo)
    dmix = dmix.astype(bf16)
    dmix_ref[...] = dmix
    prod = dmix.astype(f32) * attn_ref[...]
    high = prod.astype(bf16)
    rest = (prod - high.astype(f32)).astype(bf16)
    lane = lax.broadcasted_iota(i32, (16, D), 1)
    head = lax.broadcasted_iota(i32, (16, D), 0)
    pick = (lane // HD == head).astype(f32).astype(bf16)
    for b in range(delta_ref.shape[0]):
        at = slice(b * block, (b + 1) * block)
        delta_ref[b] = mm(pick, high[at], NT) + mm(pick, rest[at], NT)


def mid_back(gx_back, slot_cols, s_dn, resid, inv, gain, c_low, attn, dense, held, block):
    rows = resid.shape[0]
    experts, cap, _ = gx_back.shape
    row = const_spec((rows, D))
    return pl.pallas_call(
        functools.partial(mid_back_kernel, cap, block),
        grid=(1,),
        in_specs=[
            const_spec((experts, cap, D)), const_spec((rows, experts)), row, row, const_spec((rows, 1)),
            const_spec((2, D)), row, row,
        ]
        + piece_specs(held, 3 * WIDE, WIDE),
        out_specs=[row, row, row, const_spec((rows // block, 16, block)), const_spec((1, D))],
        out_shape=[
            jax.ShapeDtypeStruct((rows, D), f32),
            jax.ShapeDtypeStruct((rows, D), bf16),
            jax.ShapeDtypeStruct((rows, D), bf16),
            jax.ShapeDtypeStruct((rows // block, 16, block), f32),
            jax.ShapeDtypeStruct((1, D), f32),
        ],
        compiler_params=pltpu.CompilerParams(vmem_limit_bytes=VMEM),
        cost_estimate=BRIEF,
        name="mid_back",
    )(gx_back, slot_cols, s_dn, resid, inv, gain, c_low, attn, *[dense] * WIDE)


def out_kernel(cap, y_ref, slot_ref, chosen_ref, n_ref, last_ref, sout_ref, resid_ref, x_ref, keep_ref, out_ref, sums_ref):
    rows = n_ref.shape[0]
    logits = mm(n_ref[...], last_ref[...].reshape(D, TILE)[:, :LANES])
    lane = lax.broadcasted_iota(i32, logits.shape, 1)
    first, second = chosen_ref[:, 0:1], chosen_ref[:, 1:2]
    gap = jnp.sum(jnp.where(lane == first, logits, 0.0), axis=-1, keepdims=True) - jnp.sum(
        jnp.where(lane == second, logits, 0.0), axis=-1, keepdims=True
    )
    gate_one = 1.0 / (1.0 + jnp.exp(-gap))
    gate_two = 1.0 / (1.0 + jnp.exp(gap))
    place = lax.broadcasted_iota(i32, (rows, cap), 1)
    ffn = sout_ref[...]
    for e in range(y_ref.shape[0]):
        hot = (slot_ref[:, e : e + 1] == place).astype(f32).astype(bf16)
        gate = jnp.where(first == e, gate_one, jnp.where(second == e, gate_two, 0.0))
        ffn += gate * mm(hot, y_ref[e])
    resid, x, keep = resid_ref[...], x_ref[...].astype(f32), keep_ref[...]
    result = resid + ffn
    out_ref[...] = result.astype(bf16)
    for n, a in enumerate((x, resid - x, ffn, result)):
        total = jnp.sum(keep * jnp.sum(a * a, axis=-1, keepdims=True), axis=0, keepdims=True)
        sums_ref[n : n + 1, :] = jnp.broadcast_to(total, (1, LANES))


def finish(y_back, slot_cols, chosen, n_two, dense, held, s_out, resid, x_low, keep):
    rows = resid.shape[0]
    experts, cap, _ = y_back.shape
    row = const_spec((rows, D))
    return pl.pallas_call(
        functools.partial(out_kernel, cap),
        grid=(1,),
        in_specs=[
            const_spec((experts, cap, D)), const_spec((rows, experts)), const_spec((rows, TOPK)), row,
        ]
        + piece_specs(held, LAST, 1)
        + [row, row, row, const_spec((rows, 1))],
        out_specs=[row, const_spec((4, LANES))],
        out_shape=[jax.ShapeDtypeStruct((rows, D), bf16), jax.ShapeDtypeStruct((4, LANES), f32)],
        compiler_params=pltpu.CompilerParams(vmem_limit_bytes=VMEM),
        cost_estimate=BRIEF,
        name="finish",
    )(y_back, slot_cols, chosen, n_two, dense, s_out, resid, x_low, keep)


def tail_kernel(
    shard, n_ctx, experts, place_ref, n_ref, dk_ref, dv_ref, x_ref, dq_ref, o_ref, da_ref, router_ref, second_ref, *refs
):
    wq, wk, wv = refs[:WIDE], refs[WIDE : 2 * WIDE], refs[2 * WIDE : 3 * WIDE]
    low_ref, own_ref, *outs, acc, ggain_ref, last_sc = refs[3 * WIDE :]
    c = pl.program_id(0)
    dk, dv = dk_ref[...], dv_ref[...]
    dn = times_back(dk, wk) + times_back(dv, wv)
    nt = n_ref[...].T
    x = x_ref[...].astype(f32)
    scaled = x * lax.rsqrt(jnp.mean(x * x, axis=-1, keepdims=True) + EPS)
    low_ref[...] = dn.astype(bf16)

    @pl.when(c == 0)
    def _():
        own = times_back(dq_ref[...], wq)
        own_ref[...] = own
        ggain_ref[...] = jnp.sum((own + dn) * scaled, axis=0, keepdims=True)
        acc[0] = mm(nt, dq_ref[...])
        acc[1] = mm(nt, dk)
        acc[2] = mm(nt, dv)
        acc[3] = mm(o_ref[...], da_ref[...], TN)

    @pl.when(c > 0)
    def _():
        ggain_ref[...] += jnp.sum(dn * scaled, axis=0, keepdims=True)
        acc[1] += mm(nt, dk)
        acc[2] += mm(nt, dv)

    @pl.when(c == pl.num_programs(0) - 1)
    def _():
        lane = lax.broadcasted_iota(i32, (D, LANES), 1)
        columns = [jnp.broadcast_to(g[...], (8, D)).T[:, :1] for g in (ggain_ref, second_ref)]
        last = jnp.where(lane == experts, columns[0], router_ref[...])
        last = jnp.where(lane == experts + 1, columns[1], last)
        last_sc[...] = jnp.concatenate([last, jnp.zeros((D, TILE - LANES), f32)], axis=1)
        if shard == D:
            for n in range(4):
                outs[0][0, n * D : (n + 1) * D, :] = acc[n].astype(bf16)
            outs[1][...] = last_sc[...].astype(bf16)
            return
        me, odd = place_ref[0], place_ref[1] > 0
        span = D // n_ctx
        keep_ref, give_ref = outs
        for step in range(n_ctx):
            start = pl.multiple_of((me ^ step) * span, span)
            for n in range(4):
                view = acc[n, pl.ds(start, span), :].reshape(span // shard // 2, 2, shard, D)
                mine = jnp.where(odd, view[:, 1], view[:, 0]).astype(bf16)
                other = jnp.where(odd, view[:, 0], view[:, 1]).astype(bf16)
                for p in range(WIDE):
                    at = slice((n * WIDE + p) * shard, (n * WIDE + p + 1) * shard)
                    cols = slice(p * TILE, (p + 1) * TILE)
                    keep_ref[step, :, at, :] = mine[:, :, cols]
                    give_ref[step, :, at, :] = other[:, :, cols]
            view = last_sc[pl.ds(start, span), :].reshape(span // shard // 2, 2, shard, TILE)
            at = slice(LAST * shard, (LAST + 1) * shard)
            keep_ref[step, :, at, :] = jnp.where(odd, view[:, 1], view[:, 0]).astype(bf16)
            give_ref[step, :, at, :] = jnp.where(odd, view[:, 0], view[:, 1]).astype(bf16)


def tail(place, n_all, dk, dv, x_all, dq, attn_low, d_attn, g_router, g_second, dense, held, n_ctx, experts):
    keys, rows = n_all.shape[0], dq.shape[0]
    groups, shard, _ = held
    step = pl.BlockSpec((rows, D), lambda c, o: (c, 0))
    row = const_spec((rows, D))
    parts = [(n_ctx, groups // 2 // n_ctx, (LAST + 1) * shard, TILE)] * 2
    if groups == 1:
        parts = [(1, 4 * D, D), (D, TILE)]
    return pl.pallas_call(
        functools.partial(tail_kernel, shard, n_ctx, experts),
        grid_spec=pltpu.PrefetchScalarGridSpec(
            num_scalar_prefetch=1,
            grid=(keys // rows,),
            in_specs=[step] * 4
            + [row] * 3
            + [const_spec((D, LANES)), const_spec((1, D))]
            + piece_specs(held, 0, 3 * WIDE),
            out_specs=[pl.BlockSpec((rows, D), lambda c, o: (c ^ o[0], 0)), row]
            + [const_spec(p) for p in parts],
            scratch_shapes=[pltpu.VMEM((4, D, D), f32), pltpu.VMEM((1, D), f32), pltpu.VMEM((D, TILE), f32)],
        ),
        out_shape=[
            jax.ShapeDtypeStruct((keys, D), bf16),
            jax.ShapeDtypeStruct((rows, D), f32),
        ]
        + [jax.ShapeDtypeStruct(p, bf16) for p in parts],
        compiler_params=pltpu.CompilerParams(vmem_limit_bytes=VMEM),
        cost_estimate=BRIEF,
        name="tail",
    )(place, n_all, dk, dv, x_all, dq, attn_low, d_attn, g_router, g_second, *[dense] * (3 * WIDE))


def split_heads(dst, values, first):
    none = jnp.zeros((), bf16)
    for g in range(GRPS):
        part = values[:, g * LANES : (g + 1) * LANES]
        dst[2 * g] = jnp.where(first, part, none)
        dst[2 * g + 1] = jnp.where(first, none, part)


def pair_lanes(h):
    return slice(h // 2 * LANES, (h // 2 + 1) * LANES)


def head_rows(h):
    return slice(h * HD, (h + 1) * HD)


def key_bias(sk_ref, rk_ref, sq_ref, rq_ref):
    sk = sk_ref[...]
    ok = ((sk == 0) | (sk == sq_ref[0])) & (rk_ref[...] <= rq_ref[0])
    return jnp.where(ok, 0.0, NEG)


def attend_kernel(
    flag_ref, q_ref, k_ref, vt_ref, sq_ref, rq_ref, sk_ref, rk_ref,
    o_ref, low_ref, lse_ref, qm_sc, m_sc, l_sc, acc_sc,
):
    i, j = pl.program_id(0), pl.program_id(1)
    count = pl.num_programs(1)

    @pl.when(j == 0)
    def _():
        m_sc[...] = jnp.full(m_sc.shape, FLOOR, f32)
        l_sc[...] = jnp.zeros(l_sc.shape, f32)
        acc_sc[...] = jnp.zeros(acc_sc.shape, f32)
        split_heads(qm_sc, q_ref[...], first_head(q_ref.shape[0]))

    @pl.when(flag_ref[i * count + j] > 0)
    def _():
        bias = key_bias(sk_ref, rk_ref, sq_ref, rq_ref)
        scores = [mm(k_ref[:, pair_lanes(h)], qm_sc[h], NT) + bias for h in range(HEADS)]
        m_old = m_sc[:HEADS]
        tops = [jnp.max(s, axis=0, keepdims=True) for s in scores]
        m_new = jnp.maximum(m_old, jnp.concatenate(tops, axis=0))
        a = jnp.exp(m_old - m_new)
        m_sc[:HEADS] = m_new
        probs = [jnp.exp(s - m_new[h : h + 1]) for h, s in enumerate(scores)]
        sums = [jnp.sum(p, axis=0, keepdims=True) for p in probs]
        l_sc[:HEADS] = l_sc[:HEADS] * a + jnp.concatenate(sums, axis=0)
        for h, p in enumerate(probs):
            at = head_rows(h)
            acc_sc[at] = acc_sc[at] * a[h : h + 1] + mm(vt_ref[0, at], p.astype(bf16))

    @pl.when(j == count - 1)
    def _():
        total = jnp.maximum(l_sc[...], 1e-30)
        lse_ref[0] = m_sc[...] + jnp.log(total)
        inv = 1.0 / total
        for h in range(HEADS):
            at = head_rows(h)
            acc_sc[at] = acc_sc[at] * inv[h : h + 1]
        o = acc_sc[...].T
        o_ref[...] = o
        low_ref[...] = o.astype(bf16)


def attend(flags, q, k, vt, seg_q, rot_q, seg_k, rot_k, block):
    rows, keys = q.shape[0], k.shape[0]
    nq, nk = rows // block, keys // block
    q_spec = pl.BlockSpec((block, D), lambda i, j, f: (i, 0))
    k_spec = pl.BlockSpec((block, D), lambda i, j, f: (j, 0))
    vt_spec = pl.BlockSpec((1, D, block), lambda i, j, f: (j, 0, 0))
    row_spec = pl.BlockSpec((1, 1, block), lambda i, j, f: (i, 0, 0))
    col_spec = pl.BlockSpec((block, 1), lambda i, j, f: (j, 0))
    return pl.pallas_call(
        attend_kernel,
        grid_spec=pltpu.PrefetchScalarGridSpec(
            num_scalar_prefetch=1,
            grid=(nq, nk),
            in_specs=[q_spec, k_spec, vt_spec, row_spec, row_spec, col_spec, col_spec],
            out_specs=[q_spec, q_spec, pl.BlockSpec((1, 16, block), lambda i, j, f: (i, 0, 0))],
            scratch_shapes=[
                pltpu.VMEM((HEADS, block, LANES), bf16),
                pltpu.VMEM((16, block), f32),
                pltpu.VMEM((16, block), f32),
                pltpu.VMEM((D, block), f32),
            ],
        ),
        out_shape=[
            jax.ShapeDtypeStruct((rows, D), f32),
            jax.ShapeDtypeStruct((rows, D), bf16),
            jax.ShapeDtypeStruct((nq, 16, block), f32),
        ],
        compiler_params=pltpu.CompilerParams(vmem_limit_bytes=VMEM),
        cost_estimate=BRIEF,
        name="attend",
    )(flags, q, k, vt, seg_q, rot_q, seg_k, rot_k)


def attend_back_kernel(
    flag_ref, q_ref, do_ref, k_ref, v_ref, lse_ref, delta_ref, sq_ref, rq_ref,
    sk_ref, rk_ref, cosk_ref, sink_ref, cosq_ref, sinq_ref,
    dq_ref, dk_ref, dv_ref, dq_sc, dk_sc, dv_sc, qm_sc, dom_sc,
):
    j, i = pl.program_id(0), pl.program_id(1)
    nk, nq = pl.num_programs(0), pl.num_programs(1)

    @pl.when(i == 0)
    def _():
        dk_sc[...] = jnp.zeros(dk_sc.shape, f32)
        dv_sc[...] = jnp.zeros(dv_sc.shape, f32)

    @pl.when(j == 0)
    def _():
        first = first_head(q_ref.shape[0])
        dq_sc[i] = jnp.zeros(dq_sc.shape[1:], f32)
        split_heads(qm_sc.at[i], q_ref[...], first)
        split_heads(dom_sc.at[i], do_ref[...], first)

    @pl.when(flag_ref[i * nk + j] > 0)
    def _():
        bias = key_bias(sk_ref, rk_ref, sq_ref, rq_ref)
        kt = k_ref[...].T
        heads = range(HEADS)
        scores = [mm(k_ref[:, pair_lanes(h)], qm_sc[i, h], NT) + bias for h in heads]
        dps = [mm(v_ref[:, pair_lanes(h)], dom_sc[i, h], NT) for h in heads]
        probs = [jnp.exp(scores[h] - lse_ref[0, h : h + 1, :]) for h in heads]
        ds = [(probs[h] * (dps[h] - delta_ref[0, h : h + 1, :])).astype(bf16) for h in heads]
        low = [p.astype(bf16) for p in probs]
        for h in range(0, HEADS, 2):
            at = pair_lanes(h)
            dv_sc[:, at] += mm(low[h], dom_sc[i, h]) + mm(low[h + 1], dom_sc[i, h + 1])
            dk_sc[:, at] += mm(ds[h], qm_sc[i, h]) + mm(ds[h + 1], qm_sc[i, h + 1])
        for h in heads:
            at = head_rows(h)
            dq_sc[i, at, :] += mm(kt[at], ds[h])

    @pl.when(i == nq - 1)
    def _():
        dk_ref[...] = turn(dk_sc[...], cosk_ref[...], -sink_ref[...]).astype(bf16)
        dv_ref[...] = dv_sc[...].astype(bf16)

    @pl.when(j == nk - 1)
    def _():
        back = turn(dq_sc[i].T, cosq_ref[...], -sinq_ref[...])
        dq_ref[...] = (back * (1.0 / math.sqrt(HD))).astype(bf16)


def attend_back(flags, q, d_o, k, v, lse, delta, seg_q, rot_q, seg_k, rot_k, cosine, sine, block):
    rows, keys = q.shape[0], k.shape[0]
    nq, nk = rows // block, keys // block
    q_spec = pl.BlockSpec((block, D), lambda j, i, f: (i, 0))
    k_spec = pl.BlockSpec((block, D), lambda j, i, f: (j, 0))
    stat_spec = pl.BlockSpec((1, 16, block), lambda j, i, f: (i, 0, 0))
    row_spec = pl.BlockSpec((1, 1, block), lambda j, i, f: (i, 0, 0))
    col_spec = pl.BlockSpec((block, 1), lambda j, i, f: (j, 0))
    tabk_spec = pl.BlockSpec((block, LANES), lambda j, i, f: (j, 0))
    tabq_spec = pl.BlockSpec((block, LANES), lambda j, i, f: (i, 0))
    return pl.pallas_call(
        attend_back_kernel,
        grid_spec=pltpu.PrefetchScalarGridSpec(
            num_scalar_prefetch=1,
            grid=(nk, nq),
            in_specs=[q_spec, q_spec, k_spec, k_spec, stat_spec, stat_spec, row_spec, row_spec]
            + [col_spec] * 2
            + [tabk_spec] * 2
            + [tabq_spec] * 2,
            out_specs=[
                pl.BlockSpec((block, D), lambda j, i, f: (jnp.where(j == nk - 1, i, 0), 0)),
                k_spec,
                k_spec,
            ],
            scratch_shapes=[
                pltpu.VMEM((nq, D, block), f32),
                pltpu.VMEM((block, D), f32),
                pltpu.VMEM((block, D), f32),
                pltpu.VMEM((nq, HEADS, block, LANES), bf16),
                pltpu.VMEM((nq, HEADS, block, LANES), bf16),
            ],
        ),
        out_shape=[
            jax.ShapeDtypeStruct((rows, D), bf16),
            jax.ShapeDtypeStruct((keys, D), bf16),
            jax.ShapeDtypeStruct((keys, D), bf16),
        ],
        compiler_params=pltpu.CompilerParams(vmem_limit_bytes=VMEM),
        cost_estimate=BRIEF,
        name="attend_back",
    )(flags, q, d_o, k, v, lse, delta, seg_q, rot_q, seg_k, rot_k, cosine, sine, cosine, sine)


def input_kernel(own_ref, dres_ref, x_ref, gain_ref, got_ref, out_ref):
    grad = own_ref[...]
    for n in range(got_ref.shape[0]):
        grad += got_ref[n].astype(f32)
    x = x_ref[...].astype(f32)
    inv = lax.rsqrt(jnp.mean(x * x, axis=-1, keepdims=True) + EPS)
    out_ref[...] = dres_ref[...] + norm_back(x, inv, gain_ref[0:1, :], grad)


def input_back(own, d_resid, x_low, gain, got):
    rows = x_low.shape[0]
    row = const_spec((rows, D))
    return pl.pallas_call(
        input_kernel,
        grid=(1,),
        in_specs=[row, row, row, const_spec((2, D)), const_spec(got.shape)],
        out_specs=row,
        out_shape=jax.ShapeDtypeStruct((rows, D), f32),
        compiler_params=pltpu.CompilerParams(vmem_limit_bytes=VMEM),
        cost_estimate=BRIEF,
        name="input_back",
    )(own, d_resid, x_low, gain, got)


def hidden_back(ha, hb, dh):
    sg = 1.0 / (1.0 + jnp.exp(-ha))
    si = ha * sg
    he = (si * hb).astype(bf16)
    da = (dh * hb * (sg * (1.0 + ha * (1.0 - sg)))).astype(bf16)
    return he, da, (dh * si).astype(bf16)


def shared_kernel(
    fast, odd_ref, x_ref, gy_ref, wg_ref, wu_ref, wd_ref, y_ref, gx_ref, *refs
):
    f = pl.program_id(0)
    xt_sc = refs[-1]

    @pl.when(f == 0)
    def _():
        y_ref[...] = jnp.zeros(y_ref.shape, f32)
        gx_ref[...] = jnp.zeros(gx_ref.shape, f32)
        xt_sc[...] = x_ref[...].T

    wg, wu = wg_ref[...].reshape(D, TILE), wu_ref[...].reshape(D, TILE)
    part = wd_ref.shape[1] // WIDE
    many = wd_ref.shape[0]
    wd = [wd_ref[:, n * part : (n + 1) * part, :].reshape(TILE, TILE) for n in range(WIDE)]
    x, gy = x_ref[...], gy_ref[...]
    cut = [slice(n * TILE, (n + 1) * TILE) for n in range(WIDE)]
    ha, hb = mm(x, wg), mm(x, wu)
    dh = sum(mm(gy[:, cut[n]], wd[n], NT) for n in range(WIDE))
    he, da, db = hidden_back(ha, hb, dh)
    for n in range(WIDE):
        y_ref[:, cut[n]] += mm(he, wd[n])
    gx_ref[...] += mm(da, wg, NT) + mm(db, wu, NT)
    xt = xt_sc[...]
    gate, up = mm(xt, da), mm(xt, db)
    down = mm(he, gy, TN)
    if not fast:
        gg_ref, gu_ref, gd_ref = refs[:3]
        gg_ref[0] = gate.astype(bf16)
        gu_ref[0] = up.astype(bf16)
        for n in range(WIDE):
            gd_ref[:, n * part : (n + 1) * part, :] = down[:, cut[n]].astype(bf16).reshape(many, part, TILE)
        return

    keep_ref, give_ref, up_sc, down_sc, sem = refs[:5]
    pairs, shard = up_sc.shape[2:4]
    odd = odd_ref[0] > 0
    last = pl.num_programs(0) - 1

    def copies(tile):
        out = []
        for n, dst in enumerate((keep_ref, give_ref)):
            for m in range(2):
                rows = pl.ds((m * (last + 1) + tile) * shard, shard)
                out.append(pltpu.make_async_copy(up_sc.at[n, m], dst.at[:, rows, :], sem.at[n, m]))
            where = dst.at[pl.ds(tile * (many // 2), many // 2), pl.ds(2 * (last + 1) * shard, WIDE * part), :]
            out.append(pltpu.make_async_copy(down_sc.at[n], where, sem.at[n, 2]))
        return out

    @pl.when(f > 0)
    def _():
        for copy in copies(f - 1):
            copy.wait()

    for m, grad in enumerate((gate, up)):
        view = grad.reshape(pairs, 2, shard, TILE)
        up_sc[0, m] = jnp.where(odd, view[:, 1], view[:, 0]).astype(bf16)
        up_sc[1, m] = jnp.where(odd, view[:, 0], view[:, 1]).astype(bf16)
    for n in range(WIDE):
        view = down[:, cut[n]].reshape(many // 2, 2, part, TILE)
        at = slice(n * part, (n + 1) * part)
        down_sc[0, :, at, :] = jnp.where(odd, view[:, 1], view[:, 0]).astype(bf16)
        down_sc[1, :, at, :] = jnp.where(odd, view[:, 0], view[:, 1]).astype(bf16)
    for copy in copies(f):
        copy.start()

    @pl.when(f == last)
    def _():
        for copy in copies(f):
            copy.wait()


def shared_unit(odd, x, gy, w_gu, held, w_d, down_shard):
    rows = x.shape[0]
    devices = w_d.shape[0]
    hidden = devices * down_shard
    tiles = hidden // TILE
    groups, part, base = held
    fast = groups > 1
    wide = jax.ShapeDtypeStruct((rows, D), f32)
    many = TILE // down_shard
    piece = lambda first: pl.BlockSpec((groups, part, TILE), lambda f, o: (0, first + f, 0))
    down = pl.BlockSpec((many, WIDE * down_shard, TILE), lambda f, o: (f, 0, 0))
    if fast:
        total = 2 * tiles * part + WIDE * down_shard
        grads = [jax.ShapeDtypeStruct((devices // 2, total, TILE), bf16)] * 2
        specs = [pl.BlockSpec(memory_space=pl.ANY)] * 2
        scratch = [
            pltpu.VMEM((2, 2, devices // 2, part, TILE), bf16),
            pltpu.VMEM((2, many // 2, WIDE * down_shard, TILE), bf16),
            pltpu.SemaphoreType.DMA((2, 3)),
        ]
    else:
        grads = [jax.ShapeDtypeStruct((groups, tiles * part, TILE), bf16)] * 2
        grads.append(jax.ShapeDtypeStruct((devices, WIDE * down_shard, TILE), bf16))
        specs = [piece(0), piece(0), down]
        scratch = []
    row = const_spec((rows, D))
    outs = pl.pallas_call(
        functools.partial(shared_kernel, fast),
        grid_spec=pltpu.PrefetchScalarGridSpec(
            num_scalar_prefetch=1,
            grid=(tiles,),
            in_specs=[row, row, piece(base), piece(base + tiles), down],
            out_specs=[row, row] + specs,
            scratch_shapes=scratch + [pltpu.VMEM((D, rows), bf16)],
        ),
        out_shape=[wide, wide] + grads,
        compiler_params=pltpu.CompilerParams(vmem_limit_bytes=VMEM),
        cost_estimate=BRIEF,
        name="shared_unit",
    )(odd, x, gy, w_gu, w_gu, w_d)
    if fast:
        return outs
    y, gx, g_gate, g_up, g_down = outs
    shard = D // devices
    g_gate, g_up = (
        g.reshape(tiles, devices, shard, TILE).transpose(1, 0, 2, 3).reshape(devices, -1, TILE) for g in (g_gate, g_up)
    )
    return (y, gx) + split_cores(jnp.concatenate([g_gate, g_up, g_down], axis=1))


def expert_kernel(
    chunk, x_ref, c_ref, other_ref, mine_ref, last_ref, wg_ref, wu_ref, wd_ref,
    y_ref, gx_ref, gr_ref, da_ref, db_ref, xt_ref, down_ref, y_sc, gx_sc, gy_sc, gap_sc, gt_sc, he_sc,
):
    f = pl.program_id(0)

    def apart():
        sources, cap = other_ref.shape
        lane = lax.broadcasted_iota(i32, (cap, LANES), 1)
        other = other_ref[...].astype(f32).T.astype(i32)
        parts = [jnp.where(lane == other[:, e : e + 1], 1.0, 0.0) for e in range(sources)]
        return mine_ref[...] - jnp.concatenate(parts, axis=0)

    @pl.when(f == 0)
    def _():
        router = last_ref[...].reshape(D, TILE)[:, :LANES]
        gap = jnp.sum(mm(x_ref[...], router) * apart(), axis=-1, keepdims=True)
        gap_sc[...] = gap
        gate = 1.0 / (1.0 + jnp.exp(-gap))
        gy = (c_ref[...].astype(f32) * gate).astype(bf16)
        gy_sc[...] = gy
        xt_ref[...] = x_ref[...].T
        gt_sc[...] = gy.T
        y_sc[...] = jnp.zeros(y_sc.shape, f32)
        gx_sc[...] = jnp.zeros(gx_sc.shape, f32)

    wg, wu, wd = wg_ref[0, 0], wu_ref[0, 0], wd_ref[0, 0]
    for c in range(x_ref.shape[0] // chunk):
        at = slice(c * chunk, (c + 1) * chunk)
        x, gy = x_ref[at], gy_sc[at]
        he, da, db = hidden_back(mm(x, wg), mm(x, wu), mm(gy, wd))
        he_sc[at] = he
        da_ref[at] = da
        db_ref[at] = db
        y_sc[at] += mm(he, wd, NT)
        gx_sc[at] += mm(da, wg, NT) + mm(db, wu, NT)
    down_ref[0, 0] = mm(gt_sc[...], he_sc[...]).astype(bf16)

    @pl.when(f == pl.num_programs(0) - 1)
    def _():
        y = y_sc[...].astype(bf16)
        y_ref[...] = y
        dgate = jnp.sum(c_ref[...].astype(f32) * y.astype(f32), axis=-1, keepdims=True)
        gap = gap_sc[...]
        slope = dgate / (1.0 + jnp.exp(-gap)) / (1.0 + jnp.exp(gap))
        d_logits = slope * apart()
        high = d_logits.astype(bf16)
        rest = (d_logits - high.astype(f32)).astype(bf16)
        router = last_ref[...].reshape(D, TILE)[:, :LANES]
        gx_ref[...] = (gx_sc[...] + mm(high, router, NT) + mm(rest, router, NT)).astype(bf16)
        gr_ref[...] = mm(xt_ref[...], high) + mm(xt_ref[...], rest)


def expert_unit(x, c, other, mine, dense, held, weights):
    rows = x.shape[0]
    shards, _, _, part = weights.shape
    hidden = shards * part
    per = part // TILE
    specs = [pl.BlockSpec((1, 1, D, TILE), lambda f, w=w: (f // per, w, 0, f % per)) for w in range(3)]
    tile_spec = pl.BlockSpec((rows, TILE), lambda f: (0, f))
    kept = jax.ShapeDtypeStruct((rows, hidden), bf16)
    wide = jax.ShapeDtypeStruct((rows, D), bf16)
    tall = jax.ShapeDtypeStruct((D, rows), bf16)
    row_spec = const_spec((rows, D))
    return pl.pallas_call(
        functools.partial(expert_kernel, rows // 2),
        grid=(hidden // TILE,),
        in_specs=[row_spec, row_spec, const_spec(other.shape), const_spec((1, LANES))]
        + piece_specs(held, LAST, 1)
        + specs,
        out_specs=[row_spec] * 2
        + [const_spec((D, LANES)), tile_spec, tile_spec, const_spec((D, rows))]
        + [pl.BlockSpec((1, 1, D, TILE), lambda f: (f // per, 0, 0, f % per))],
        out_shape=[wide, wide, jax.ShapeDtypeStruct((D, LANES), f32), kept, kept, tall]
        + [jax.ShapeDtypeStruct((shards, 1, D, part), bf16)],
        scratch_shapes=[
            pltpu.VMEM((rows, D), f32),
            pltpu.VMEM((rows, D), f32),
            pltpu.VMEM((rows, D), bf16),
            pltpu.VMEM((rows, 1), f32),
            pltpu.VMEM((D, rows), bf16),
            pltpu.VMEM((rows, TILE), bf16),
        ],
        compiler_params=pltpu.CompilerParams(vmem_limit_bytes=VMEM),
        cost_estimate=BRIEF,
        name="expert_unit",
    )(x, c, other, mine, dense, weights, weights, weights)


def expert_grads_kernel(left_ref, *refs):
    left = left_ref[...]
    for n, ref in enumerate(refs[:-1]):
        refs[-1][0, n] = mm(left, ref[...]).astype(bf16)


def expert_grads(left, rights, shards):
    rows, hidden = rights[0].shape
    part = hidden // shards
    per = part // TILE
    count = len(rights)
    return pl.pallas_call(
        expert_grads_kernel,
        grid=(hidden // TILE,),
        in_specs=[const_spec((D, rows))] + [pl.BlockSpec((rows, TILE), lambda f: (0, f))] * count,
        out_specs=pl.BlockSpec((1, count, D, TILE), lambda f: (f // per, 0, 0, f % per)),
        out_shape=jax.ShapeDtypeStruct((shards, count, D, part), bf16),
        compiler_params=pltpu.CompilerParams(vmem_limit_bytes=VMEM),
        cost_estimate=BRIEF,
        name="expert_grads",
    )(left, *rights)


EVERY = ("ctx", "fsdp")


def swap_fsdp(values):
    return lax.all_to_all(values, "fsdp", split_axis=0, concat_axis=0, tiled=True)


def peer(values, axis, size, step):
    return lax.ppermute(values, axis, [(i, i ^ step) for i in range(size)])


def block_of(array, index):
    return lax.dynamic_index_in_dim(array, index, 0, keepdims=False)


def by_step(array, n_ctx):
    array = array.reshape((n_ctx, array.shape[0] // n_ctx) + array.shape[1:])
    me = lax.axis_index("ctx")
    return [block_of(array, me ^ step) for step in range(n_ctx)]


def meet_core(keep, got):
    parts = [mine.astype(f32) + other.astype(f32) for mine, other in zip(keep, got)]
    return parts[:1] + [p.astype(bf16) for p in parts[1:]]


def meet_ctx(parts, n_ctx):
    return list(parts[:1]) + [peer(parts[step], "ctx", n_ctx, step) for step in range(1, n_ctx)]


def add_up(parts):
    total = sum(p.astype(f32) for p in parts)
    return total, total.astype(bf16)


def meet_far(total, low, n_fsdp):
    me = lax.axis_index("fsdp") // 2
    out = block_of(total, me)
    for step in range(1, n_fsdp // 2):
        out += peer(block_of(low, me ^ step), "fsdp", n_fsdp, 2 * step).astype(f32)
    return out


def meet_far_once(low, n_fsdp):
    groups = [[2 * i + c for i in range(n_fsdp // 2)] for c in range(2)]
    got = lax.all_to_all(low, "fsdp", split_axis=0, concat_axis=0, tiled=True, axis_index_groups=groups)
    return jnp.sum(got.astype(f32), axis=0)


def split_cores(chunks):
    odd = lax.axis_index("fsdp") % 2
    view = chunks.reshape((chunks.shape[0] // 2, 2) + chunks.shape[1:])
    return jnp.where(odd == 0, view[:, 0], view[:, 1]), jnp.where(odd == 0, view[:, 1], view[:, 0])


def norm_back(values, inv, gain, grad):
    scaled = grad * gain
    mean = jnp.mean(scaled * values, axis=-1, keepdims=True)
    return inv * scaled - values * (inv * inv * inv * mean)


def positions(order, order_rows, segment_row, valid_row, block):
    blocks = order_rows
    hot = order[:, None] == jnp.arange(blocks, dtype=i32)[None, :]

    def pick(row):
        return jnp.sum(jnp.where(hot[:, :, None], row.reshape(1, blocks, block), 0), axis=1)

    segment, valid = pick(segment_row), pick(valid_row)
    position = order[:, None] * block + jnp.arange(block, dtype=i32)[None, :]
    bounds = jnp.arange(NCONT + 1, dtype=i32)
    starts = jnp.sum((segment_row[None, :] < bounds[:, None]).astype(i32), axis=1)
    begin = jnp.sum(jnp.where(segment[:, :, None] == bounds, starts, 0), axis=-1)
    rotary = position - begin + jnp.where(segment > 0, starts[1], 0)
    return segment, rotary, valid


def local(
    n_ctx, n_fsdp,
    tokens, cotangent, block_order, segment_ids, valid_mask, routes,
    attention_gain, query_weight, key_weight, value_weight, out_weight,
    feedforward_gain, router, shared_gate, shared_up, shared_down,
    expert_gate, expert_up, expert_down,
):
    devices = n_ctx * n_fsdp
    x_low, c_low = tokens[0], cotangent[0]
    rows = x_low.shape[0]
    group = segment_ids.shape[1]
    blocks = block_order.shape[1]
    block = group // blocks
    own = rows // block
    experts = n_fsdp
    cap = 2 * rows * TOPK // experts
    slots = experts * cap
    my_ctx = lax.axis_index("ctx")
    my_fsdp = lax.axis_index("fsdp")
    shard = query_weight.shape[0]
    down_shard = shared_down.shape[0]
    hidden = shared_gate.shape[1]
    tiles = hidden // TILE
    tie = lax.optimization_barrier

    gains = jnp.stack([attention_gain, feedforward_gain], axis=1)
    squares = (query_weight, key_weight, value_weight, out_weight)
    dense = lax.all_gather(pack_weights(squares, (router, gains)), EVERY, axis=0, tiled=False)

    x_all = jnp.concatenate(
        [x_low] + [peer(x_low, "ctx", n_ctx, step) for step in range(1, n_ctx)], axis=0
    )
    dev = my_ctx ^ jnp.arange(n_ctx, dtype=i32)
    which = (dev[:, None] * own + jnp.arange(own, dtype=i32)[None, :]).reshape(-1)
    order = jnp.sum(
        jnp.where(which[:, None] == jnp.arange(blocks, dtype=i32)[None, :], block_order[0][None, :], 0), axis=1
    )
    seg, rot, val = positions(order, blocks, segment_ids[0], valid_mask[0], block)
    seg_q, rot_q = seg[:own], rot[:own]
    seg_k = jnp.where(val > 0, seg, -1)
    allowed = (
        (seg_k[None, :, None, :] == 0) | (seg_k[None, :, None, :] == seg_q[:, None, :, None])
    ) & (rot[None, :, None, :] <= rot_q[:, None, :, None])
    flags = jnp.any(allowed, axis=(2, 3)).astype(i32).reshape(-1)
    half = HD // 2
    lane = jnp.arange(LANES, dtype=i32)
    frequency = jnp.exp((lane % half).astype(f32) * (-math.log(BASE) / half))
    angles = rot.reshape(-1).astype(f32)[:, None] * frequency[None, :]
    cosine = jnp.cos(angles)
    sine = jnp.sin(angles) * jnp.where(lane % HD < half, -1.0, 1.0)
    seg_rows, rot_rows = seg_q.reshape(own, 1, block), rot_q.reshape(own, 1, block)
    seg_cols, rot_cols = seg_k.reshape(-1, 1), rot.reshape(-1, 1)
    keep = val[:own].reshape(-1, 1).astype(f32)

    chosen = routes[0]
    every = jnp.arange(experts, dtype=i32)
    hot = jnp.any(chosen[:, :, None] == every, axis=1)
    before = (jnp.arange(rows)[:, None] > jnp.arange(rows)[None, :]).astype(bf16)
    rank = mm(before, hot.astype(bf16)).astype(i32)
    slot_cols = jnp.where(hot, rank, -1)
    slot_rows = slot_cols.T
    place = slot_rows[:, None, :] == jnp.arange(cap, dtype=i32)[None, :, None]
    other = jnp.sum(chosen, axis=-1)[None, :] - every[:, None]
    other = jnp.sum(jnp.where(place, other[:, None, :], 0), axis=-1)
    other = swap_fsdp(other)
    c_send = mm(place.astype(bf16).reshape(slots, rows), c_low).astype(bf16).reshape(experts, cap, D)

    early = (dense, x_all, flags, cosine, sine, seg_rows, rot_rows, seg_cols, rot_cols, slot_cols, slot_rows, other, c_send, keep)
    (dense, x_all, flags, cosine, sine, seg_rows, rot_rows, seg_cols, rot_cols, slot_cols, slot_rows, other, c_send, keep) = tie(early)

    mine = jnp.stack([expert_gate[0], expert_up[0], expert_down[0].T])
    mine, dense = tie((mine, dense))
    expert_w = lax.all_gather(mine, "ctx", axis=0, tiled=False)
    c_slots = swap_fsdp(c_send).reshape(slots, D)

    cut = 2 * tiles * shard
    square, held = in_pieces(dense, 0, LAST + 1, shard)

    n_all, q, k, v, vt, gains = project(x_all, experts, square, held, cosine, sine, block, rows, 1)
    attn, attn_low, lse = attend(flags, q, k, vt, seg_rows, rot_rows, seg_cols, rot_cols, block)
    resid, n_two, inv_two, x_send = mid(attn_low, x_low, gains, slot_rows, square, held, cap)
    x_send, n_two, c_slots = tie((x_send, n_two, c_slots))
    x_slots = swap_fsdp(x_send).reshape(slots, D)

    shared_pack = pack_weights((shared_down, shared_gate, shared_up), ())
    shared_pack, n_two = tie((shared_pack, n_two))
    shared_w = lax.all_gather(shared_pack, EVERY, axis=0, tiled=False)
    shared_sq, shared_held = in_pieces(shared_w, WIDE * down_shard, 2 * tiles, shard)

    is_mine = (lane == my_fsdp).astype(f32)[None, :]
    y_slots, gx_slots, grad_router, e_da, e_db, e_xt, e_down = expert_unit(
        x_slots, c_slots, other, is_mine, square, held, expert_w
    )
    gx_slots, n_shared = tie((gx_slots, n_two))
    gx_back = swap_fsdp(gx_slots.reshape(experts, cap, D))
    e_down, e_xt = tie((e_down, e_xt))
    e_down_sums = lax.psum_scatter(e_down, "ctx", scatter_dimension=0, tiled=False).astype(f32)
    e_grads = expert_grads(e_xt, (e_da, e_db), n_ctx)

    e_grads, n_shared = tie((e_grads, n_shared))
    odd = (my_fsdp % 2).reshape(1)
    s_out, s_dn, s_keep, s_give = shared_unit(odd, n_shared, c_low, shared_sq, shared_held, shared_w, down_shard)
    s_give = s_give.reshape((n_ctx, -1) + s_give.shape[1:])
    s_got = jnp.stack([peer(s_give[n], "fsdp", n_fsdp, 1) for n in range(n_ctx)])
    s_parts = (s_keep.reshape(s_got.shape).astype(f32) + s_got.astype(f32)).astype(bf16)
    e_grads, gx_back, s_parts = tie((e_grads, gx_back, s_parts))
    s_low = lax.psum_scatter(s_parts, "ctx", scatter_dimension=0, tiled=False)

    d_resid, d_attn, d_mix, delta, grad_gain_two = mid_back(
        gx_back, slot_cols, s_dn, resid, inv_two, gains, c_low, attn, square, held, block
    )
    d_mix, y_slots, e_grads = tie((d_mix, y_slots, e_grads))
    e_sums = lax.psum_scatter(e_grads, "ctx", scatter_dimension=0, tiled=False)
    y_back = swap_fsdp(y_slots.reshape(experts, cap, D))
    dq, dk, dv = attend_back(
        flags, q, d_mix, k, v, lse, delta, seg_rows, rot_rows, seg_cols, rot_cols, cosine, sine, block
    )
    where = jnp.stack([my_ctx, my_fsdp % 2])
    d_low, d_own, *halves = tail(
        where, n_all, dk, dv, x_all, dq, attn_low, d_attn, grad_router, grad_gain_two, square, held, n_ctx, experts
    )
    if held[0] == 1:
        g_all = halves[0].reshape(4, devices, shard, WIDE, TILE).transpose(1, 0, 3, 2, 4)
        g_all = g_all.reshape(devices, 4 * WIDE * shard, TILE)
        g_all = jnp.concatenate([g_all, halves[1].reshape(devices, shard, TILE)], axis=1)
        g_keep, g_give = (jnp.stack(by_step(h, n_ctx)) for h in split_cores(g_all))
    else:
        g_keep, g_give = halves
    y_back, s_low = tie((y_back, s_low))
    s_grads = meet_far_once(s_low, n_fsdp)
    g_give, e_down_sums = tie((g_give, e_down_sums))
    g_parts = meet_core(g_keep, peer(g_give, "fsdp", n_fsdp, 1))
    y_back, *g_parts = tie((y_back, *g_parts))
    g_parts = meet_ctx(g_parts, n_ctx)

    output, sums = finish(y_back, slot_cols, chosen, n_two, square, held, s_out, resid, x_low, keep)

    e_down_out = e_down_sums[0].T[None]
    d_low, s_grads, output, *g_parts = tie((d_low, s_grads, output, *g_parts))
    g_total, g_low = add_up(g_parts)
    dense_grads = meet_far(g_total, g_low, n_fsdp)
    sums, dense_grads = tie((sums, dense_grads))
    level = [sums] + [peer(sums, "ctx", n_ctx, step) for step in range(1, n_ctx)]
    while len(level) > 1:
        level = [a + b for a, b in zip(level[0::2], level[1::2])]
    group_sums = level[0]
    valid_count = jnp.sum(valid_mask[0]).astype(f32)
    stats = jnp.sqrt(group_sums[:, 0] / (valid_count * D))[None]

    def from_pieces(array, part):
        return array.reshape(-1, part, TILE).transpose(1, 0, 2).reshape(part, -1)

    grad_shared_gate = from_pieces(s_grads[: tiles * shard], shard)
    grad_shared_up = from_pieces(s_grads[tiles * shard : cut], shard)
    grad_shared_down = from_pieces(s_grads[cut:], down_shard)
    span = WIDE * shard
    g_query, g_key, g_value, g_out = (from_pieces(dense_grads[n * span : (n + 1) * span], shard) for n in range(4))
    got = lax.all_to_all(d_low.reshape(n_ctx, rows, D), "ctx", split_axis=0, concat_axis=0, tiled=True)
    input_grad = input_back(d_own, d_resid, x_low, gains, got)[None]
    input_grad, e_sums = tie((input_grad, e_sums))
    e_sums = e_sums.astype(f32)

    last = dense_grads[LAST * shard :]
    g_router, g_gain_one, g_gain_two = last[:, :experts], last[:, experts], last[:, experts + 1]

    return (
        output[None], input_grad, g_gain_one, g_query, g_key, g_value, g_out, g_gain_two, g_router,
        grad_shared_gate, grad_shared_up, grad_shared_down,
        e_sums[0][None], e_sums[1][None], e_down_out, stats,
    )


def solution(mesh):
    sizes = dict(mesh.shape)
    rows3 = P("fsdp", "ctx", None)
    group = P("fsdp", None)
    dense1 = P(("ctx", "fsdp"))
    dense2 = P(("ctx", "fsdp"), None)
    column = P("fsdp", None, "ctx")
    return jax.shard_map(
        functools.partial(local, sizes["ctx"], sizes["fsdp"]),
        mesh=mesh,
        in_specs=(rows3, rows3, group, group, group, rows3)
        + (dense1, dense2, dense2, dense2, dense2, dense1)
        + (dense2,) * 4
        + (column, column, rows3),
        out_specs=(rows3, rows3)
        + (dense1, dense2, dense2, dense2, dense2, dense1)
        + (dense2,) * 4
        + (column, column, rows3, group),
        check_vma=False,
    )
```

```python
import functools
import math

import jax
import jax.numpy as jnp
from jax import lax
from jax.experimental import pallas as pl
from jax.experimental.pallas import tpu as pltpu
from jax.sharding import PartitionSpec as P

D = 768
HEADS = 12
HD = 64
TOPK = 2
NCONT = 4

HIGH = lax.Precision.HIGHEST
EPS = 1e-06
NEG = -1e30
FLOOR = -5e29
BASE = 10000.0
LANES = 128
TILE = 256
GRPS = D // LANES
VMEM = 60 * 1024 * 1024

f32 = jnp.float32
bf16 = jnp.bfloat16
i32 = jnp.int32

NT = (((1,), (1,)), ((), ()))
NN = (((1,), (0,)), ((), ()))
TN = (((0,), (0,)), ((), ()))


def mm(a, b, dims=NN):
    return lax.dot_general(a, b, dims, preferred_element_type=f32)


def low_lanes(rows):
    lane = lax.broadcasted_iota(i32, (rows, LANES), 1)
    return lane % HD < HD // 2


def first_head(rows):
    return lax.broadcasted_iota(i32, (rows, LANES), 1) < HD


def turn(values, cosine, sine):
    low = low_lanes(values.shape[0])
    parts = []
    for g in range(GRPS):
        part = values[:, g * LANES : (g + 1) * LANES]
        other = jnp.where(
            low, pltpu.roll(part, LANES - HD // 2, 1), pltpu.roll(part, HD // 2, 1)
        )
        parts.append(part * cosine + other * sine)
    return jnp.concatenate(parts, axis=1)


def const_spec(shape):
    zeros = (0,) * len(shape)
    return pl.BlockSpec(shape, lambda *_: zeros)


BRIEF = pl.CostEstimate(flops=10**9, transcendentals=0, bytes_accessed=10**6)
WIDE = D // TILE
LAST = 4 * WIDE


def times(rows, pieces, out_dtype=f32):
    parts = [mm(rows, p[...].reshape(D, TILE)) for p in pieces]
    return jnp.concatenate(parts, axis=1).astype(out_dtype)


def times_back(rows, pieces):
    parts = [mm(rows[:, n * TILE : (n + 1) * TILE], p[...].reshape(D, TILE), NT) for n, p in enumerate(pieces)]
    return parts[0] + parts[1] + parts[2]


def piece_specs(held, first, count):
    groups, part, base = held
    first = first + base
    return [pl.BlockSpec((groups, part, TILE), lambda *_, p=p: (0, p, 0)) for p in range(first, first + count)]


def pack_kernel(with_last, *refs):
    out_ref = refs[-1]
    at = 0
    for ref in refs[:-3] if with_last else refs[:-1]:
        rows = ref.shape[0]
        for n in range(ref.shape[1] // TILE):
            out_ref[at : at + rows, :] = ref[:, n * TILE : (n + 1) * TILE]
            at += rows
    if with_last:
        router_ref, gains_ref = refs[-3:-1]
        rows, experts = router_ref.shape
        rest = jnp.zeros((rows, TILE - experts - 2), f32)
        last = [router_ref[...].astype(f32), gains_ref[...].astype(f32), rest]
        out_ref[at : at + rows, :] = jnp.concatenate(last, axis=1).astype(bf16)


def pack_weights(weights, last):
    operands = (*weights, *last)
    if weights[-1].shape[0] % 8:
        flat = [a.reshape(a.shape[0], -1, TILE).transpose(1, 0, 2).reshape(-1, TILE) for a in weights]
        if last:
            both = jnp.concatenate(last, axis=1)
            flat.append(jnp.pad(both, ((0, 0), (0, TILE - both.shape[1]))))
        return jnp.concatenate(flat, axis=0)
    rows = sum(a.shape[0] * (a.shape[1] // TILE) for a in weights) + (last[0].shape[0] if last else 0)
    return pl.pallas_call(
        functools.partial(pack_kernel, bool(last)),
        out_shape=jax.ShapeDtypeStruct((rows, TILE), bf16),
        compiler_params=pltpu.CompilerParams(vmem_limit_bytes=VMEM),
        cost_estimate=BRIEF,
        name="pack",
    )(*operands)


def in_pieces(dense, first, count, shard):
    if shard % 8 == 0:
        return dense, (dense.shape[0], shard, first // shard)
    square = dense[:, first : first + count * shard].reshape(dense.shape[0], count, shard, TILE)
    return square.transpose(1, 0, 2, 3).reshape(1, -1, TILE), (1, D, 0)


def qkv_kernel(own, experts, x_ref, last_ref, *refs):
    wq, wk, wv = refs[:WIDE], refs[WIDE : 2 * WIDE], refs[2 * WIDE : 3 * WIDE]
    cos_ref, sin_ref, n_ref, q_ref, k_ref, v_ref, vt_ref, gain_ref = refs[3 * WIDE :]

    @pl.when(pl.program_id(0) == 0)
    def _():
        last = last_ref[...].reshape(D, TILE)[:, :LANES].astype(f32).T
        gain_ref[...] = last[experts : experts + 2]

    x = x_ref[...].astype(f32)
    inv = lax.rsqrt(jnp.mean(x * x, axis=-1, keepdims=True) + EPS)
    n = (x * inv * gain_ref[0:1, :]).astype(bf16)
    n_ref[...] = n
    cosine = cos_ref[...]
    sine = sin_ref[...]
    k_ref[...] = turn(times(n, wk), cosine, sine).astype(bf16)
    v = times(n, wv, bf16)
    v_ref[...] = v
    block = vt_ref.shape[2]
    for b in range(vt_ref.shape[0]):
        vt_ref[b] = v[b * block : (b + 1) * block].T

    @pl.when(pl.program_id(0) < own)
    def _():
        q = turn(times(n, wq), cosine, sine)
        q_ref[...] = (q * (1.0 / math.sqrt(HD))).astype(bf16)


def project(x_all, experts, dense, held, cosine, sine, block, step, own):
    rows = x_all.shape[0]
    row_spec = pl.BlockSpec((step, D), lambda i: (i, 0))
    tab_spec = pl.BlockSpec((step, LANES), lambda i: (i, 0))
    wide = jax.ShapeDtypeStruct((rows, D), bf16)
    return pl.pallas_call(
        functools.partial(qkv_kernel, own, experts),
        grid=(rows // step,),
        in_specs=[row_spec] + piece_specs(held, LAST, 1) + piece_specs(held, 0, 3 * WIDE) + [tab_spec] * 2,
        out_specs=[
            row_spec,
            pl.BlockSpec((step, D), lambda i: (jnp.minimum(i, own - 1), 0)),
            row_spec,
            row_spec,
            pl.BlockSpec((step // block, D, block), lambda i: (i, 0, 0)),
            const_spec((2, D)),
        ],
        out_shape=[
            wide,
            jax.ShapeDtypeStruct((own * step, D), bf16),
            wide,
            wide,
            jax.ShapeDtypeStruct((rows // block, D, block), bf16),
            jax.ShapeDtypeStruct((2, D), f32),
        ],
        compiler_params=pltpu.CompilerParams(vmem_limit_bytes=VMEM),
        cost_estimate=BRIEF,
        name="qkv",
    )(x_all, *[dense] * (3 * WIDE + 1), cosine, sine)


def mid_kernel(cap, o_ref, x_ref, gain_ref, slot_ref, *refs):
    wo = refs[:WIDE]
    resid_ref, n_ref, inv_ref, send_ref = refs[WIDE:]
    resid = x_ref[...].astype(f32) + times(o_ref[...], wo)
    inv = lax.rsqrt(jnp.mean(resid * resid, axis=-1, keepdims=True) + EPS)
    n = (resid * inv * gain_ref[1:2, :]).astype(bf16)
    resid_ref[...] = resid
    n_ref[...] = n
    inv_ref[...] = inv
    place = lax.broadcasted_iota(i32, (cap, n.shape[0]), 0)
    for e in range(slot_ref.shape[0]):
        hot = (slot_ref[e : e + 1, :] == place).astype(f32).astype(bf16)
        send_ref[e] = mm(hot, n).astype(bf16)


def mid(attn_low, x_low, gain, slot_rows, dense, held, cap):
    rows = x_low.shape[0]
    experts = slot_rows.shape[0]
    return pl.pallas_call(
        functools.partial(mid_kernel, cap),
        grid=(1,),
        in_specs=[const_spec((rows, D)), const_spec((rows, D)), const_spec((2, D)), const_spec((experts, rows))]
        + piece_specs(held, 3 * WIDE, WIDE),
        out_specs=[const_spec((rows, D))] * 2 + [const_spec((rows, 1)), const_spec((experts, cap, D))],
        out_shape=[
            jax.ShapeDtypeStruct((rows, D), f32),
            jax.ShapeDtypeStruct((rows, D), bf16),
            jax.ShapeDtypeStruct((rows, 1), f32),
            jax.ShapeDtypeStruct((experts, cap, D), bf16),
        ],
        compiler_params=pltpu.CompilerParams(vmem_limit_bytes=VMEM),
        cost_estimate=BRIEF,
        name="mid",
    )(attn_low, x_low, gain, slot_rows, *[dense] * WIDE)


def mid_back_kernel(
    cap, block, gx_ref, slot_ref, sdn_ref, resid_ref, inv_ref, gain_ref, c_ref, attn_ref, *refs
):
    wo = refs[:WIDE]
    dres_ref, dattn_ref, dmix_ref, delta_ref, ggain_ref = refs[WIDE:]
    resid, inv, gain = resid_ref[...], inv_ref[...], gain_ref[1:2, :]
    rows = resid.shape[0]
    place = lax.broadcasted_iota(i32, (rows, cap), 1)
    grad = sdn_ref[...]
    for e in range(gx_ref.shape[0]):
        hot = (slot_ref[:, e : e + 1] == place).astype(f32).astype(bf16)
        grad += mm(hot, gx_ref[e])
    ggain_ref[...] = jnp.sum(grad * resid * inv, axis=0, keepdims=True)
    dres = c_ref[...].astype(f32) + norm_back(resid, inv, gain, grad)
    dres_ref[...] = dres
    dattn = dres.astype(bf16)
    dattn_ref[...] = dattn
    dmix = times_back(dattn, wo)
    dmix = dmix.astype(bf16)
    dmix_ref[...] = dmix
    prod = dmix.astype(f32) * attn_ref[...]
    high = prod.astype(bf16)
    rest = (prod - high.astype(f32)).astype(bf16)
    lane = lax.broadcasted_iota(i32, (16, D), 1)
    head = lax.broadcasted_iota(i32, (16, D), 0)
    pick = (lane // HD == head).astype(f32).astype(bf16)
    for b in range(delta_ref.shape[0]):
        at = slice(b * block, (b + 1) * block)
        delta_ref[b] = mm(pick, high[at], NT) + mm(pick, rest[at], NT)


def mid_back(gx_back, slot_cols, s_dn, resid, inv, gain, c_low, attn, dense, held, block):
    rows = resid.shape[0]
    experts, cap, _ = gx_back.shape
    row = const_spec((rows, D))
    return pl.pallas_call(
        functools.partial(mid_back_kernel, cap, block),
        grid=(1,),
        in_specs=[
            const_spec((experts, cap, D)), const_spec((rows, experts)), row, row, const_spec((rows, 1)),
            const_spec((2, D)), row, row,
        ]
        + piece_specs(held, 3 * WIDE, WIDE),
        out_specs=[row, row, row, const_spec((rows // block, 16, block)), const_spec((1, D))],
        out_shape=[
            jax.ShapeDtypeStruct((rows, D), f32),
            jax.ShapeDtypeStruct((rows, D), bf16),
            jax.ShapeDtypeStruct((rows, D), bf16),
            jax.ShapeDtypeStruct((rows // block, 16, block), f32),
            jax.ShapeDtypeStruct((1, D), f32),
        ],
        compiler_params=pltpu.CompilerParams(vmem_limit_bytes=VMEM),
        cost_estimate=BRIEF,
        name="mid_back",
    )(gx_back, slot_cols, s_dn, resid, inv, gain, c_low, attn, *[dense] * WIDE)


def out_kernel(cap, y_ref, slot_ref, chosen_ref, n_ref, last_ref, sout_ref, resid_ref, x_ref, keep_ref, out_ref, sums_ref):
    rows = n_ref.shape[0]
    logits = mm(n_ref[...], last_ref[...].reshape(D, TILE)[:, :LANES])
    lane = lax.broadcasted_iota(i32, logits.shape, 1)
    first, second = chosen_ref[:, 0:1], chosen_ref[:, 1:2]
    gap = jnp.sum(jnp.where(lane == first, logits, 0.0), axis=-1, keepdims=True) - jnp.sum(
        jnp.where(lane == second, logits, 0.0), axis=-1, keepdims=True
    )
    gate_one = 1.0 / (1.0 + jnp.exp(-gap))
    gate_two = 1.0 / (1.0 + jnp.exp(gap))
    place = lax.broadcasted_iota(i32, (rows, cap), 1)
    ffn = sout_ref[...]
    for e in range(y_ref.shape[0]):
        hot = (slot_ref[:, e : e + 1] == place).astype(f32).astype(bf16)
        gate = jnp.where(first == e, gate_one, jnp.where(second == e, gate_two, 0.0))
        ffn += gate * mm(hot, y_ref[e])
    resid, x, keep = resid_ref[...], x_ref[...].astype(f32), keep_ref[...]
    result = resid + ffn
    out_ref[...] = result.astype(bf16)
    for n, a in enumerate((x, resid - x, ffn, result)):
        total = jnp.sum(keep * jnp.sum(a * a, axis=-1, keepdims=True), axis=0, keepdims=True)
        sums_ref[n : n + 1, :] = jnp.broadcast_to(total, (1, LANES))


def finish(y_back, slot_cols, chosen, n_two, dense, held, s_out, resid, x_low, keep):
    rows = resid.shape[0]
    experts, cap, _ = y_back.shape
    row = const_spec((rows, D))
    return pl.pallas_call(
        functools.partial(out_kernel, cap),
        grid=(1,),
        in_specs=[
            const_spec((experts, cap, D)), const_spec((rows, experts)), const_spec((rows, TOPK)), row,
        ]
        + piece_specs(held, LAST, 1)
        + [row, row, row, const_spec((rows, 1))],
        out_specs=[row, const_spec((4, LANES))],
        out_shape=[jax.ShapeDtypeStruct((rows, D), bf16), jax.ShapeDtypeStruct((4, LANES), f32)],
        compiler_params=pltpu.CompilerParams(vmem_limit_bytes=VMEM),
        cost_estimate=BRIEF,
        name="finish",
    )(y_back, slot_cols, chosen, n_two, dense, s_out, resid, x_low, keep)


def tail_kernel(
    shard, n_ctx, experts, place_ref, n_ref, dk_ref, dv_ref, x_ref, dq_ref, o_ref, da_ref, router_ref, second_ref, *refs
):
    wq, wk, wv = refs[:WIDE], refs[WIDE : 2 * WIDE], refs[2 * WIDE : 3 * WIDE]
    low_ref, own_ref, *outs, acc, ggain_ref, last_sc = refs[3 * WIDE :]
    c = pl.program_id(0)
    dk, dv = dk_ref[...], dv_ref[...]
    dn = times_back(dk, wk) + times_back(dv, wv)
    nt = n_ref[...].T
    x = x_ref[...].astype(f32)
    scaled = x * lax.rsqrt(jnp.mean(x * x, axis=-1, keepdims=True) + EPS)
    low_ref[...] = dn.astype(bf16)

    @pl.when(c == 0)
    def _():
        own = times_back(dq_ref[...], wq)
        own_ref[...] = own
        ggain_ref[...] = jnp.sum((own + dn) * scaled, axis=0, keepdims=True)
        acc[0] = mm(nt, dq_ref[...])
        acc[1] = mm(nt, dk)
        acc[2] = mm(nt, dv)
        acc[3] = mm(o_ref[...], da_ref[...], TN)

    @pl.when(c > 0)
    def _():
        ggain_ref[...] += jnp.sum(dn * scaled, axis=0, keepdims=True)
        acc[1] += mm(nt, dk)
        acc[2] += mm(nt, dv)

    @pl.when(c == pl.num_programs(0) - 1)
    def _():
        lane = lax.broadcasted_iota(i32, (D, LANES), 1)
        columns = [jnp.broadcast_to(g[...], (8, D)).T[:, :1] for g in (ggain_ref, second_ref)]
        last = jnp.where(lane == experts, columns[0], router_ref[...])
        last = jnp.where(lane == experts + 1, columns[1], last)
        last_sc[...] = jnp.concatenate([last, jnp.zeros((D, TILE - LANES), f32)], axis=1)
        if shard == D:
            for n in range(4):
                outs[0][0, n * D : (n + 1) * D, :] = acc[n].astype(bf16)
            outs[1][...] = last_sc[...].astype(bf16)
            return
        me, odd = place_ref[0], place_ref[1] > 0
        span = D // n_ctx
        keep_ref, give_ref = outs
        for step in range(n_ctx):
            start = pl.multiple_of((me ^ step) * span, span)
            for n in range(4):
                view = acc[n, pl.ds(start, span), :].reshape(span // shard // 2, 2, shard, D)
                mine = jnp.where(odd, view[:, 1], view[:, 0]).astype(bf16)
                other = jnp.where(odd, view[:, 0], view[:, 1]).astype(bf16)
                for p in range(WIDE):
                    at = slice((n * WIDE + p) * shard, (n * WIDE + p + 1) * shard)
                    cols = slice(p * TILE, (p + 1) * TILE)
                    keep_ref[step, :, at, :] = mine[:, :, cols]
                    give_ref[step, :, at, :] = other[:, :, cols]
            view = last_sc[pl.ds(start, span), :].reshape(span // shard // 2, 2, shard, TILE)
            at = slice(LAST * shard, (LAST + 1) * shard)
            keep_ref[step, :, at, :] = jnp.where(odd, view[:, 1], view[:, 0]).astype(bf16)
            give_ref[step, :, at, :] = jnp.where(odd, view[:, 0], view[:, 1]).astype(bf16)


def tail(place, n_all, dk, dv, x_all, dq, attn_low, d_attn, g_router, g_second, dense, held, n_ctx, experts):
    keys, rows = n_all.shape[0], dq.shape[0]
    groups, shard, _ = held
    step = pl.BlockSpec((rows, D), lambda c, o: (c, 0))
    row = const_spec((rows, D))
    parts = [(n_ctx, groups // 2 // n_ctx, (LAST + 1) * shard, TILE)] * 2
    if groups == 1:
        parts = [(1, 4 * D, D), (D, TILE)]
    return pl.pallas_call(
        functools.partial(tail_kernel, shard, n_ctx, experts),
        grid_spec=pltpu.PrefetchScalarGridSpec(
            num_scalar_prefetch=1,
            grid=(keys // rows,),
            in_specs=[step] * 4
            + [row] * 3
            + [const_spec((D, LANES)), const_spec((1, D))]
            + piece_specs(held, 0, 3 * WIDE),
            out_specs=[pl.BlockSpec((rows, D), lambda c, o: (c ^ o[0], 0)), row]
            + [const_spec(p) for p in parts],
            scratch_shapes=[pltpu.VMEM((4, D, D), f32), pltpu.VMEM((1, D), f32), pltpu.VMEM((D, TILE), f32)],
        ),
        out_shape=[
            jax.ShapeDtypeStruct((keys, D), bf16),
            jax.ShapeDtypeStruct((rows, D), f32),
        ]
        + [jax.ShapeDtypeStruct(p, bf16) for p in parts],
        compiler_params=pltpu.CompilerParams(vmem_limit_bytes=VMEM),
        cost_estimate=BRIEF,
        name="tail",
    )(place, n_all, dk, dv, x_all, dq, attn_low, d_attn, g_router, g_second, *[dense] * (3 * WIDE))


def split_heads(dst, values, first):
    none = jnp.zeros((), bf16)
    for g in range(GRPS):
        part = values[:, g * LANES : (g + 1) * LANES]
        dst[2 * g] = jnp.where(first, part, none)
        dst[2 * g + 1] = jnp.where(first, none, part)


def pair_lanes(h):
    return slice(h // 2 * LANES, (h // 2 + 1) * LANES)


def head_rows(h):
    return slice(h * HD, (h + 1) * HD)


def key_bias(sk_ref, rk_ref, sq_ref, rq_ref):
    sk = sk_ref[...]
    ok = ((sk == 0) | (sk == sq_ref[0])) & (rk_ref[...] <= rq_ref[0])
    return jnp.where(ok, 0.0, NEG)


def attend_kernel(
    flag_ref, q_ref, k_ref, vt_ref, sq_ref, rq_ref, sk_ref, rk_ref,
    o_ref, low_ref, lse_ref, qm_sc, m_sc, l_sc, acc_sc,
):
    i, j = pl.program_id(0), pl.program_id(1)
    count = pl.num_programs(1)

    @pl.when(j == 0)
    def _():
        m_sc[...] = jnp.full(m_sc.shape, FLOOR, f32)
        l_sc[...] = jnp.zeros(l_sc.shape, f32)
        acc_sc[...] = jnp.zeros(acc_sc.shape, f32)
        split_heads(qm_sc, q_ref[...], first_head(q_ref.shape[0]))

    @pl.when(flag_ref[i * count + j] > 0)
    def _():
        bias = key_bias(sk_ref, rk_ref, sq_ref, rq_ref)
        scores = [mm(k_ref[:, pair_lanes(h)], qm_sc[h], NT) + bias for h in range(HEADS)]
        m_old = m_sc[:HEADS]
        tops = [jnp.max(s, axis=0, keepdims=True) for s in scores]
        m_new = jnp.maximum(m_old, jnp.concatenate(tops, axis=0))
        a = jnp.exp(m_old - m_new)
        m_sc[:HEADS] = m_new
        probs = [jnp.exp(s - m_new[h : h + 1]) for h, s in enumerate(scores)]
        sums = [jnp.sum(p, axis=0, keepdims=True) for p in probs]
        l_sc[:HEADS] = l_sc[:HEADS] * a + jnp.concatenate(sums, axis=0)
        for h, p in enumerate(probs):
            at = head_rows(h)
            acc_sc[at] = acc_sc[at] * a[h : h + 1] + mm(vt_ref[0, at], p.astype(bf16))

    @pl.when(j == count - 1)
    def _():
        total = jnp.maximum(l_sc[...], 1e-30)
        lse_ref[0] = m_sc[...] + jnp.log(total)
        inv = 1.0 / total
        for h in range(HEADS):
            at = head_rows(h)
            acc_sc[at] = acc_sc[at] * inv[h : h + 1]
        o = acc_sc[...].T
        o_ref[...] = o
        low_ref[...] = o.astype(bf16)


def attend(flags, q, k, vt, seg_q, rot_q, seg_k, rot_k, block):
    rows, keys = q.shape[0], k.shape[0]
    nq, nk = rows // block, keys // block
    q_spec = pl.BlockSpec((block, D), lambda i, j, f: (i, 0))
    k_spec = pl.BlockSpec((block, D), lambda i, j, f: (j, 0))
    vt_spec = pl.BlockSpec((1, D, block), lambda i, j, f: (j, 0, 0))
    row_spec = pl.BlockSpec((1, 1, block), lambda i, j, f: (i, 0, 0))
    col_spec = pl.BlockSpec((block, 1), lambda i, j, f: (j, 0))
    return pl.pallas_call(
        attend_kernel,
        grid_spec=pltpu.PrefetchScalarGridSpec(
            num_scalar_prefetch=1,
            grid=(nq, nk),
            in_specs=[q_spec, k_spec, vt_spec, row_spec, row_spec, col_spec, col_spec],
            out_specs=[q_spec, q_spec, pl.BlockSpec((1, 16, block), lambda i, j, f: (i, 0, 0))],
            scratch_shapes=[
                pltpu.VMEM((HEADS, block, LANES), bf16),
                pltpu.VMEM((16, block), f32),
                pltpu.VMEM((16, block), f32),
                pltpu.VMEM((D, block), f32),
            ],
        ),
        out_shape=[
            jax.ShapeDtypeStruct((rows, D), f32),
            jax.ShapeDtypeStruct((rows, D), bf16),
            jax.ShapeDtypeStruct((nq, 16, block), f32),
        ],
        compiler_params=pltpu.CompilerParams(vmem_limit_bytes=VMEM),
        cost_estimate=BRIEF,
        name="attend",
    )(flags, q, k, vt, seg_q, rot_q, seg_k, rot_k)


def attend_back_kernel(
    flag_ref, q_ref, do_ref, k_ref, v_ref, lse_ref, delta_ref, sq_ref, rq_ref,
    sk_ref, rk_ref, cosk_ref, sink_ref, cosq_ref, sinq_ref,
    dq_ref, dk_ref, dv_ref, dq_sc, dk_sc, dv_sc, qm_sc, dom_sc,
):
    j, i = pl.program_id(0), pl.program_id(1)
    nk, nq = pl.num_programs(0), pl.num_programs(1)

    @pl.when(i == 0)
    def _():
        dk_sc[...] = jnp.zeros(dk_sc.shape, f32)
        dv_sc[...] = jnp.zeros(dv_sc.shape, f32)

    @pl.when(j == 0)
    def _():
        first = first_head(q_ref.shape[0])
        dq_sc[i] = jnp.zeros(dq_sc.shape[1:], f32)
        split_heads(qm_sc.at[i], q_ref[...], first)
        split_heads(dom_sc.at[i], do_ref[...], first)

    @pl.when(flag_ref[i * nk + j] > 0)
    def _():
        bias = key_bias(sk_ref, rk_ref, sq_ref, rq_ref)
        kt = k_ref[...].T
        heads = range(HEADS)
        scores = [mm(k_ref[:, pair_lanes(h)], qm_sc[i, h], NT) + bias for h in heads]
        dps = [mm(v_ref[:, pair_lanes(h)], dom_sc[i, h], NT) for h in heads]
        probs = [jnp.exp(scores[h] - lse_ref[0, h : h + 1, :]) for h in heads]
        ds = [(probs[h] * (dps[h] - delta_ref[0, h : h + 1, :])).astype(bf16) for h in heads]
        low = [p.astype(bf16) for p in probs]
        for h in range(0, HEADS, 2):
            at = pair_lanes(h)
            dv_sc[:, at] += mm(low[h], dom_sc[i, h]) + mm(low[h + 1], dom_sc[i, h + 1])
            dk_sc[:, at] += mm(ds[h], qm_sc[i, h]) + mm(ds[h + 1], qm_sc[i, h + 1])
        for h in heads:
            at = head_rows(h)
            dq_sc[i, at, :] += mm(kt[at], ds[h])

    @pl.when(i == nq - 1)
    def _():
        dk_ref[...] = turn(dk_sc[...], cosk_ref[...], -sink_ref[...]).astype(bf16)
        dv_ref[...] = dv_sc[...].astype(bf16)

    @pl.when(j == nk - 1)
    def _():
        back = turn(dq_sc[i].T, cosq_ref[...], -sinq_ref[...])
        dq_ref[...] = (back * (1.0 / math.sqrt(HD))).astype(bf16)


def attend_back(flags, q, d_o, k, v, lse, delta, seg_q, rot_q, seg_k, rot_k, cosine, sine, block):
    rows, keys = q.shape[0], k.shape[0]
    nq, nk = rows // block, keys // block
    q_spec = pl.BlockSpec((block, D), lambda j, i, f: (i, 0))
    k_spec = pl.BlockSpec((block, D), lambda j, i, f: (j, 0))
    stat_spec = pl.BlockSpec((1, 16, block), lambda j, i, f: (i, 0, 0))
    row_spec = pl.BlockSpec((1, 1, block), lambda j, i, f: (i, 0, 0))
    col_spec = pl.BlockSpec((block, 1), lambda j, i, f: (j, 0))
    tabk_spec = pl.BlockSpec((block, LANES), lambda j, i, f: (j, 0))
    tabq_spec = pl.BlockSpec((block, LANES), lambda j, i, f: (i, 0))
    return pl.pallas_call(
        attend_back_kernel,
        grid_spec=pltpu.PrefetchScalarGridSpec(
            num_scalar_prefetch=1,
            grid=(nk, nq),
            in_specs=[q_spec, q_spec, k_spec, k_spec, stat_spec, stat_spec, row_spec, row_spec]
            + [col_spec] * 2
            + [tabk_spec] * 2
            + [tabq_spec] * 2,
            out_specs=[
                pl.BlockSpec((block, D), lambda j, i, f: (jnp.where(j == nk - 1, i, 0), 0)),
                k_spec,
                k_spec,
            ],
            scratch_shapes=[
                pltpu.VMEM((nq, D, block), f32),
                pltpu.VMEM((block, D), f32),
                pltpu.VMEM((block, D), f32),
                pltpu.VMEM((nq, HEADS, block, LANES), bf16),
                pltpu.VMEM((nq, HEADS, block, LANES), bf16),
            ],
        ),
        out_shape=[
            jax.ShapeDtypeStruct((rows, D), bf16),
            jax.ShapeDtypeStruct((keys, D), bf16),
            jax.ShapeDtypeStruct((keys, D), bf16),
        ],
        compiler_params=pltpu.CompilerParams(vmem_limit_bytes=VMEM),
        cost_estimate=BRIEF,
        name="attend_back",
    )(flags, q, d_o, k, v, lse, delta, seg_q, rot_q, seg_k, rot_k, cosine, sine, cosine, sine)


def input_kernel(own_ref, dres_ref, x_ref, gain_ref, got_ref, out_ref):
    grad = own_ref[...]
    for n in range(got_ref.shape[0]):
        grad += got_ref[n].astype(f32)
    x = x_ref[...].astype(f32)
    inv = lax.rsqrt(jnp.mean(x * x, axis=-1, keepdims=True) + EPS)
    out_ref[...] = dres_ref[...] + norm_back(x, inv, gain_ref[0:1, :], grad)


def input_back(own, d_resid, x_low, gain, got):
    rows = x_low.shape[0]
    row = const_spec((rows, D))
    return pl.pallas_call(
        input_kernel,
        grid=(1,),
        in_specs=[row, row, row, const_spec((2, D)), const_spec(got.shape)],
        out_specs=row,
        out_shape=jax.ShapeDtypeStruct((rows, D), f32),
        compiler_params=pltpu.CompilerParams(vmem_limit_bytes=VMEM),
        cost_estimate=BRIEF,
        name="input_back",
    )(own, d_resid, x_low, gain, got)


def hidden_back(ha, hb, dh):
    sg = 1.0 / (1.0 + jnp.exp(-ha))
    si = ha * sg
    he = (si * hb).astype(bf16)
    da = (dh * hb * (sg * (1.0 + ha * (1.0 - sg)))).astype(bf16)
    return he, da, (dh * si).astype(bf16)


def shared_kernel(
    fast, odd_ref, x_ref, gy_ref, wg_ref, wu_ref, wd_ref, y_ref, gx_ref, *refs
):
    f = pl.program_id(0)
    xt_sc = refs[-1]

    @pl.when(f == 0)
    def _():
        y_ref[...] = jnp.zeros(y_ref.shape, f32)
        gx_ref[...] = jnp.zeros(gx_ref.shape, f32)
        xt_sc[...] = x_ref[...].T

    wg, wu = wg_ref[...].reshape(D, TILE), wu_ref[...].reshape(D, TILE)
    part = wd_ref.shape[1] // WIDE
    many = wd_ref.shape[0]
    wd = [wd_ref[:, n * part : (n + 1) * part, :].reshape(TILE, TILE) for n in range(WIDE)]
    x, gy = x_ref[...], gy_ref[...]
    cut = [slice(n * TILE, (n + 1) * TILE) for n in range(WIDE)]
    ha, hb = mm(x, wg), mm(x, wu)
    dh = sum(mm(gy[:, cut[n]], wd[n], NT) for n in range(WIDE))
    he, da, db = hidden_back(ha, hb, dh)
    for n in range(WIDE):
        y_ref[:, cut[n]] += mm(he, wd[n])
    gx_ref[...] += mm(da, wg, NT) + mm(db, wu, NT)
    xt = xt_sc[...]
    gate, up = mm(xt, da), mm(xt, db)
    down = mm(he, gy, TN)
    if not fast:
        gg_ref, gu_ref, gd_ref = refs[:3]
        gg_ref[0] = gate.astype(bf16)
        gu_ref[0] = up.astype(bf16)
        for n in range(WIDE):
            gd_ref[:, n * part : (n + 1) * part, :] = down[:, cut[n]].astype(bf16).reshape(many, part, TILE)
        return

    keep_ref, give_ref, up_sc, down_sc, sem = refs[:5]
    pairs, shard = up_sc.shape[2:4]
    odd = odd_ref[0] > 0
    last = pl.num_programs(0) - 1

    def copies(tile):
        out = []
        for n, dst in enumerate((keep_ref, give_ref)):
            for m in range(2):
                rows = pl.ds((m * (last + 1) + tile) * shard, shard)
                out.append(pltpu.make_async_copy(up_sc.at[n, m], dst.at[:, rows, :], sem.at[n, m]))
            where = dst.at[pl.ds(tile * (many // 2), many // 2), pl.ds(2 * (last + 1) * shard, WIDE * part), :]
            out.append(pltpu.make_async_copy(down_sc.at[n], where, sem.at[n, 2]))
        return out

    @pl.when(f > 0)
    def _():
        for copy in copies(f - 1):
            copy.wait()

    for m, grad in enumerate((gate, up)):
        view = grad.reshape(pairs, 2, shard, TILE)
        up_sc[0, m] = jnp.where(odd, view[:, 1], view[:, 0]).astype(bf16)
        up_sc[1, m] = jnp.where(odd, view[:, 0], view[:, 1]).astype(bf16)
    for n in range(WIDE):
        view = down[:, cut[n]].reshape(many // 2, 2, part, TILE)
        at = slice(n * part, (n + 1) * part)
        down_sc[0, :, at, :] = jnp.where(odd, view[:, 1], view[:, 0]).astype(bf16)
        down_sc[1, :, at, :] = jnp.where(odd, view[:, 0], view[:, 1]).astype(bf16)
    for copy in copies(f):
        copy.start()

    @pl.when(f == last)
    def _():
        for copy in copies(f):
            copy.wait()


def shared_unit(odd, x, gy, w_gu, held, w_d, down_shard):
    rows = x.shape[0]
    devices = w_d.shape[0]
    hidden = devices * down_shard
    tiles = hidden // TILE
    groups, part, base = held
    fast = groups > 1
    wide = jax.ShapeDtypeStruct((rows, D), f32)
    many = TILE // down_shard
    piece = lambda first: pl.BlockSpec((groups, part, TILE), lambda f, o: (0, first + f, 0))
    down = pl.BlockSpec((many, WIDE * down_shard, TILE), lambda f, o: (f, 0, 0))
    if fast:
        total = 2 * tiles * part + WIDE * down_shard
        grads = [jax.ShapeDtypeStruct((devices // 2, total, TILE), bf16)] * 2
        specs = [pl.BlockSpec(memory_space=pl.ANY)] * 2
        scratch = [
            pltpu.VMEM((2, 2, devices // 2, part, TILE), bf16),
            pltpu.VMEM((2, many // 2, WIDE * down_shard, TILE), bf16),
            pltpu.SemaphoreType.DMA((2, 3)),
        ]
    else:
        grads = [jax.ShapeDtypeStruct((groups, tiles * part, TILE), bf16)] * 2
        grads.append(jax.ShapeDtypeStruct((devices, WIDE * down_shard, TILE), bf16))
        specs = [piece(0), piece(0), down]
        scratch = []
    row = const_spec((rows, D))
    outs = pl.pallas_call(
        functools.partial(shared_kernel, fast),
        grid_spec=pltpu.PrefetchScalarGridSpec(
            num_scalar_prefetch=1,
            grid=(tiles,),
            in_specs=[row, row, piece(base), piece(base + tiles), down],
            out_specs=[row, row] + specs,
            scratch_shapes=scratch + [pltpu.VMEM((D, rows), bf16)],
        ),
        out_shape=[wide, wide] + grads,
        compiler_params=pltpu.CompilerParams(vmem_limit_bytes=VMEM),
        cost_estimate=BRIEF,
        name="shared_unit",
    )(odd, x, gy, w_gu, w_gu, w_d)
    if fast:
        return outs
    y, gx, g_gate, g_up, g_down = outs
    shard = D // devices
    g_gate, g_up = (
        g.reshape(tiles, devices, shard, TILE).transpose(1, 0, 2, 3).reshape(devices, -1, TILE) for g in (g_gate, g_up)
    )
    return (y, gx) + split_cores(jnp.concatenate([g_gate, g_up, g_down], axis=1))


def expert_kernel(
    chunk, x_ref, c_ref, other_ref, mine_ref, last_ref, wg_ref, wu_ref, wd_ref,
    y_ref, gx_ref, gr_ref, da_ref, db_ref, xt_ref, down_ref, y_sc, gx_sc, gy_sc, gap_sc, gt_sc, he_sc,
):
    f = pl.program_id(0)

    def apart():
        sources, cap = other_ref.shape
        lane = lax.broadcasted_iota(i32, (cap, LANES), 1)
        other = other_ref[...].astype(f32).T.astype(i32)
        parts = [jnp.where(lane == other[:, e : e + 1], 1.0, 0.0) for e in range(sources)]
        return mine_ref[...] - jnp.concatenate(parts, axis=0)

    @pl.when(f == 0)
    def _():
        router = last_ref[...].reshape(D, TILE)[:, :LANES]
        gap = jnp.sum(mm(x_ref[...], router) * apart(), axis=-1, keepdims=True)
        gap_sc[...] = gap
        gate = 1.0 / (1.0 + jnp.exp(-gap))
        gy = (c_ref[...].astype(f32) * gate).astype(bf16)
        gy_sc[...] = gy
        xt_ref[...] = x_ref[...].T
        gt_sc[...] = gy.T
        y_sc[...] = jnp.zeros(y_sc.shape, f32)
        gx_sc[...] = jnp.zeros(gx_sc.shape, f32)

    wg, wu, wd = wg_ref[0, 0], wu_ref[0, 0], wd_ref[0, 0]
    for c in range(x_ref.shape[0] // chunk):
        at = slice(c * chunk, (c + 1) * chunk)
        x, gy = x_ref[at], gy_sc[at]
        he, da, db = hidden_back(mm(x, wg), mm(x, wu), mm(gy, wd))
        he_sc[at] = he
        da_ref[at] = da
        db_ref[at] = db
        y_sc[at] += mm(he, wd, NT)
        gx_sc[at] += mm(da, wg, NT) + mm(db, wu, NT)
    down_ref[0, 0] = mm(gt_sc[...], he_sc[...]).astype(bf16)

    @pl.when(f == pl.num_programs(0) - 1)
    def _():
        y = y_sc[...].astype(bf16)
        y_ref[...] = y
        dgate = jnp.sum(c_ref[...].astype(f32) * y.astype(f32), axis=-1, keepdims=True)
        gap = gap_sc[...]
        slope = dgate / (1.0 + jnp.exp(-gap)) / (1.0 + jnp.exp(gap))
        d_logits = slope * apart()
        high = d_logits.astype(bf16)
        rest = (d_logits - high.astype(f32)).astype(bf16)
        router = last_ref[...].reshape(D, TILE)[:, :LANES]
        gx_ref[...] = (gx_sc[...] + mm(high, router, NT) + mm(rest, router, NT)).astype(bf16)
        gr_ref[...] = mm(xt_ref[...], high) + mm(xt_ref[...], rest)


def expert_unit(x, c, other, mine, dense, held, weights):
    rows = x.shape[0]
    shards, _, _, part = weights.shape
    hidden = shards * part
    per = part // TILE
    specs = [pl.BlockSpec((1, 1, D, TILE), lambda f, w=w: (f // per, w, 0, f % per)) for w in range(3)]
    tile_spec = pl.BlockSpec((rows, TILE), lambda f: (0, f))
    kept = jax.ShapeDtypeStruct((rows, hidden), bf16)
    wide = jax.ShapeDtypeStruct((rows, D), bf16)
    tall = jax.ShapeDtypeStruct((D, rows), bf16)
    row_spec = const_spec((rows, D))
    return pl.pallas_call(
        functools.partial(expert_kernel, rows // 2),
        grid=(hidden // TILE,),
        in_specs=[row_spec, row_spec, const_spec(other.shape), const_spec((1, LANES))]
        + piece_specs(held, LAST, 1)
        + specs,
        out_specs=[row_spec] * 2
        + [const_spec((D, LANES)), tile_spec, tile_spec, const_spec((D, rows))]
        + [pl.BlockSpec((1, 1, D, TILE), lambda f: (f // per, 0, 0, f % per))],
        out_shape=[wide, wide, jax.ShapeDtypeStruct((D, LANES), f32), kept, kept, tall]
        + [jax.ShapeDtypeStruct((shards, 1, D, part), bf16)],
        scratch_shapes=[
            pltpu.VMEM((rows, D), f32),
            pltpu.VMEM((rows, D), f32),
            pltpu.VMEM((rows, D), bf16),
            pltpu.VMEM((rows, 1), f32),
            pltpu.VMEM((D, rows), bf16),
            pltpu.VMEM((rows, TILE), bf16),
        ],
        compiler_params=pltpu.CompilerParams(vmem_limit_bytes=VMEM),
        cost_estimate=BRIEF,
        name="expert_unit",
    )(x, c, other, mine, dense, weights, weights, weights)


def expert_grads_kernel(left_ref, *refs):
    left = left_ref[...]
    for n, ref in enumerate(refs[:-1]):
        refs[-1][0, n] = mm(left, ref[...]).astype(bf16)


def expert_grads(left, rights, shards):
    rows, hidden = rights[0].shape
    part = hidden // shards
    per = part // TILE
    count = len(rights)
    return pl.pallas_call(
        expert_grads_kernel,
        grid=(hidden // TILE,),
        in_specs=[const_spec((D, rows))] + [pl.BlockSpec((rows, TILE), lambda f: (0, f))] * count,
        out_specs=pl.BlockSpec((1, count, D, TILE), lambda f: (f // per, 0, 0, f % per)),
        out_shape=jax.ShapeDtypeStruct((shards, count, D, part), bf16),
        compiler_params=pltpu.CompilerParams(vmem_limit_bytes=VMEM),
        cost_estimate=BRIEF,
        name="expert_grads",
    )(left, *rights)


EVERY = ("ctx", "fsdp")


def swap_fsdp(values):
    return lax.all_to_all(values, "fsdp", split_axis=0, concat_axis=0, tiled=True)


def peer(values, axis, size, step):
    return lax.ppermute(values, axis, [(i, i ^ step) for i in range(size)])


def block_of(array, index):
    return lax.dynamic_index_in_dim(array, index, 0, keepdims=False)


def by_step(array, n_ctx):
    array = array.reshape((n_ctx, array.shape[0] // n_ctx) + array.shape[1:])
    me = lax.axis_index("ctx")
    return [block_of(array, me ^ step) for step in range(n_ctx)]


def meet_core(keep, got):
    parts = [mine.astype(f32) + other.astype(f32) for mine, other in zip(keep, got)]
    return parts[:1] + [p.astype(bf16) for p in parts[1:]]


def meet_ctx(parts, n_ctx):
    return list(parts[:1]) + [peer(parts[step], "ctx", n_ctx, step) for step in range(1, n_ctx)]


def add_up(parts):
    total = sum(p.astype(f32) for p in parts)
    return total, total.astype(bf16)


def meet_far(total, low, n_fsdp):
    me = lax.axis_index("fsdp") // 2
    out = block_of(total, me)
    for step in range(1, n_fsdp // 2):
        out += peer(block_of(low, me ^ step), "fsdp", n_fsdp, 2 * step).astype(f32)
    return out


def meet_far_once(low, n_fsdp):
    groups = [[2 * i + c for i in range(n_fsdp // 2)] for c in range(2)]
    got = lax.all_to_all(low, "fsdp", split_axis=0, concat_axis=0, tiled=True, axis_index_groups=groups)
    return jnp.sum(got.astype(f32), axis=0)


def split_cores(chunks):
    odd = lax.axis_index("fsdp") % 2
    view = chunks.reshape((chunks.shape[0] // 2, 2) + chunks.shape[1:])
    return jnp.where(odd == 0, view[:, 0], view[:, 1]), jnp.where(odd == 0, view[:, 1], view[:, 0])


def norm_back(values, inv, gain, grad):
    scaled = grad * gain
    mean = jnp.mean(scaled * values, axis=-1, keepdims=True)
    return inv * scaled - values * (inv * inv * inv * mean)


def positions(order, order_rows, segment_row, valid_row, block):
    blocks = order_rows
    hot = order[:, None] == jnp.arange(blocks, dtype=i32)[None, :]

    def pick(row):
        return jnp.sum(jnp.where(hot[:, :, None], row.reshape(1, blocks, block), 0), axis=1)

    segment, valid = pick(segment_row), pick(valid_row)
    position = order[:, None] * block + jnp.arange(block, dtype=i32)[None, :]
    bounds = jnp.arange(NCONT + 1, dtype=i32)
    starts = jnp.sum((segment_row[None, :] < bounds[:, None]).astype(i32), axis=1)
    begin = jnp.sum(jnp.where(segment[:, :, None] == bounds, starts, 0), axis=-1)
    rotary = position - begin + jnp.where(segment > 0, starts[1], 0)
    return segment, rotary, valid


def local(
    n_ctx, n_fsdp,
    tokens, cotangent, block_order, segment_ids, valid_mask, routes,
    attention_gain, query_weight, key_weight, value_weight, out_weight,
    feedforward_gain, router, shared_gate, shared_up, shared_down,
    expert_gate, expert_up, expert_down,
):
    devices = n_ctx * n_fsdp
    x_low, c_low = tokens[0], cotangent[0]
    rows = x_low.shape[0]
    group = segment_ids.shape[1]
    blocks = block_order.shape[1]
    block = group // blocks
    own = rows // block
    experts = n_fsdp
    cap = 2 * rows * TOPK // experts
    slots = experts * cap
    my_ctx = lax.axis_index("ctx")
    my_fsdp = lax.axis_index("fsdp")
    shard = query_weight.shape[0]
    down_shard = shared_down.shape[0]
    hidden = shared_gate.shape[1]
    tiles = hidden // TILE
    tie = lax.optimization_barrier

    gains = jnp.stack([attention_gain, feedforward_gain], axis=1)
    squares = (query_weight, key_weight, value_weight, out_weight)
    dense = lax.all_gather(pack_weights(squares, (router, gains)), EVERY, axis=0, tiled=False)

    x_all = jnp.concatenate(
        [x_low] + [peer(x_low, "ctx", n_ctx, step) for step in range(1, n_ctx)], axis=0
    )
    dev = my_ctx ^ jnp.arange(n_ctx, dtype=i32)
    which = (dev[:, None] * own + jnp.arange(own, dtype=i32)[None, :]).reshape(-1)
    order = jnp.sum(
        jnp.where(which[:, None] == jnp.arange(blocks, dtype=i32)[None, :], block_order[0][None, :], 0), axis=1
    )
    seg, rot, val = positions(order, blocks, segment_ids[0], valid_mask[0], block)
    seg_q, rot_q = seg[:own], rot[:own]
    seg_k = jnp.where(val > 0, seg, -1)
    allowed = (
        (seg_k[None, :, None, :] == 0) | (seg_k[None, :, None, :] == seg_q[:, None, :, None])
    ) & (rot[None, :, None, :] <= rot_q[:, None, :, None])
    flags = jnp.any(allowed, axis=(2, 3)).astype(i32).reshape(-1)
    half = HD // 2
    lane = jnp.arange(LANES, dtype=i32)
    frequency = jnp.exp((lane % half).astype(f32) * (-math.log(BASE) / half))
    angles = rot.reshape(-1).astype(f32)[:, None] * frequency[None, :]
    cosine = jnp.cos(angles)
    sine = jnp.sin(angles) * jnp.where(lane % HD < half, -1.0, 1.0)
    seg_rows, rot_rows = seg_q.reshape(own, 1, block), rot_q.reshape(own, 1, block)
    seg_cols, rot_cols = seg_k.reshape(-1, 1), rot.reshape(-1, 1)
    keep = val[:own].reshape(-1, 1).astype(f32)

    chosen = routes[0]
    every = jnp.arange(experts, dtype=i32)
    hot = jnp.any(chosen[:, :, None] == every, axis=1)
    before = (jnp.arange(rows)[:, None] > jnp.arange(rows)[None, :]).astype(bf16)
    rank = mm(before, hot.astype(bf16)).astype(i32)
    slot_cols = jnp.where(hot, rank, -1)
    slot_rows = slot_cols.T
    place = slot_rows[:, None, :] == jnp.arange(cap, dtype=i32)[None, :, None]
    other = jnp.sum(chosen, axis=-1)[None, :] - every[:, None]
    other = jnp.sum(jnp.where(place, other[:, None, :], 0), axis=-1)
    other = swap_fsdp(other)
    c_send = mm(place.astype(bf16).reshape(slots, rows), c_low).astype(bf16).reshape(experts, cap, D)

    early = (dense, x_all, flags, cosine, sine, seg_rows, rot_rows, seg_cols, rot_cols, slot_cols, slot_rows, other, c_send, keep)
    (dense, x_all, flags, cosine, sine, seg_rows, rot_rows, seg_cols, rot_cols, slot_cols, slot_rows, other, c_send, keep) = tie(early)

    mine = jnp.stack([expert_gate[0], expert_up[0], expert_down[0].T])
    mine, dense = tie((mine, dense))
    expert_w = lax.all_gather(mine, "ctx", axis=0, tiled=False)
    c_slots = swap_fsdp(c_send).reshape(slots, D)

    cut = 2 * tiles * shard
    square, held = in_pieces(dense, 0, LAST + 1, shard)

    n_all, q, k, v, vt, gains = project(x_all, experts, square, held, cosine, sine, block, rows, 1)
    attn, attn_low, lse = attend(flags, q, k, vt, seg_rows, rot_rows, seg_cols, rot_cols, block)
    resid, n_two, inv_two, x_send = mid(attn_low, x_low, gains, slot_rows, square, held, cap)
    x_send, n_two, c_slots = tie((x_send, n_two, c_slots))
    x_slots = swap_fsdp(x_send).reshape(slots, D)

    shared_pack = pack_weights((shared_down, shared_gate, shared_up), ())
    shared_pack, n_two = tie((shared_pack, n_two))
    shared_w = lax.all_gather(shared_pack, EVERY, axis=0, tiled=False)
    shared_sq, shared_held = in_pieces(shared_w, WIDE * down_shard, 2 * tiles, shard)

    is_mine = (lane == my_fsdp).astype(f32)[None, :]
    y_slots, gx_slots, grad_router, e_da, e_db, e_xt, e_down = expert_unit(
        x_slots, c_slots, other, is_mine, square, held, expert_w
    )
    gx_slots, n_shared = tie((gx_slots, n_two))
    gx_back = swap_fsdp(gx_slots.reshape(experts, cap, D))
    e_down, e_xt = tie((e_down, e_xt))
    e_down_sums = lax.psum_scatter(e_down, "ctx", scatter_dimension=0, tiled=False)
    e_grads = expert_grads(e_xt, (e_da, e_db), n_ctx)

    e_grads, n_shared = tie((e_grads, n_shared))
    odd = (my_fsdp % 2).reshape(1)
    s_out, s_dn, s_keep, s_give = shared_unit(odd, n_shared, c_low, shared_sq, shared_held, shared_w, down_shard)
    s_give = s_give.reshape((n_ctx, -1) + s_give.shape[1:])
    s_got = jnp.stack([peer(s_give[n], "fsdp", n_fsdp, 1) for n in range(n_ctx)])
    s_parts = (s_keep.reshape(s_got.shape).astype(f32) + s_got.astype(f32)).astype(bf16)
    e_grads, gx_back, s_parts = tie((e_grads, gx_back, s_parts))
    s_low = lax.psum_scatter(s_parts, "ctx", scatter_dimension=0, tiled=False)

    d_resid, d_attn, d_mix, delta, grad_gain_two = mid_back(
        gx_back, slot_cols, s_dn, resid, inv_two, gains, c_low, attn, square, held, block
    )
    d_mix, y_slots, e_grads = tie((d_mix, y_slots, e_grads))
    e_sums = lax.psum_scatter(e_grads, "ctx", scatter_dimension=0, tiled=False)
    y_back = swap_fsdp(y_slots.reshape(experts, cap, D))
    dq, dk, dv = attend_back(
        flags, q, d_mix, k, v, lse, delta, seg_rows, rot_rows, seg_cols, rot_cols, cosine, sine, block
    )
    where = jnp.stack([my_ctx, my_fsdp % 2])
    d_low, d_own, *halves = tail(
        where, n_all, dk, dv, x_all, dq, attn_low, d_attn, grad_router, grad_gain_two, square, held, n_ctx, experts
    )
    if held[0] == 1:
        g_all = halves[0].reshape(4, devices, shard, WIDE, TILE).transpose(1, 0, 3, 2, 4)
        g_all = g_all.reshape(devices, 4 * WIDE * shard, TILE)
        g_all = jnp.concatenate([g_all, halves[1].reshape(devices, shard, TILE)], axis=1)
        g_keep, g_give = (jnp.stack(by_step(h, n_ctx)) for h in split_cores(g_all))
    else:
        g_keep, g_give = halves
    y_back, s_low = tie((y_back, s_low))
    s_grads = meet_far_once(s_low, n_fsdp)
    g_give, e_down_sums = tie((g_give, e_down_sums))
    g_parts = meet_core(g_keep, peer(g_give, "fsdp", n_fsdp, 1))
    y_back, *g_parts = tie((y_back, *g_parts))
    g_parts = meet_ctx(g_parts, n_ctx)

    output, sums = finish(y_back, slot_cols, chosen, n_two, square, held, s_out, resid, x_low, keep)

    e_down_out = e_down_sums[0].astype(f32).T[None]
    d_low, s_grads, output, e_down_out, *g_parts = tie((d_low, s_grads, output, e_down_out, *g_parts))
    g_total, g_low = add_up(g_parts)
    dense_grads = meet_far(g_total, g_low, n_fsdp)
    sums, dense_grads = tie((sums, dense_grads))
    level = [sums] + [peer(sums, "ctx", n_ctx, step) for step in range(1, n_ctx)]
    while len(level) > 1:
        level = [a + b for a, b in zip(level[0::2], level[1::2])]
    group_sums = level[0]
    valid_count = jnp.sum(valid_mask[0]).astype(f32)
    stats = jnp.sqrt(group_sums[:, 0] / (valid_count * D))[None]

    def from_pieces(array, part):
        return array.reshape(-1, part, TILE).transpose(1, 0, 2).reshape(part, -1)

    grad_shared_gate = from_pieces(s_grads[: tiles * shard], shard)
    grad_shared_up = from_pieces(s_grads[tiles * shard : cut], shard)
    grad_shared_down = from_pieces(s_grads[cut:], down_shard)
    span = WIDE * shard
    g_query, g_key, g_value, g_out = (from_pieces(dense_grads[n * span : (n + 1) * span], shard) for n in range(4))
    got = lax.all_to_all(d_low.reshape(n_ctx, rows, D), "ctx", split_axis=0, concat_axis=0, tiled=True)
    input_grad = input_back(d_own, d_resid, x_low, gains, got)[None]
    input_grad, e_sums = tie((input_grad, e_sums))
    e_sums = e_sums.astype(f32)

    last = dense_grads[LAST * shard :]
    g_router, g_gain_one, g_gain_two = last[:, :experts], last[:, experts], last[:, experts + 1]

    return (
        output[None], input_grad, g_gain_one, g_query, g_key, g_value, g_out, g_gain_two, g_router,
        grad_shared_gate, grad_shared_up, grad_shared_down,
        e_sums[0][None], e_sums[1][None], e_down_out, stats,
    )


def solution(mesh):
    sizes = dict(mesh.shape)
    rows3 = P("fsdp", "ctx", None)
    group = P("fsdp", None)
    dense1 = P(("ctx", "fsdp"))
    dense2 = P(("ctx", "fsdp"), None)
    column = P("fsdp", None, "ctx")
    return jax.shard_map(
        functools.partial(local, sizes["ctx"], sizes["fsdp"]),
        mesh=mesh,
        in_specs=(rows3, rows3, group, group, group, rows3)
        + (dense1, dense2, dense2, dense2, dense2, dense1)
        + (dense2,) * 4
        + (column, column, rows3),
        out_specs=(rows3, rows3)
        + (dense1, dense2, dense2, dense2, dense2, dense1)
        + (dense2,) * 4
        + (column, column, rows3, group),
        check_vma=False,
    )
```

```python
import functools
import math

import jax
import jax.numpy as jnp
from jax import lax
from jax.experimental import pallas as pl
from jax.experimental.pallas import tpu as pltpu
from jax.sharding import PartitionSpec as P

D = 768
HEADS = 12
HD = 64
TOPK = 2
NCONT = 4

HIGH = lax.Precision.HIGHEST
EPS = 1e-06
NEG = -1e30
FLOOR = -5e29
BASE = 10000.0
LANES = 128
TILE = 256
GRPS = D // LANES
VMEM = 60 * 1024 * 1024

f32 = jnp.float32
bf16 = jnp.bfloat16
i32 = jnp.int32

NT = (((1,), (1,)), ((), ()))
NN = (((1,), (0,)), ((), ()))
TN = (((0,), (0,)), ((), ()))


def mm(a, b, dims=NN):
    return lax.dot_general(a, b, dims, preferred_element_type=f32)


def low_lanes(rows):
    lane = lax.broadcasted_iota(i32, (rows, LANES), 1)
    return lane % HD < HD // 2


def first_head(rows):
    return lax.broadcasted_iota(i32, (rows, LANES), 1) < HD


def turn(values, cosine, sine):
    low = low_lanes(values.shape[0])
    parts = []
    for g in range(GRPS):
        part = values[:, g * LANES : (g + 1) * LANES]
        other = jnp.where(
            low, pltpu.roll(part, LANES - HD // 2, 1), pltpu.roll(part, HD // 2, 1)
        )
        parts.append(part * cosine + other * sine)
    return jnp.concatenate(parts, axis=1)


def const_spec(shape):
    zeros = (0,) * len(shape)
    return pl.BlockSpec(shape, lambda *_: zeros)


BRIEF = pl.CostEstimate(flops=10**9, transcendentals=0, bytes_accessed=10**6)
WIDE = D // TILE
LAST = 4 * WIDE


def times(rows, pieces, out_dtype=f32):
    parts = [mm(rows, p[...].reshape(D, TILE)) for p in pieces]
    return jnp.concatenate(parts, axis=1).astype(out_dtype)


def times_back(rows, pieces):
    parts = [mm(rows[:, n * TILE : (n + 1) * TILE], p[...].reshape(D, TILE), NT) for n, p in enumerate(pieces)]
    return parts[0] + parts[1] + parts[2]


def piece_specs(held, first, count):
    groups, part, base = held
    first = first + base
    return [pl.BlockSpec((groups, part, TILE), lambda *_, p=p: (0, p, 0)) for p in range(first, first + count)]


def pack_kernel(with_last, *refs):
    out_ref = refs[-1]
    at = 0
    for ref in refs[:-3] if with_last else refs[:-1]:
        rows = ref.shape[0]
        for n in range(ref.shape[1] // TILE):
            out_ref[at : at + rows, :] = ref[:, n * TILE : (n + 1) * TILE]
            at += rows
    if with_last:
        router_ref, gains_ref = refs[-3:-1]
        rows, experts = router_ref.shape
        rest = jnp.zeros((rows, TILE - experts - 2), f32)
        last = [router_ref[...].astype(f32), gains_ref[...].astype(f32), rest]
        out_ref[at : at + rows, :] = jnp.concatenate(last, axis=1).astype(bf16)


def pack_weights(weights, last):
    operands = (*weights, *last)
    if weights[-1].shape[0] % 8:
        flat = [a.reshape(a.shape[0], -1, TILE).transpose(1, 0, 2).reshape(-1, TILE) for a in weights]
        if last:
            both = jnp.concatenate(last, axis=1)
            flat.append(jnp.pad(both, ((0, 0), (0, TILE - both.shape[1]))))
        return jnp.concatenate(flat, axis=0)
    rows = sum(a.shape[0] * (a.shape[1] // TILE) for a in weights) + (last[0].shape[0] if last else 0)
    return pl.pallas_call(
        functools.partial(pack_kernel, bool(last)),
        out_shape=jax.ShapeDtypeStruct((rows, TILE), bf16),
        compiler_params=pltpu.CompilerParams(vmem_limit_bytes=VMEM),
        cost_estimate=BRIEF,
        name="pack",
    )(*operands)


def in_pieces(dense, first, count, shard):
    if shard % 8 == 0:
        return dense, (dense.shape[0], shard, first // shard)
    square = dense[:, first : first + count * shard].reshape(dense.shape[0], count, shard, TILE)
    return square.transpose(1, 0, 2, 3).reshape(1, -1, TILE), (1, D, 0)


def qkv_kernel(own, experts, x_ref, last_ref, *refs):
    wq, wk, wv = refs[:WIDE], refs[WIDE : 2 * WIDE], refs[2 * WIDE : 3 * WIDE]
    cos_ref, sin_ref, n_ref, q_ref, k_ref, v_ref, vt_ref, gain_ref = refs[3 * WIDE :]

    @pl.when(pl.program_id(0) == 0)
    def _():
        last = last_ref[...].reshape(D, TILE)[:, :LANES].astype(f32).T
        gain_ref[...] = last[experts : experts + 2]

    x = x_ref[...].astype(f32)
    inv = lax.rsqrt(jnp.mean(x * x, axis=-1, keepdims=True) + EPS)
    n = (x * inv * gain_ref[0:1, :]).astype(bf16)
    n_ref[...] = n
    cosine = cos_ref[...]
    sine = sin_ref[...]
    k_ref[...] = turn(times(n, wk), cosine, sine).astype(bf16)
    v = times(n, wv, bf16)
    v_ref[...] = v
    block = vt_ref.shape[2]
    for b in range(vt_ref.shape[0]):
        vt_ref[b] = v[b * block : (b + 1) * block].T

    @pl.when(pl.program_id(0) < own)
    def _():
        q = turn(times(n, wq), cosine, sine)
        q_ref[...] = (q * (1.0 / math.sqrt(HD))).astype(bf16)


def project(x_all, experts, dense, held, cosine, sine, block, step, own):
    rows = x_all.shape[0]
    row_spec = pl.BlockSpec((step, D), lambda i: (i, 0))
    tab_spec = pl.BlockSpec((step, LANES), lambda i: (i, 0))
    wide = jax.ShapeDtypeStruct((rows, D), bf16)
    return pl.pallas_call(
        functools.partial(qkv_kernel, own, experts),
        grid=(rows // step,),
        in_specs=[row_spec] + piece_specs(held, LAST, 1) + piece_specs(held, 0, 3 * WIDE) + [tab_spec] * 2,
        out_specs=[
            row_spec,
            pl.BlockSpec((step, D), lambda i: (jnp.minimum(i, own - 1), 0)),
            row_spec,
            row_spec,
            pl.BlockSpec((step // block, D, block), lambda i: (i, 0, 0)),
            const_spec((2, D)),
        ],
        out_shape=[
            wide,
            jax.ShapeDtypeStruct((own * step, D), bf16),
            wide,
            wide,
            jax.ShapeDtypeStruct((rows // block, D, block), bf16),
            jax.ShapeDtypeStruct((2, D), f32),
        ],
        compiler_params=pltpu.CompilerParams(vmem_limit_bytes=VMEM),
        cost_estimate=BRIEF,
        name="qkv",
    )(x_all, *[dense] * (3 * WIDE + 1), cosine, sine)


def mid_kernel(cap, o_ref, x_ref, gain_ref, slot_ref, *refs):
    wo = refs[:WIDE]
    resid_ref, n_ref, inv_ref, send_ref = refs[WIDE:]
    resid = x_ref[...].astype(f32) + times(o_ref[...], wo)
    inv = lax.rsqrt(jnp.mean(resid * resid, axis=-1, keepdims=True) + EPS)
    n = (resid * inv * gain_ref[1:2, :]).astype(bf16)
    resid_ref[...] = resid
    n_ref[...] = n
    inv_ref[...] = inv
    place = lax.broadcasted_iota(i32, (cap, n.shape[0]), 0)
    for e in range(slot_ref.shape[0]):
        hot = (slot_ref[e : e + 1, :] == place).astype(f32).astype(bf16)
        send_ref[e] = mm(hot, n).astype(bf16)


def mid(attn_low, x_low, gain, slot_rows, dense, held, cap):
    rows = x_low.shape[0]
    experts = slot_rows.shape[0]
    return pl.pallas_call(
        functools.partial(mid_kernel, cap),
        grid=(1,),
        in_specs=[const_spec((rows, D)), const_spec((rows, D)), const_spec((2, D)), const_spec((experts, rows))]
        + piece_specs(held, 3 * WIDE, WIDE),
        out_specs=[const_spec((rows, D))] * 2 + [const_spec((rows, 1)), const_spec((experts, cap, D))],
        out_shape=[
            jax.ShapeDtypeStruct((rows, D), f32),
            jax.ShapeDtypeStruct((rows, D), bf16),
            jax.ShapeDtypeStruct((rows, 1), f32),
            jax.ShapeDtypeStruct((experts, cap, D), bf16),
        ],
        compiler_params=pltpu.CompilerParams(vmem_limit_bytes=VMEM),
        cost_estimate=BRIEF,
        name="mid",
    )(attn_low, x_low, gain, slot_rows, *[dense] * WIDE)


def mid_back_kernel(
    cap, block, gx_ref, slot_ref, sdn_ref, resid_ref, inv_ref, gain_ref, c_ref, attn_ref, *refs
):
    wo = refs[:WIDE]
    dres_ref, dattn_ref, dmix_ref, delta_ref, ggain_ref = refs[WIDE:]
    resid, inv, gain = resid_ref[...], inv_ref[...], gain_ref[1:2, :]
    rows = resid.shape[0]
    place = lax.broadcasted_iota(i32, (rows, cap), 1)
    grad = sdn_ref[...]
    for e in range(gx_ref.shape[0]):
        hot = (slot_ref[:, e : e + 1] == place).astype(f32).astype(bf16)
        grad += mm(hot, gx_ref[e])
    ggain_ref[...] = jnp.sum(grad * resid * inv, axis=0, keepdims=True)
    dres = c_ref[...].astype(f32) + norm_back(resid, inv, gain, grad)
    dres_ref[...] = dres
    dattn = dres.astype(bf16)
    dattn_ref[...] = dattn
    dmix = times_back(dattn, wo)
    dmix = dmix.astype(bf16)
    dmix_ref[...] = dmix
    prod = dmix.astype(f32) * attn_ref[...]
    high = prod.astype(bf16)
    rest = (prod - high.astype(f32)).astype(bf16)
    lane = lax.broadcasted_iota(i32, (16, D), 1)
    head = lax.broadcasted_iota(i32, (16, D), 0)
    pick = (lane // HD == head).astype(f32).astype(bf16)
    for b in range(delta_ref.shape[0]):
        at = slice(b * block, (b + 1) * block)
        delta_ref[b] = mm(pick, high[at], NT) + mm(pick, rest[at], NT)


def mid_back(gx_back, slot_cols, s_dn, resid, inv, gain, c_low, attn, dense, held, block):
    rows = resid.shape[0]
    experts, cap, _ = gx_back.shape
    row = const_spec((rows, D))
    return pl.pallas_call(
        functools.partial(mid_back_kernel, cap, block),
        grid=(1,),
        in_specs=[
            const_spec((experts, cap, D)), const_spec((rows, experts)), row, row, const_spec((rows, 1)),
            const_spec((2, D)), row, row,
        ]
        + piece_specs(held, 3 * WIDE, WIDE),
        out_specs=[row, row, row, const_spec((rows // block, 16, block)), const_spec((1, D))],
        out_shape=[
            jax.ShapeDtypeStruct((rows, D), f32),
            jax.ShapeDtypeStruct((rows, D), bf16),
            jax.ShapeDtypeStruct((rows, D), bf16),
            jax.ShapeDtypeStruct((rows // block, 16, block), f32),
            jax.ShapeDtypeStruct((1, D), f32),
        ],
        compiler_params=pltpu.CompilerParams(vmem_limit_bytes=VMEM),
        cost_estimate=BRIEF,
        name="mid_back",
    )(gx_back, slot_cols, s_dn, resid, inv, gain, c_low, attn, *[dense] * WIDE)


def out_kernel(cap, y_ref, slot_ref, chosen_ref, n_ref, last_ref, sout_ref, resid_ref, x_ref, keep_ref, out_ref, sums_ref):
    rows = n_ref.shape[0]
    logits = mm(n_ref[...], last_ref[...].reshape(D, TILE)[:, :LANES])
    lane = lax.broadcasted_iota(i32, logits.shape, 1)
    first, second = chosen_ref[:, 0:1], chosen_ref[:, 1:2]
    gap = jnp.sum(jnp.where(lane == first, logits, 0.0), axis=-1, keepdims=True) - jnp.sum(
        jnp.where(lane == second, logits, 0.0), axis=-1, keepdims=True
    )
    gate_one = 1.0 / (1.0 + jnp.exp(-gap))
    gate_two = 1.0 / (1.0 + jnp.exp(gap))
    place = lax.broadcasted_iota(i32, (rows, cap), 1)
    ffn = sout_ref[...]
    for e in range(y_ref.shape[0]):
        hot = (slot_ref[:, e : e + 1] == place).astype(f32).astype(bf16)
        gate = jnp.where(first == e, gate_one, jnp.where(second == e, gate_two, 0.0))
        ffn += gate * mm(hot, y_ref[e])
    resid, x, keep = resid_ref[...], x_ref[...].astype(f32), keep_ref[...]
    result = resid + ffn
    out_ref[...] = result.astype(bf16)
    for n, a in enumerate((x, resid - x, ffn, result)):
        total = jnp.sum(keep * jnp.sum(a * a, axis=-1, keepdims=True), axis=0, keepdims=True)
        sums_ref[n : n + 1, :] = jnp.broadcast_to(total, (1, LANES))


def finish(y_back, slot_cols, chosen, n_two, dense, held, s_out, resid, x_low, keep):
    rows = resid.shape[0]
    experts, cap, _ = y_back.shape
    row = const_spec((rows, D))
    return pl.pallas_call(
        functools.partial(out_kernel, cap),
        grid=(1,),
        in_specs=[
            const_spec((experts, cap, D)), const_spec((rows, experts)), const_spec((rows, TOPK)), row,
        ]
        + piece_specs(held, LAST, 1)
        + [row, row, row, const_spec((rows, 1))],
        out_specs=[row, const_spec((4, LANES))],
        out_shape=[jax.ShapeDtypeStruct((rows, D), bf16), jax.ShapeDtypeStruct((4, LANES), f32)],
        compiler_params=pltpu.CompilerParams(vmem_limit_bytes=VMEM),
        cost_estimate=BRIEF,
        name="finish",
    )(y_back, slot_cols, chosen, n_two, dense, s_out, resid, x_low, keep)


def tail_kernel(
    shard, n_ctx, experts, place_ref, n_ref, dk_ref, dv_ref, x_ref, dq_ref, o_ref, da_ref, router_ref, second_ref, *refs
):
    wq, wk, wv = refs[:WIDE], refs[WIDE : 2 * WIDE], refs[2 * WIDE : 3 * WIDE]
    low_ref, own_ref, *outs, acc, ggain_ref, last_sc = refs[3 * WIDE :]
    c = pl.program_id(0)
    dk, dv = dk_ref[...], dv_ref[...]
    dn = times_back(dk, wk) + times_back(dv, wv)
    nt = n_ref[...].T
    x = x_ref[...].astype(f32)
    scaled = x * lax.rsqrt(jnp.mean(x * x, axis=-1, keepdims=True) + EPS)
    low_ref[...] = dn.astype(bf16)

    @pl.when(c == 0)
    def _():
        own = times_back(dq_ref[...], wq)
        own_ref[...] = own
        ggain_ref[...] = jnp.sum((own + dn) * scaled, axis=0, keepdims=True)
        acc[0] = mm(nt, dq_ref[...])
        acc[1] = mm(nt, dk)
        acc[2] = mm(nt, dv)
        acc[3] = mm(o_ref[...], da_ref[...], TN)

    @pl.when(c > 0)
    def _():
        ggain_ref[...] += jnp.sum(dn * scaled, axis=0, keepdims=True)
        acc[1] += mm(nt, dk)
        acc[2] += mm(nt, dv)

    @pl.when(c == pl.num_programs(0) - 1)
    def _():
        lane = lax.broadcasted_iota(i32, (D, LANES), 1)
        columns = [jnp.broadcast_to(g[...], (8, D)).T[:, :1] for g in (ggain_ref, second_ref)]
        last = jnp.where(lane == experts, columns[0], router_ref[...])
        last = jnp.where(lane == experts + 1, columns[1], last)
        last_sc[...] = jnp.concatenate([last, jnp.zeros((D, TILE - LANES), f32)], axis=1)
        if shard == D:
            for n in range(4):
                outs[0][0, n * D : (n + 1) * D, :] = acc[n].astype(bf16)
            outs[1][...] = last_sc[...].astype(bf16)
            return
        me, odd = place_ref[0], place_ref[1] > 0
        span = D // n_ctx
        keep_ref, give_ref = outs
        for step in range(n_ctx):
            start = pl.multiple_of((me ^ step) * span, span)
            for n in range(4):
                view = acc[n, pl.ds(start, span), :].reshape(span // shard // 2, 2, shard, D)
                mine = jnp.where(odd, view[:, 1], view[:, 0]).astype(bf16)
                other = jnp.where(odd, view[:, 0], view[:, 1]).astype(bf16)
                for p in range(WIDE):
                    at = slice((n * WIDE + p) * shard, (n * WIDE + p + 1) * shard)
                    cols = slice(p * TILE, (p + 1) * TILE)
                    keep_ref[step, :, at, :] = mine[:, :, cols]
                    give_ref[step, :, at, :] = other[:, :, cols]
            view = last_sc[pl.ds(start, span), :].reshape(span // shard // 2, 2, shard, TILE)
            at = slice(LAST * shard, (LAST + 1) * shard)
            keep_ref[step, :, at, :] = jnp.where(odd, view[:, 1], view[:, 0]).astype(bf16)
            give_ref[step, :, at, :] = jnp.where(odd, view[:, 0], view[:, 1]).astype(bf16)


def tail(place, n_all, dk, dv, x_all, dq, attn_low, d_attn, g_router, g_second, dense, held, n_ctx, experts):
    keys, rows = n_all.shape[0], dq.shape[0]
    groups, shard, _ = held
    step = pl.BlockSpec((rows, D), lambda c, o: (c, 0))
    row = const_spec((rows, D))
    parts = [(n_ctx, groups // 2 // n_ctx, (LAST + 1) * shard, TILE)] * 2
    if groups == 1:
        parts = [(1, 4 * D, D), (D, TILE)]
    return pl.pallas_call(
        functools.partial(tail_kernel, shard, n_ctx, experts),
        grid_spec=pltpu.PrefetchScalarGridSpec(
            num_scalar_prefetch=1,
            grid=(keys // rows,),
            in_specs=[step] * 4
            + [row] * 3
            + [const_spec((D, LANES)), const_spec((1, D))]
            + piece_specs(held, 0, 3 * WIDE),
            out_specs=[pl.BlockSpec((rows, D), lambda c, o: (c ^ o[0], 0)), row]
            + [const_spec(p) for p in parts],
            scratch_shapes=[pltpu.VMEM((4, D, D), f32), pltpu.VMEM((1, D), f32), pltpu.VMEM((D, TILE), f32)],
        ),
        out_shape=[
            jax.ShapeDtypeStruct((keys, D), bf16),
            jax.ShapeDtypeStruct((rows, D), f32),
        ]
        + [jax.ShapeDtypeStruct(p, bf16) for p in parts],
        compiler_params=pltpu.CompilerParams(vmem_limit_bytes=VMEM),
        cost_estimate=BRIEF,
        name="tail",
    )(place, n_all, dk, dv, x_all, dq, attn_low, d_attn, g_router, g_second, *[dense] * (3 * WIDE))


def split_heads(dst, values, first):
    none = jnp.zeros((), bf16)
    for g in range(GRPS):
        part = values[:, g * LANES : (g + 1) * LANES]
        dst[2 * g] = jnp.where(first, part, none)
        dst[2 * g + 1] = jnp.where(first, none, part)


def pair_lanes(h):
    return slice(h // 2 * LANES, (h // 2 + 1) * LANES)


def head_rows(h):
    return slice(h * HD, (h + 1) * HD)


def key_bias(sk_ref, rk_ref, sq_ref, rq_ref):
    sk = sk_ref[...]
    ok = ((sk == 0) | (sk == sq_ref[0])) & (rk_ref[...] <= rq_ref[0])
    return jnp.where(ok, 0.0, NEG)


def attend_kernel(
    flag_ref, q_ref, k_ref, vt_ref, sq_ref, rq_ref, sk_ref, rk_ref,
    o_ref, low_ref, lse_ref, qm_sc, m_sc, l_sc, acc_sc,
):
    i, j = pl.program_id(0), pl.program_id(1)
    count = pl.num_programs(1)

    @pl.when(j == 0)
    def _():
        m_sc[...] = jnp.full(m_sc.shape, FLOOR, f32)
        l_sc[...] = jnp.zeros(l_sc.shape, f32)
        acc_sc[...] = jnp.zeros(acc_sc.shape, f32)
        split_heads(qm_sc, q_ref[...], first_head(q_ref.shape[0]))

    @pl.when(flag_ref[i * count + j] > 0)
    def _():
        bias = key_bias(sk_ref, rk_ref, sq_ref, rq_ref)
        scores = [mm(k_ref[:, pair_lanes(h)], qm_sc[h], NT) + bias for h in range(HEADS)]
        m_old = m_sc[:HEADS]
        tops = [jnp.max(s, axis=0, keepdims=True) for s in scores]
        m_new = jnp.maximum(m_old, jnp.concatenate(tops, axis=0))
        a = jnp.exp(m_old - m_new)
        m_sc[:HEADS] = m_new
        probs = [jnp.exp(s - m_new[h : h + 1]) for h, s in enumerate(scores)]
        sums = [jnp.sum(p, axis=0, keepdims=True) for p in probs]
        l_sc[:HEADS] = l_sc[:HEADS] * a + jnp.concatenate(sums, axis=0)
        for h, p in enumerate(probs):
            at = head_rows(h)
            acc_sc[at] = acc_sc[at] * a[h : h + 1] + mm(vt_ref[0, at], p.astype(bf16))

    @pl.when(j == count - 1)
    def _():
        total = jnp.maximum(l_sc[...], 1e-30)
        lse_ref[0] = m_sc[...] + jnp.log(total)
        inv = 1.0 / total
        for h in range(HEADS):
            at = head_rows(h)
            acc_sc[at] = acc_sc[at] * inv[h : h + 1]
        o = acc_sc[...].T
        o_ref[...] = o
        low_ref[...] = o.astype(bf16)


def attend(flags, q, k, vt, seg_q, rot_q, seg_k, rot_k, block):
    rows, keys = q.shape[0], k.shape[0]
    nq, nk = rows // block, keys // block
    q_spec = pl.BlockSpec((block, D), lambda i, j, f: (i, 0))
    k_spec = pl.BlockSpec((block, D), lambda i, j, f: (j, 0))
    vt_spec = pl.BlockSpec((1, D, block), lambda i, j, f: (j, 0, 0))
    row_spec = pl.BlockSpec((1, 1, block), lambda i, j, f: (i, 0, 0))
    col_spec = pl.BlockSpec((block, 1), lambda i, j, f: (j, 0))
    return pl.pallas_call(
        attend_kernel,
        grid_spec=pltpu.PrefetchScalarGridSpec(
            num_scalar_prefetch=1,
            grid=(nq, nk),
            in_specs=[q_spec, k_spec, vt_spec, row_spec, row_spec, col_spec, col_spec],
            out_specs=[q_spec, q_spec, pl.BlockSpec((1, 16, block), lambda i, j, f: (i, 0, 0))],
            scratch_shapes=[
                pltpu.VMEM((HEADS, block, LANES), bf16),
                pltpu.VMEM((16, block), f32),
                pltpu.VMEM((16, block), f32),
                pltpu.VMEM((D, block), f32),
            ],
        ),
        out_shape=[
            jax.ShapeDtypeStruct((rows, D), f32),
            jax.ShapeDtypeStruct((rows, D), bf16),
            jax.ShapeDtypeStruct((nq, 16, block), f32),
        ],
        compiler_params=pltpu.CompilerParams(vmem_limit_bytes=VMEM),
        cost_estimate=BRIEF,
        name="attend",
    )(flags, q, k, vt, seg_q, rot_q, seg_k, rot_k)


def attend_back_kernel(
    flag_ref, q_ref, do_ref, k_ref, v_ref, lse_ref, delta_ref, sq_ref, rq_ref,
    sk_ref, rk_ref, cosk_ref, sink_ref, cosq_ref, sinq_ref,
    dq_ref, dk_ref, dv_ref, dq_sc, dk_sc, dv_sc, qm_sc, dom_sc,
):
    j, i = pl.program_id(0), pl.program_id(1)
    nk, nq = pl.num_programs(0), pl.num_programs(1)

    @pl.when(i == 0)
    def _():
        dk_sc[...] = jnp.zeros(dk_sc.shape, f32)
        dv_sc[...] = jnp.zeros(dv_sc.shape, f32)

    @pl.when(j == 0)
    def _():
        first = first_head(q_ref.shape[0])
        dq_sc[i] = jnp.zeros(dq_sc.shape[1:], f32)
        split_heads(qm_sc.at[i], q_ref[...], first)
        split_heads(dom_sc.at[i], do_ref[...], first)

    @pl.when(flag_ref[i * nk + j] > 0)
    def _():
        bias = key_bias(sk_ref, rk_ref, sq_ref, rq_ref)
        kt = k_ref[...].T
        heads = range(HEADS)
        scores = [mm(k_ref[:, pair_lanes(h)], qm_sc[i, h], NT) + bias for h in heads]
        dps = [mm(v_ref[:, pair_lanes(h)], dom_sc[i, h], NT) for h in heads]
        probs = [jnp.exp(scores[h] - lse_ref[0, h : h + 1, :]) for h in heads]
        ds = [(probs[h] * (dps[h] - delta_ref[0, h : h + 1, :])).astype(bf16) for h in heads]
        low = [p.astype(bf16) for p in probs]
        for h in range(0, HEADS, 2):
            at = pair_lanes(h)
            dv_sc[:, at] += mm(low[h], dom_sc[i, h]) + mm(low[h + 1], dom_sc[i, h + 1])
            dk_sc[:, at] += mm(ds[h], qm_sc[i, h]) + mm(ds[h + 1], qm_sc[i, h + 1])
        for h in heads:
            at = head_rows(h)
            dq_sc[i, at, :] += mm(kt[at], ds[h])

    @pl.when(i == nq - 1)
    def _():
        dk_ref[...] = turn(dk_sc[...], cosk_ref[...], -sink_ref[...]).astype(bf16)
        dv_ref[...] = dv_sc[...].astype(bf16)

    @pl.when(j == nk - 1)
    def _():
        back = turn(dq_sc[i].T, cosq_ref[...], -sinq_ref[...])
        dq_ref[...] = (back * (1.0 / math.sqrt(HD))).astype(bf16)


def attend_back(flags, q, d_o, k, v, lse, delta, seg_q, rot_q, seg_k, rot_k, cosine, sine, block):
    rows, keys = q.shape[0], k.shape[0]
    nq, nk = rows // block, keys // block
    q_spec = pl.BlockSpec((block, D), lambda j, i, f: (i, 0))
    k_spec = pl.BlockSpec((block, D), lambda j, i, f: (j, 0))
    stat_spec = pl.BlockSpec((1, 16, block), lambda j, i, f: (i, 0, 0))
    row_spec = pl.BlockSpec((1, 1, block), lambda j, i, f: (i, 0, 0))
    col_spec = pl.BlockSpec((block, 1), lambda j, i, f: (j, 0))
    tabk_spec = pl.BlockSpec((block, LANES), lambda j, i, f: (j, 0))
    tabq_spec = pl.BlockSpec((block, LANES), lambda j, i, f: (i, 0))
    return pl.pallas_call(
        attend_back_kernel,
        grid_spec=pltpu.PrefetchScalarGridSpec(
            num_scalar_prefetch=1,
            grid=(nk, nq),
            in_specs=[q_spec, q_spec, k_spec, k_spec, stat_spec, stat_spec, row_spec, row_spec]
            + [col_spec] * 2
            + [tabk_spec] * 2
            + [tabq_spec] * 2,
            out_specs=[
                pl.BlockSpec((block, D), lambda j, i, f: (jnp.where(j == nk - 1, i, 0), 0)),
                k_spec,
                k_spec,
            ],
            scratch_shapes=[
                pltpu.VMEM((nq, D, block), f32),
                pltpu.VMEM((block, D), f32),
                pltpu.VMEM((block, D), f32),
                pltpu.VMEM((nq, HEADS, block, LANES), bf16),
                pltpu.VMEM((nq, HEADS, block, LANES), bf16),
            ],
        ),
        out_shape=[
            jax.ShapeDtypeStruct((rows, D), bf16),
            jax.ShapeDtypeStruct((keys, D), bf16),
            jax.ShapeDtypeStruct((keys, D), bf16),
        ],
        compiler_params=pltpu.CompilerParams(vmem_limit_bytes=VMEM),
        cost_estimate=BRIEF,
        name="attend_back",
    )(flags, q, d_o, k, v, lse, delta, seg_q, rot_q, seg_k, rot_k, cosine, sine, cosine, sine)


def input_kernel(own_ref, dres_ref, x_ref, gain_ref, got_ref, out_ref):
    grad = own_ref[...]
    for n in range(got_ref.shape[0]):
        grad += got_ref[n].astype(f32)
    x = x_ref[...].astype(f32)
    inv = lax.rsqrt(jnp.mean(x * x, axis=-1, keepdims=True) + EPS)
    out_ref[...] = dres_ref[...] + norm_back(x, inv, gain_ref[0:1, :], grad)


def input_back(own, d_resid, x_low, gain, got):
    rows = x_low.shape[0]
    row = const_spec((rows, D))
    return pl.pallas_call(
        input_kernel,
        grid=(1,),
        in_specs=[row, row, row, const_spec((2, D)), const_spec(got.shape)],
        out_specs=row,
        out_shape=jax.ShapeDtypeStruct((rows, D), f32),
        compiler_params=pltpu.CompilerParams(vmem_limit_bytes=VMEM),
        cost_estimate=BRIEF,
        name="input_back",
    )(own, d_resid, x_low, gain, got)


def hidden_back(ha, hb, dh):
    sg = 1.0 / (1.0 + jnp.exp(-ha))
    si = ha * sg
    he = (si * hb).astype(bf16)
    da = (dh * hb * (sg * (1.0 + ha * (1.0 - sg)))).astype(bf16)
    return he, da, (dh * si).astype(bf16)


def shared_kernel(
    fast, odd_ref, x_ref, gy_ref, wg_ref, wu_ref, wd_ref, y_ref, gx_ref, *refs
):
    f = pl.program_id(0)
    xt_sc = refs[-1]

    @pl.when(f == 0)
    def _():
        y_ref[...] = jnp.zeros(y_ref.shape, f32)
        gx_ref[...] = jnp.zeros(gx_ref.shape, f32)
        xt_sc[...] = x_ref[...].T

    wg, wu = wg_ref[...].reshape(D, TILE), wu_ref[...].reshape(D, TILE)
    part = wd_ref.shape[1] // WIDE
    many = wd_ref.shape[0]
    wd = [wd_ref[:, n * part : (n + 1) * part, :].reshape(TILE, TILE) for n in range(WIDE)]
    x, gy = x_ref[...], gy_ref[...]
    cut = [slice(n * TILE, (n + 1) * TILE) for n in range(WIDE)]
    ha, hb = mm(x, wg), mm(x, wu)
    dh = sum(mm(gy[:, cut[n]], wd[n], NT) for n in range(WIDE))
    he, da, db = hidden_back(ha, hb, dh)
    for n in range(WIDE):
        y_ref[:, cut[n]] += mm(he, wd[n])
    gx_ref[...] += mm(da, wg, NT) + mm(db, wu, NT)
    xt = xt_sc[...]
    gate, up = mm(xt, da), mm(xt, db)
    down = mm(he, gy, TN)
    if not fast:
        gg_ref, gu_ref, gd_ref = refs[:3]
        gg_ref[0] = gate.astype(bf16)
        gu_ref[0] = up.astype(bf16)
        for n in range(WIDE):
            gd_ref[:, n * part : (n + 1) * part, :] = down[:, cut[n]].astype(bf16).reshape(many, part, TILE)
        return

    keep_ref, give_ref, up_sc, down_sc, sem = refs[:5]
    pairs, shard = up_sc.shape[2:4]
    odd = odd_ref[0] > 0
    last = pl.num_programs(0) - 1

    def copies(tile):
        out = []
        for n, dst in enumerate((keep_ref, give_ref)):
            for m in range(2):
                rows = pl.ds((m * (last + 1) + tile) * shard, shard)
                out.append(pltpu.make_async_copy(up_sc.at[n, m], dst.at[:, rows, :], sem.at[n, m]))
            where = dst.at[pl.ds(tile * (many // 2), many // 2), pl.ds(2 * (last + 1) * shard, WIDE * part), :]
            out.append(pltpu.make_async_copy(down_sc.at[n], where, sem.at[n, 2]))
        return out

    @pl.when(f > 0)
    def _():
        for copy in copies(f - 1):
            copy.wait()

    for m, grad in enumerate((gate, up)):
        view = grad.reshape(pairs, 2, shard, TILE)
        up_sc[0, m] = jnp.where(odd, view[:, 1], view[:, 0]).astype(bf16)
        up_sc[1, m] = jnp.where(odd, view[:, 0], view[:, 1]).astype(bf16)
    for n in range(WIDE):
        view = down[:, cut[n]].reshape(many // 2, 2, part, TILE)
        at = slice(n * part, (n + 1) * part)
        down_sc[0, :, at, :] = jnp.where(odd, view[:, 1], view[:, 0]).astype(bf16)
        down_sc[1, :, at, :] = jnp.where(odd, view[:, 0], view[:, 1]).astype(bf16)
    for copy in copies(f):
        copy.start()

    @pl.when(f == last)
    def _():
        for copy in copies(f):
            copy.wait()


def shared_unit(odd, x, gy, w_gu, held, w_d, down_shard):
    rows = x.shape[0]
    devices = w_d.shape[0]
    hidden = devices * down_shard
    tiles = hidden // TILE
    groups, part, base = held
    fast = groups > 1
    wide = jax.ShapeDtypeStruct((rows, D), f32)
    many = TILE // down_shard
    piece = lambda first: pl.BlockSpec((groups, part, TILE), lambda f, o: (0, first + f, 0))
    down = pl.BlockSpec((many, WIDE * down_shard, TILE), lambda f, o: (f, 0, 0))
    if fast:
        total = 2 * tiles * part + WIDE * down_shard
        grads = [jax.ShapeDtypeStruct((devices // 2, total, TILE), bf16)] * 2
        specs = [pl.BlockSpec(memory_space=pl.ANY)] * 2
        scratch = [
            pltpu.VMEM((2, 2, devices // 2, part, TILE), bf16),
            pltpu.VMEM((2, many // 2, WIDE * down_shard, TILE), bf16),
            pltpu.SemaphoreType.DMA((2, 3)),
        ]
    else:
        grads = [jax.ShapeDtypeStruct((groups, tiles * part, TILE), bf16)] * 2
        grads.append(jax.ShapeDtypeStruct((devices, WIDE * down_shard, TILE), bf16))
        specs = [piece(0), piece(0), down]
        scratch = []
    row = const_spec((rows, D))
    outs = pl.pallas_call(
        functools.partial(shared_kernel, fast),
        grid_spec=pltpu.PrefetchScalarGridSpec(
            num_scalar_prefetch=1,
            grid=(tiles,),
            in_specs=[row, row, piece(base), piece(base + tiles), down],
            out_specs=[row, row] + specs,
            scratch_shapes=scratch + [pltpu.VMEM((D, rows), bf16)],
        ),
        out_shape=[wide, wide] + grads,
        compiler_params=pltpu.CompilerParams(vmem_limit_bytes=VMEM),
        cost_estimate=BRIEF,
        name="shared_unit",
    )(odd, x, gy, w_gu, w_gu, w_d)
    if fast:
        return outs
    y, gx, g_gate, g_up, g_down = outs
    shard = D // devices
    g_gate, g_up = (
        g.reshape(tiles, devices, shard, TILE).transpose(1, 0, 2, 3).reshape(devices, -1, TILE) for g in (g_gate, g_up)
    )
    return (y, gx) + split_cores(jnp.concatenate([g_gate, g_up, g_down], axis=1))


def expert_kernel(
    chunk, x_ref, c_ref, other_ref, mine_ref, last_ref, wg_ref, wu_ref, wd_ref,
    y_ref, gx_ref, gr_ref, da_ref, db_ref, xt_ref, down_ref, y_sc, gx_sc, gy_sc, gap_sc, gt_sc, he_sc,
):
    f = pl.program_id(0)

    def apart():
        sources, cap = other_ref.shape
        lane = lax.broadcasted_iota(i32, (cap, LANES), 1)
        other = other_ref[...].astype(f32).T.astype(i32)
        parts = [jnp.where(lane == other[:, e : e + 1], 1.0, 0.0) for e in range(sources)]
        return mine_ref[...] - jnp.concatenate(parts, axis=0)

    @pl.when(f == 0)
    def _():
        router = last_ref[...].reshape(D, TILE)[:, :LANES]
        gap = jnp.sum(mm(x_ref[...], router) * apart(), axis=-1, keepdims=True)
        gap_sc[...] = gap
        gate = 1.0 / (1.0 + jnp.exp(-gap))
        gy = (c_ref[...].astype(f32) * gate).astype(bf16)
        gy_sc[...] = gy
        xt_ref[...] = x_ref[...].T
        gt_sc[...] = gy.T
        y_sc[...] = jnp.zeros(y_sc.shape, f32)
        gx_sc[...] = jnp.zeros(gx_sc.shape, f32)

    wg, wu, wd = wg_ref[0, 0], wu_ref[0, 0], wd_ref[0, 0]
    for c in range(x_ref.shape[0] // chunk):
        at = slice(c * chunk, (c + 1) * chunk)
        x, gy = x_ref[at], gy_sc[at]
        he, da, db = hidden_back(mm(x, wg), mm(x, wu), mm(gy, wd))
        he_sc[at] = he
        da_ref[at] = da
        db_ref[at] = db
        y_sc[at] += mm(he, wd, NT)
        gx_sc[at] += mm(da, wg, NT) + mm(db, wu, NT)
    down_ref[0, 0] = mm(gt_sc[...], he_sc[...]).astype(bf16)

    @pl.when(f == pl.num_programs(0) - 1)
    def _():
        y = y_sc[...].astype(bf16)
        y_ref[...] = y
        dgate = jnp.sum(c_ref[...].astype(f32) * y.astype(f32), axis=-1, keepdims=True)
        gap = gap_sc[...]
        slope = dgate / (1.0 + jnp.exp(-gap)) / (1.0 + jnp.exp(gap))
        d_logits = slope * apart()
        high = d_logits.astype(bf16)
        rest = (d_logits - high.astype(f32)).astype(bf16)
        router = last_ref[...].reshape(D, TILE)[:, :LANES]
        gx_ref[...] = (gx_sc[...] + mm(high, router, NT) + mm(rest, router, NT)).astype(bf16)
        gr_ref[...] = mm(xt_ref[...], high) + mm(xt_ref[...], rest)


def expert_unit(x, c, other, mine, dense, held, weights):
    rows = x.shape[0]
    shards, _, _, part = weights.shape
    hidden = shards * part
    per = part // TILE
    specs = [pl.BlockSpec((1, 1, D, TILE), lambda f, w=w: (f // per, w, 0, f % per)) for w in range(3)]
    tile_spec = pl.BlockSpec((rows, TILE), lambda f: (0, f))
    kept = jax.ShapeDtypeStruct((rows, hidden), bf16)
    wide = jax.ShapeDtypeStruct((rows, D), bf16)
    tall = jax.ShapeDtypeStruct((D, rows), bf16)
    row_spec = const_spec((rows, D))
    return pl.pallas_call(
        functools.partial(expert_kernel, rows // 2),
        grid=(hidden // TILE,),
        in_specs=[row_spec, row_spec, const_spec(other.shape), const_spec((1, LANES))]
        + piece_specs(held, LAST, 1)
        + specs,
        out_specs=[row_spec] * 2
        + [const_spec((D, LANES)), tile_spec, tile_spec, const_spec((D, rows))]
        + [pl.BlockSpec((1, 1, D, TILE), lambda f: (f // per, 0, 0, f % per))],
        out_shape=[wide, wide, jax.ShapeDtypeStruct((D, LANES), f32), kept, kept, tall]
        + [jax.ShapeDtypeStruct((shards, 1, D, part), bf16)],
        scratch_shapes=[
            pltpu.VMEM((rows, D), f32),
            pltpu.VMEM((rows, D), f32),
            pltpu.VMEM((rows, D), bf16),
            pltpu.VMEM((rows, 1), f32),
            pltpu.VMEM((D, rows), bf16),
            pltpu.VMEM((rows, TILE), bf16),
        ],
        compiler_params=pltpu.CompilerParams(vmem_limit_bytes=VMEM),
        cost_estimate=BRIEF,
        name="expert_unit",
    )(x, c, other, mine, dense, weights, weights, weights)


def expert_grads_kernel(left_ref, *refs):
    left = left_ref[...]
    for n, ref in enumerate(refs[:-1]):
        refs[-1][0, n] = mm(left, ref[...]).astype(bf16)


def expert_grads(left, rights, shards):
    rows, hidden = rights[0].shape
    part = hidden // shards
    per = part // TILE
    count = len(rights)
    return pl.pallas_call(
        expert_grads_kernel,
        grid=(hidden // TILE,),
        in_specs=[const_spec((D, rows))] + [pl.BlockSpec((rows, TILE), lambda f: (0, f))] * count,
        out_specs=pl.BlockSpec((1, count, D, TILE), lambda f: (f // per, 0, 0, f % per)),
        out_shape=jax.ShapeDtypeStruct((shards, count, D, part), bf16),
        compiler_params=pltpu.CompilerParams(vmem_limit_bytes=VMEM),
        cost_estimate=BRIEF,
        name="expert_grads",
    )(left, *rights)


EVERY = ("ctx", "fsdp")


def swap_fsdp(values):
    return lax.all_to_all(values, "fsdp", split_axis=0, concat_axis=0, tiled=True)


def peer(values, axis, size, step):
    return lax.ppermute(values, axis, [(i, i ^ step) for i in range(size)])


def block_of(array, index):
    return lax.dynamic_index_in_dim(array, index, 0, keepdims=False)


def by_step(array, n_ctx):
    array = array.reshape((n_ctx, array.shape[0] // n_ctx) + array.shape[1:])
    me = lax.axis_index("ctx")
    return [block_of(array, me ^ step) for step in range(n_ctx)]


def meet_core(keep, got):
    parts = [mine.astype(f32) + other.astype(f32) for mine, other in zip(keep, got)]
    return parts[:1] + [p.astype(bf16) for p in parts[1:]]


def meet_ctx(parts, n_ctx):
    return list(parts[:1]) + [peer(parts[step], "ctx", n_ctx, step) for step in range(1, n_ctx)]


def add_up(parts):
    total = sum(p.astype(f32) for p in parts)
    return total, total.astype(bf16)


def meet_far(total, low, n_fsdp):
    me = lax.axis_index("fsdp") // 2
    out = block_of(total, me)
    for step in range(1, n_fsdp // 2):
        out += peer(block_of(low, me ^ step), "fsdp", n_fsdp, 2 * step).astype(f32)
    return out


def meet_far_once(low, n_fsdp):
    groups = [[2 * i + c for i in range(n_fsdp // 2)] for c in range(2)]
    got = lax.all_to_all(low, "fsdp", split_axis=0, concat_axis=0, tiled=True, axis_index_groups=groups)
    return jnp.sum(got.astype(f32), axis=0)


def split_cores(chunks):
    odd = lax.axis_index("fsdp") % 2
    view = chunks.reshape((chunks.shape[0] // 2, 2) + chunks.shape[1:])
    return jnp.where(odd == 0, view[:, 0], view[:, 1]), jnp.where(odd == 0, view[:, 1], view[:, 0])


def norm_back(values, inv, gain, grad):
    scaled = grad * gain
    mean = jnp.mean(scaled * values, axis=-1, keepdims=True)
    return inv * scaled - values * (inv * inv * inv * mean)


def positions(order, order_rows, segment_row, valid_row, block):
    blocks = order_rows
    hot = order[:, None] == jnp.arange(blocks, dtype=i32)[None, :]

    def pick(row):
        return jnp.sum(jnp.where(hot[:, :, None], row.reshape(1, blocks, block), 0), axis=1)

    segment, valid = pick(segment_row), pick(valid_row)
    position = order[:, None] * block + jnp.arange(block, dtype=i32)[None, :]
    bounds = jnp.arange(NCONT + 1, dtype=i32)
    starts = jnp.sum((segment_row[None, :] < bounds[:, None]).astype(i32), axis=1)
    begin = jnp.sum(jnp.where(segment[:, :, None] == bounds, starts, 0), axis=-1)
    rotary = position - begin + jnp.where(segment > 0, starts[1], 0)
    return segment, rotary, valid


def local(
    n_ctx, n_fsdp,
    tokens, cotangent, block_order, segment_ids, valid_mask, routes,
    attention_gain, query_weight, key_weight, value_weight, out_weight,
    feedforward_gain, router, shared_gate, shared_up, shared_down,
    expert_gate, expert_up, expert_down,
):
    devices = n_ctx * n_fsdp
    x_low, c_low = tokens[0], cotangent[0]
    rows = x_low.shape[0]
    group = segment_ids.shape[1]
    blocks = block_order.shape[1]
    block = group // blocks
    own = rows // block
    experts = n_fsdp
    cap = 2 * rows * TOPK // experts
    slots = experts * cap
    my_ctx = lax.axis_index("ctx")
    my_fsdp = lax.axis_index("fsdp")
    shard = query_weight.shape[0]
    down_shard = shared_down.shape[0]
    hidden = shared_gate.shape[1]
    tiles = hidden // TILE
    tie = lax.optimization_barrier

    gains = jnp.stack([attention_gain, feedforward_gain], axis=1)
    squares = (query_weight, key_weight, value_weight, out_weight)
    dense = lax.all_gather(pack_weights(squares, (router, gains)), EVERY, axis=0, tiled=False)

    x_all = jnp.concatenate(
        [x_low] + [peer(x_low, "ctx", n_ctx, step) for step in range(1, n_ctx)], axis=0
    )
    dev = my_ctx ^ jnp.arange(n_ctx, dtype=i32)
    which = (dev[:, None] * own + jnp.arange(own, dtype=i32)[None, :]).reshape(-1)
    order = jnp.sum(
        jnp.where(which[:, None] == jnp.arange(blocks, dtype=i32)[None, :], block_order[0][None, :], 0), axis=1
    )
    seg, rot, val = positions(order, blocks, segment_ids[0], valid_mask[0], block)
    seg_q, rot_q = seg[:own], rot[:own]
    seg_k = jnp.where(val > 0, seg, -1)
    allowed = (
        (seg_k[None, :, None, :] == 0) | (seg_k[None, :, None, :] == seg_q[:, None, :, None])
    ) & (rot[None, :, None, :] <= rot_q[:, None, :, None])
    flags = jnp.any(allowed, axis=(2, 3)).astype(i32).reshape(-1)
    half = HD // 2
    lane = jnp.arange(LANES, dtype=i32)
    frequency = jnp.exp((lane % half).astype(f32) * (-math.log(BASE) / half))
    angles = rot.reshape(-1).astype(f32)[:, None] * frequency[None, :]
    cosine = jnp.cos(angles)
    sine = jnp.sin(angles) * jnp.where(lane % HD < half, -1.0, 1.0)
    seg_rows, rot_rows = seg_q.reshape(own, 1, block), rot_q.reshape(own, 1, block)
    seg_cols, rot_cols = seg_k.reshape(-1, 1), rot.reshape(-1, 1)
    keep = val[:own].reshape(-1, 1).astype(f32)

    chosen = routes[0]
    every = jnp.arange(experts, dtype=i32)
    hot = jnp.any(chosen[:, :, None] == every, axis=1)
    before = (jnp.arange(rows)[:, None] > jnp.arange(rows)[None, :]).astype(bf16)
    rank = mm(before, hot.astype(bf16)).astype(i32)
    slot_cols = jnp.where(hot, rank, -1)
    slot_rows = slot_cols.T
    place = slot_rows[:, None, :] == jnp.arange(cap, dtype=i32)[None, :, None]
    other = jnp.sum(chosen, axis=-1)[None, :] - every[:, None]
    other = jnp.sum(jnp.where(place, other[:, None, :], 0), axis=-1)
    other = swap_fsdp(other)
    c_send = mm(place.astype(bf16).reshape(slots, rows), c_low).astype(bf16).reshape(experts, cap, D)

    early = (dense, x_all, flags, cosine, sine, seg_rows, rot_rows, seg_cols, rot_cols, slot_cols, slot_rows, other, c_send, keep)
    (dense, x_all, flags, cosine, sine, seg_rows, rot_rows, seg_cols, rot_cols, slot_cols, slot_rows, other, c_send, keep) = tie(early)

    mine = jnp.stack([expert_gate[0], expert_up[0], expert_down[0].T])
    mine, dense = tie((mine, dense))
    expert_w = lax.all_gather(mine, "ctx", axis=0, tiled=False)
    c_slots = swap_fsdp(c_send).reshape(slots, D)

    cut = 2 * tiles * shard
    square, held = in_pieces(dense, 0, LAST + 1, shard)

    n_all, q, k, v, vt, gains = project(x_all, experts, square, held, cosine, sine, block, rows, 1)
    attn, attn_low, lse = attend(flags, q, k, vt, seg_rows, rot_rows, seg_cols, rot_cols, block)
    resid, n_two, inv_two, x_send = mid(attn_low, x_low, gains, slot_rows, square, held, cap)
    x_send, n_two, c_slots = tie((x_send, n_two, c_slots))
    x_slots = swap_fsdp(x_send).reshape(slots, D)

    shared_pack = pack_weights((shared_down, shared_gate, shared_up), ())
    shared_pack, x_slots = tie((shared_pack, x_slots))
    shared_w = lax.all_gather(shared_pack, EVERY, axis=0, tiled=False)
    shared_sq, shared_held = in_pieces(shared_w, WIDE * down_shard, 2 * tiles, shard)

    is_mine = (lane == my_fsdp).astype(f32)[None, :]
    y_slots, gx_slots, grad_router, e_da, e_db, e_xt, e_down = expert_unit(
        x_slots, c_slots, other, is_mine, square, held, expert_w
    )
    gx_slots, n_shared = tie((gx_slots, n_two))
    gx_back = swap_fsdp(gx_slots.reshape(experts, cap, D))
    e_down, e_xt = tie((e_down, e_xt))
    e_down_sums = lax.psum_scatter(e_down, "ctx", scatter_dimension=0, tiled=False)
    e_grads = expert_grads(e_xt, (e_da, e_db), n_ctx)

    e_grads, n_shared = tie((e_grads, n_shared))
    odd = (my_fsdp % 2).reshape(1)
    s_out, s_dn, s_keep, s_give = shared_unit(odd, n_shared, c_low, shared_sq, shared_held, shared_w, down_shard)
    s_give = s_give.reshape((n_ctx, -1) + s_give.shape[1:])
    s_got = jnp.stack([peer(s_give[n], "fsdp", n_fsdp, 1) for n in range(n_ctx)])
    s_parts = (s_keep.reshape(s_got.shape).astype(f32) + s_got.astype(f32)).astype(bf16)
    e_grads, gx_back, s_parts = tie((e_grads, gx_back, s_parts))
    s_low = lax.psum_scatter(s_parts, "ctx", scatter_dimension=0, tiled=False)

    d_resid, d_attn, d_mix, delta, grad_gain_two = mid_back(
        gx_back, slot_cols, s_dn, resid, inv_two, gains, c_low, attn, square, held, block
    )
    d_mix, y_slots, e_grads = tie((d_mix, y_slots, e_grads))
    e_sums = lax.psum_scatter(e_grads, "ctx", scatter_dimension=0, tiled=False)
    y_back = swap_fsdp(y_slots.reshape(experts, cap, D))
    dq, dk, dv = attend_back(
        flags, q, d_mix, k, v, lse, delta, seg_rows, rot_rows, seg_cols, rot_cols, cosine, sine, block
    )
    where = jnp.stack([my_ctx, my_fsdp % 2])
    d_low, d_own, *halves = tail(
        where, n_all, dk, dv, x_all, dq, attn_low, d_attn, grad_router, grad_gain_two, square, held, n_ctx, experts
    )
    if held[0] == 1:
        g_all = halves[0].reshape(4, devices, shard, WIDE, TILE).transpose(1, 0, 3, 2, 4)
        g_all = g_all.reshape(devices, 4 * WIDE * shard, TILE)
        g_all = jnp.concatenate([g_all, halves[1].reshape(devices, shard, TILE)], axis=1)
        g_keep, g_give = (jnp.stack(by_step(h, n_ctx)) for h in split_cores(g_all))
    else:
        g_keep, g_give = halves
    y_back, s_low = tie((y_back, s_low))
    s_grads = meet_far_once(s_low, n_fsdp)
    g_give, e_down_sums = tie((g_give, e_down_sums))
    g_parts = meet_core(g_keep, peer(g_give, "fsdp", n_fsdp, 1))
    y_back, *g_parts = tie((y_back, *g_parts))
    g_parts = meet_ctx(g_parts, n_ctx)

    output, sums = finish(y_back, slot_cols, chosen, n_two, square, held, s_out, resid, x_low, keep)

    e_down_out = e_down_sums[0].astype(f32).T[None]
    d_low, s_grads, output, e_down_out, *g_parts = tie((d_low, s_grads, output, e_down_out, *g_parts))
    g_total, g_low = add_up(g_parts)
    dense_grads = meet_far(g_total, g_low, n_fsdp)
    sums, dense_grads = tie((sums, dense_grads))
    level = [sums] + [peer(sums, "ctx", n_ctx, step) for step in range(1, n_ctx)]
    while len(level) > 1:
        level = [a + b for a, b in zip(level[0::2], level[1::2])]
    group_sums = level[0]
    valid_count = jnp.sum(valid_mask[0]).astype(f32)
    stats = jnp.sqrt(group_sums[:, 0] / (valid_count * D))[None]

    def from_pieces(array, part):
        return array.reshape(-1, part, TILE).transpose(1, 0, 2).reshape(part, -1)

    grad_shared_gate = from_pieces(s_grads[: tiles * shard], shard)
    grad_shared_up = from_pieces(s_grads[tiles * shard : cut], shard)
    grad_shared_down = from_pieces(s_grads[cut:], down_shard)
    span = WIDE * shard
    g_query, g_key, g_value, g_out = (from_pieces(dense_grads[n * span : (n + 1) * span], shard) for n in range(4))
    got = lax.all_to_all(d_low.reshape(n_ctx, rows, D), "ctx", split_axis=0, concat_axis=0, tiled=True)
    input_grad = input_back(d_own, d_resid, x_low, gains, got)[None]
    input_grad, e_sums = tie((input_grad, e_sums))
    e_sums = e_sums.astype(f32)

    last = dense_grads[LAST * shard :]
    g_router, g_gain_one, g_gain_two = last[:, :experts], last[:, experts], last[:, experts + 1]

    return (
        output[None], input_grad, g_gain_one, g_query, g_key, g_value, g_out, g_gain_two, g_router,
        grad_shared_gate, grad_shared_up, grad_shared_down,
        e_sums[0][None], e_sums[1][None], e_down_out, stats,
    )


def solution(mesh):
    sizes = dict(mesh.shape)
    rows3 = P("fsdp", "ctx", None)
    group = P("fsdp", None)
    dense1 = P(("ctx", "fsdp"))
    dense2 = P(("ctx", "fsdp"), None)
    column = P("fsdp", None, "ctx")
    return jax.shard_map(
        functools.partial(local, sizes["ctx"], sizes["fsdp"]),
        mesh=mesh,
        in_specs=(rows3, rows3, group, group, group, rows3)
        + (dense1, dense2, dense2, dense2, dense2, dense1)
        + (dense2,) * 4
        + (column, column, rows3),
        out_specs=(rows3, rows3)
        + (dense1, dense2, dense2, dense2, dense2, dense1)
        + (dense2,) * 4
        + (column, column, rows3, group),
        check_vma=False,
    )
```
